32 devices in a mesh: panel: 2 (over y), row: 4 (over z), layer: 4 (over x, core).
Axes of the slice: x: 2, y: 2, z: 4, core: 2. Of those that a mesh axis runs over, the one named last changes fastest.
Arguments:
- layers: bfloat16 [4, 8192, 512], P('layer', 'row', 'panel'), parts along dimension 2, may hold values from -6 to 6
- table: bfloat16 [16, 128, 64], replicated, may hold values from -0.375 to 0.375
- fitting: bfloat16 [8192, 6600], P('row', 'layer'), may hold values from -0.09375 to 0.09375
- owner: int32 [4, 128, 1], P('layer', 'row'), may hold values from 0 to 3; in each aligned block of 32 rows (0 to 31, 32 to 63, ..., all dimensions but the last counted through in order) at most 16 rows name the same one
- local_slice: int32 [4, 128], P('layer', 'row'), may hold values from 0 to 15
- block_index: int32 [4, 128], P('layer', 'row'), may hold values from 0 to 31
- weight_index: int32 [4, 128], P('layer', 'row'), may hold values from 0 to 15
Outputs:
- actuators: bfloat16 [512, 6600], P(('panel', 'row'), 'layer'), parts along dimension 0
The draws below stay inside these ranges and needn't reach their ends.
There are 2 independent parts, one for each index of `panel`. The reference program is written for one: setup_inputs(seed, part) draws one part's arguments, and reference() takes and returns one part's arrays. A program takes and returns all parts, laid end to end along the dimension named above; an argument that names none is the same for every part. Nothing has to cross between parts.
Inputs may be any that keep to these rules, and one draw needn't show every extreme that they name: `owner`: within the 32 entries of one layer on one row device (aligned blocks of 32 entries), no value is named more than 16 times, and in every draw some block names one value exactly 16 times.
All inputs are finite; a program needn't handle non-finite values.
Results may differ from the reference program's by a relative error of at most 0.0058.
Values may be sent and summed in bfloat16 or wider, within the bound.
A program may use at most 64 MiB of HBM per device.

```python
import math
import jax
import jax.numpy as jnp
import numpy as np
from jax import lax

C = 256
NA = 6600
S = 128
B = 64
K = 16
SL_DEV = 16
E_DEV = 32
NL = 4
NP = 8192
NB = 32
NS = 64
NQ = 8192
ENT = 128
CAP = 16
N_ROW = 4


def touch_ends(result, rng, smallest, largest):
    place = [jax.random.randint(jax.random.fold_in(rng, axis), (), 0, length) for axis, length in enumerate(result.shape)]
    longest = result.shape.index(max(result.shape))
    beside = place[:longest] + [(place[longest] + 1) % result.shape[longest]] + place[longest + 1:]
    return result.at[tuple(place)].set(smallest).at[tuple(beside)].set(largest)


def raised(values, stream_key, source, target, parts, factor):
    def block_of(dim):
        return (jnp.arange(values.shape[dim]) // (values.shape[dim] // parts)).reshape((-1,) + (1,) * (values.ndim - 1 - dim))

    one_side = jax.random.permutation(stream_key, parts)[block_of(target)]
    other_side = (block_of(target) + parts // 2) % parts
    return jnp.where((block_of(source) == one_side) | (block_of(source) == other_side), factor * values, values)


def steps_of(key, shape, cuts, low, largest):
    loudness, own = 1.0, jax.random.fold_in(key, 6)
    for axis_at, shards_of in cuts:
        heights = jnp.exp(jax.random.uniform(jax.random.fold_in(own, axis_at), (shards_of,), jnp.float32, low / len(cuts), largest / len(cuts)))
        loudness = loudness * jnp.repeat(heights, shape[axis_at] // shards_of).reshape([-1 if axis == axis_at else 1 for axis in range(len(shape))])
    return loudness


def routed_block(key, own, number, rows, count, top, reach, slope):
    sequence = jax.random.permutation(key, count)
    crowded, common = load_shares(count, rows * top, reach, slope, True), load_shares(count, rows * top, reach, slope, False)
    places = jnp.arange(count)

    def named(sizes, turn):
        used = int((sizes > 0).sum())
        fixed = max(1, used // 4)
        passed = fixed + (places - fixed + turn * (used - fixed)) % max(1, count - fixed)
        return jnp.zeros((count,), jnp.int32).at[sequence[jnp.where(places < fixed, places, passed)]].set(jnp.asarray(sizes, jnp.int32))

    sizes = jnp.where(number % 4 == 0, named(crowded, number // 4), named(common, number - number // 4 - 1))
    mixed = jax.random.permutation(jax.random.fold_in(own, 3), count)
    source_of, receiver = mixed[0:count // 2 * 2:2], mixed[1:count // 2 * 2:2]
    slack = jnp.minimum(sizes[source_of] - 1, reach - sizes[receiver]) // 2
    slack = jnp.where((source_of == sequence[0]) | (receiver == sequence[0]) | (sizes[receiver] == 0), 0, jnp.maximum(slack, 0))
    passed = jax.random.randint(jax.random.fold_in(own, 4), (count // 2,), 0, 1 << 20) % (slack + 1)
    sizes = sizes.at[source_of].add(-passed).at[receiver].add(passed)
    labels = jnp.searchsorted(jnp.cumsum(sizes), jnp.arange(rows * top), side="right").astype(jnp.int32)
    grid = labels.reshape(top, rows).T
    grid = grid[jax.random.permutation(jax.random.fold_in(own, 1), rows)]
    turn = jax.random.randint(jax.random.fold_in(own, 2), (rows, 1), 0, top)
    return jnp.take_along_axis(grid, (jnp.arange(top)[None, :] + turn) % top, axis=1)


def load_shares(amount, total, most, slope, full):
    loads = [(1 << 20) // math.isqrt(grade ** slope) + 1 for grade in range(1, amount + 1)]
    largest = most if full else min(most, max(-(-total // amount), total * loads[0] // sum(loads)))
    least = 1 if total - largest >= amount - 1 else 0
    holding, rest = [largest] + [least] * (amount - 1), total - largest - least * (amount - 1)
    while rest > 0:
        movable = [i for i in range(1, amount) if holding[i] < largest] or [i for i in range(1, amount) if holding[i] < most]
        pool, left = sum([loads[i] for i in movable]), rest
        for i in movable:
            extra = min(most - holding[i], max(1, left * loads[i] // pool), rest)
            holding[i] = holding[i] + extra
            rest = rest - extra
    return np.array(holding)


def centred(stream_key, shape, deviation, most, pieces=(), kind=jnp.bfloat16):
    loudness = steps_of(stream_key, shape, pieces, -0.22, 0.18) if pieces else 1.0
    drawn = jax.random.normal(stream_key, shape, jnp.float32) * deviation * loudness
    return jnp.minimum(jnp.maximum(drawn, -most), most).astype(kind)


def gaussian_with(key, dims, width, limit, pieces, heavy, held_as=jnp.bfloat16):
    values = width * jax.random.normal(key, dims, jnp.float32)
    if pieces:
        values = values * steps_of(key, dims, pieces, -0.22, 0.18)
    return jnp.clip(raised(values, jax.random.fold_in(key, 3), *heavy), -limit, limit).astype(held_as)


def setup_inputs(seed: int = 0, part: int = 0) -> dict:
    splits = jax.random.split(jax.random.key(seed), 8)
    part_keys = jax.random.split(jax.random.fold_in(splits[7], part), 8)
    layers = centred(part_keys[0], (NL, NP, C), 1.0, 6.0, ((0, 4), (1, 4)))
    table = centred(splits[1], (K, S, B), (4 * B) ** -0.5, 0.375)
    fitting = gaussian_with(splits[2], (NQ, NA), NQ ** -0.5, 0.09375, ((0, 4), (1, 4)), (0, 1, 4, 2.0))
    owner_keys = jax.random.split(jax.random.fold_in(splits[3], 1), NL * ENT // E_DEV)
    owner_turns = jax.random.permutation(jax.random.fold_in(splits[3], 3), NL * ENT // E_DEV)
    owner = jax.vmap(lambda own, number: routed_block(jax.random.fold_in(splits[3], 2), own, number, E_DEV, N_ROW, 1, CAP, 2))(owner_keys, owner_turns).reshape((NL, ENT, 1))
    local_slice = touch_ends(jax.random.randint(splits[4], (NL, ENT), 0, SL_DEV), jax.random.fold_in(splits[4], 1), 0, SL_DEV - 1).astype(jnp.int32)
    block_index = touch_ends(jax.random.randint(splits[5], (NL, ENT), 0, NB), jax.random.fold_in(splits[5], 1), 0, NB - 1).astype(jnp.int32)
    weight_index = touch_ends(jax.random.randint(splits[6], (NL, ENT), 0, K), jax.random.fold_in(splits[6], 1), 0, K - 1).astype(jnp.int32)
    return {"layers": layers, "table": table, "fitting": fitting, "owner": owner, "local_slice": local_slice, "block_index": block_index, "weight_index": weight_index}


def reference(layers, table, fitting, owner, local_slice, block_index, weight_index):
    layer_total = layers.shape[0]

    def one_layer(running, layer_index):
        layer_rows = lax.dynamic_index_in_dim(layers, layer_index, 0, keepdims=False)
        owner_now = lax.dynamic_index_in_dim(owner, layer_index, 0, keepdims=False)[:, 0]
        local_now = lax.dynamic_index_in_dim(local_slice, layer_index, 0, keepdims=False)
        block_now = lax.dynamic_index_in_dim(block_index, layer_index, 0, keepdims=False)
        weight_now = lax.dynamic_index_in_dim(weight_index, layer_index, 0, keepdims=False)
        source_dev = (jnp.arange(ENT, dtype=jnp.int32) // E_DEV).astype(jnp.int32)
        start_block = (source_dev * NB + block_now).astype(jnp.int32)
        grouped = layer_rows.reshape(NB * N_ROW, B, C)
        picked = grouped[start_block].astype(jnp.float32)
        weights = table[weight_now].astype(jnp.float32)
        term = jnp.einsum("esb,ebc->esc", weights, picked).astype(jnp.bfloat16)
        destination = (owner_now * SL_DEV + local_now).astype(jnp.int32)
        running = running + jax.ops.segment_sum(term.astype(jnp.float32), destination, num_segments=NS)
        return running, None

    pupil, _ = lax.scan(one_layer, jnp.zeros((NS, S, C), jnp.float32), jnp.arange(layer_total, dtype=jnp.int32))
    pupil_rounded = pupil.reshape(NQ, C).astype(jnp.bfloat16)
    return jnp.dot(pupil_rounded.T, fitting, preferred_element_type=jnp.float32).astype(jnp.bfloat16)
```

```python
import functools

import jax
import jax.numpy as jnp
from jax import lax
from jax.experimental import pallas as pl
from jax.experimental.pallas import tpu as pltpu

MESH = pl.DeviceIdType.MESH
from jax.sharding import PartitionSpec as P


def local_rows(layers, table, fitting, owner, local_slice, block_index, weight_index):
    rows_dev = layers.shape[1]
    columns = layers.shape[2]
    slice_rows = table.shape[1]
    block_rows = table.shape[2]
    entries = owner.shape[1]
    peer_count = lax.axis_size("row")
    capacity = max(2, 2 * entries // peer_count)
    slot_count = peer_count * capacity
    owned_slices = fitting.shape[0] // slice_rows
    owner_now = owner[0, :, 0]
    local_now = local_slice[0]
    owner_match = (owner_now[:, None] == jnp.arange(peer_count, dtype=jnp.int32)[None, :]).astype(
        jnp.int32
    )
    slot_rank = jnp.sum((jnp.cumsum(owner_match, axis=0) - 1) * owner_match, axis=1)
    target = owner_now * capacity + slot_rank
    placed = target[None, :] == jnp.arange(slot_count, dtype=jnp.int32)[:, None]
    filled = jnp.any(placed, axis=1)
    source = jnp.sum(jnp.where(placed, jnp.arange(entries, dtype=jnp.int32)[None, :], 0), axis=1)
    send_local = jnp.where(filled, local_now[source], -1).reshape(peer_count, capacity)
    grouped = layers[0].reshape(rows_dev // block_rows, block_rows, columns)
    picked = grouped[block_index[0][source]].reshape(peer_count, capacity, block_rows, columns)
    send_weight = weight_index[0][source].reshape(peer_count, capacity)
    got_rows, got_weight, got_local = (
        lax.all_to_all(picked, "row", split_axis=0, concat_axis=0, tiled=True),
        lax.all_to_all(send_weight, "row", split_axis=0, concat_axis=0, tiled=True),
        lax.all_to_all(send_local, "row", split_axis=0, concat_axis=0, tiled=True),
    )
    pupil_terms = jnp.einsum(
        "ksb,kbc->ksc",
        table[got_weight.reshape(-1)],
        got_rows.reshape(slot_count, block_rows, columns),
        preferred_element_type=jnp.float32,
    ).astype(jnp.bfloat16)
    selector = (
        jnp.arange(owned_slices, dtype=jnp.int32)[:, None] == got_local.reshape(-1)[None, :]
    ).astype(jnp.bfloat16)
    partial_pupil = jnp.dot(
        selector,
        pupil_terms.reshape(slot_count, slice_rows * columns),
        preferred_element_type=jnp.float32,
    ).reshape(owned_slices * slice_rows, columns)
    pupil_rounded = lax.psum(partial_pupil, "layer").astype(jnp.bfloat16)
    return lax.psum_scatter(
        lax.dot_general(
            pupil_rounded, fitting, (((0,), (0,)), ((), ())), preferred_element_type=jnp.float32
        ),
        "row",
        scatter_dimension=0,
        tiled=True,
    ).astype(jnp.bfloat16)


def index_table(owner, local_slice, block, weight, owned, weights, slices, out_ref):
    entries = owner.shape[1]
    square = (entries, entries)
    down = lax.broadcasted_iota(jnp.int32, square, 0)
    along = lax.broadcasted_iota(jnp.int32, square, 1)

    def upright(row):
        return jnp.sum(jnp.where(down == along, jnp.broadcast_to(row, square), 0), axis=1, keepdims=True)

    place = owner * owned + local_slice
    place_up = upright(place)
    place_row = jnp.broadcast_to(place, square)
    twin = (place_row == place_up) & (along < down)
    rank = jnp.sum(((place_row < place_up) | twin).astype(jnp.int32), axis=1, keepdims=True)
    follows = (jnp.sum(twin.astype(jnp.int32), axis=1, keepdims=True) > 0).astype(jnp.int32)
    code = upright(block * weights + weight)
    moved = rank == along
    code = jnp.sum(jnp.where(moved, jnp.broadcast_to(code, square), 0), axis=0, keepdims=True)
    follows = jnp.sum(jnp.where(moved, jnp.broadcast_to(follows, square), 0), axis=0, keepdims=True)
    names = lax.broadcasted_iota(jnp.int32, (entries, slices), 1)
    place_wide = jnp.broadcast_to(place_up, (entries, slices))
    until = jnp.sum((place_wide <= names).astype(jnp.int32), axis=0, keepdims=True)
    held = jnp.sum((place_wide == names).astype(jnp.int32), axis=0, keepdims=True)
    block = code // weights
    out_ref[0:1, 0:entries] = block // 2
    out_ref[1:2, 0:entries] = (block % 2) * weights + code % weights
    out_ref[2:3, 0:entries] = follows
    out_ref[3:4, 0:slices] = jnp.where(held > 0, until, 0)


def fused_kernel(
    peers, owned, spans,
    layers_ref, turned_ref, owner_ref, local_ref, block_ref, weight_ref, fitting_ref, out_ref,
    other_raw, own_raw, own_turned, wide_table, own_sums, got_sums, meta, own_index, got_index,
    fit, left, total, own_part, chunk_refs,
    in_sem, meta_sem, swap_sem, core_sem, row_sem, layer_sem, end_sem,
):
    row = lax.axis_index("row")
    me = lax.axis_index("layer")
    core = lax.rem(me, 2)
    half = other_raw.shape[1]
    width = fit.shape[0]
    weights, block_rows, points = turned_ref.shape
    pairs = own_turned.shape[0]
    entries = owner_ref.shape[1]
    half_owned = owned // 2
    slices = peers * owned
    group = 8 if entries % 8 == 0 else 1
    owner_width = half // 2
    mate = row + 1 - 2 * lax.rem(row, 2)
    cross = lax.rem(row + 2, peers)
    opposite = peers - 1 - row
    is_end = jnp.logical_or(row == 0, row == peers - 1)
    is_middle = jnp.logical_not(is_end)
    layer_peers = [lax.rem(me + k, 4) for k in range(1, 4)]
    partner = layer_peers[1]
    sibling = me + 1 - 2 * core
    order = (opposite, cross, mate, row)

    first_own = pl.multiple_of(me // 2 * half, half)
    first_other = pl.multiple_of((1 - me // 2) * half, half)
    other_copy = pltpu.make_async_copy(layers_ref.at[:, pl.ds(first_other, half)], other_raw, in_sem.at[0])
    own_copy = pltpu.make_async_copy(layers_ref.at[:, pl.ds(first_own, half)], own_raw, in_sem.at[1])
    fit_copy = pltpu.make_async_copy(fitting_ref, fit, in_sem.at[2])
    other_copy.start()
    own_copy.start()

    barrier = pltpu.get_barrier_semaphore()
    for peer in (mate, cross, opposite):
        pl.semaphore_signal(barrier, inc=1, device_id={"row": peer}, device_id_type=MESH)
    for peer in layer_peers:
        pl.semaphore_signal(barrier, inc=1, device_id={"layer": peer}, device_id_type=MESH)

    index_table(
        owner_ref[...], local_ref[...], block_ref[...], weight_ref[...], owned, weights, slices, meta
    )

    def remote(source, target, sems, where, axis, peer):
        return pltpu.make_async_remote_copy(
            src_ref=source,
            dst_ref=target,
            send_sem=sems.at[(0, *where)],
            recv_sem=sems.at[(1, *where)],
            device_id={axis: peer},
            device_id_type=MESH,
        )

    def turn(raw, targets):
        def body(pair, carry):
            turned = raw[pl.ds(pl.multiple_of(pair * points, points), points), :].T
            for (low, high), (target, base) in zip(spans, targets):
                size = high - low
                for side in range(2):
                    start = side * owner_width + low
                    target[pair, base + side * size : base + (side + 1) * size, :] = turned[
                        start : start + size
                    ]
            return carry

        lax.fori_loop(0, pairs, body, 0, unroll=4)

    other_copy.wait()
    turn(other_raw, [(refs["swap_out"], 0) for refs in chunk_refs])
    pl.semaphore_wait(barrier, peers - 1 + 3)
    meta_copy = remote(meta, got_index, meta_sem, (0,), "layer", partner)
    meta_copy.start()
    swaps = [
        remote(refs["swap_out"], refs["swap_in"], swap_sem, (index,), "layer", partner)
        for index, refs in enumerate(chunk_refs)
    ]
    for copy in swaps:
        copy.start()
    index_copy = pltpu.make_async_copy(meta, own_index, meta_sem.at[2, 0])
    index_copy.start()
    fit_copy.start()

    wide_table[...] = jnp.zeros_like(wide_table)
    for index in range(weights):
        wide_table[index, 0:block_rows, :] = turned_ref[index]
        wide_table[weights + index, block_rows:, :] = turned_ref[index]
    own_sums[0] = jnp.zeros(own_sums.shape[1:], own_sums.dtype)
    got_sums[0] = jnp.zeros(got_sums.shape[1:], got_sums.dtype)
    own_copy.wait()
    turn(own_raw, [(own_turned, 2 * low) for low, _ in spans])
    index_copy.wait()

    def sum_terms(index_ref, rows_ref, sums_ref, size):
        def body(step, carry):
            terms = []
            for offset in range(group):
                entry = step * group + offset
                terms.append(
                    jnp.dot(
                        rows_ref[index_ref[0, entry]],
                        wide_table[index_ref[1, entry]],
                        preferred_element_type=jnp.float32,
                    )
                )
            running = sums_ref[step * group, 0:size, :]
            for offset in range(group):
                entry = step * group + offset
                running = terms[offset] + index_ref[2, entry].astype(jnp.float32) * running
                sums_ref[entry + 1, 0:size, :] = running
            return carry

        lax.fori_loop(0, entries // group, body, 0)

    sum_terms(own_index, own_turned, own_sums, half)
    meta_copy.wait_recv()

    def core_copy(chunk, place):
        refs = chunk_refs[chunk]
        return remote(
            refs["core_out"].at[place], refs["core_in"].at[place], core_sem, (chunk, place), "layer", sibling
        )

    def row_copy(chunk, slot, source, peer):
        refs = chunk_refs[chunk]
        return remote(
            refs["row_out"].at[source], refs["row_in"].at[slot], row_sem, (chunk, slot), "row", peer
        )

    def layer_copy(chunk, k):
        refs = chunk_refs[chunk]
        return remote(
            refs["pieces"].at[me], refs["pieces"].at[me], layer_sem, (chunk, k), "layer", layer_peers[k]
        )

    def end_copy(chunk, slot, source, peer):
        refs = chunk_refs[chunk]
        return remote(
            refs["product"].at[source], refs["landed"].at[slot], end_sem, (chunk, slot), "row", peer
        )

    def partial(chunk, owner, which, index):
        low, high = spans[chunk]
        name = owner * owned + which * half_owned + index
        return (
            own_sums[own_index[3, name], 2 * low : 2 * high, :]
            + got_sums[got_index[3, name], 0 : 2 * (high - low), :]
        )

    def begin(chunk):
        refs = chunk_refs[chunk]
        low, high = spans[chunk]
        swaps[chunk].wait_recv()
        sum_terms(got_index, refs["swap_in"], got_sums, 2 * (high - low))

    def share(chunk):
        refs = chunk_refs[chunk]
        for place, owner in enumerate(order):

            def body(index, carry):
                refs["core_out"][place, index] = partial(chunk, owner, 1 - core, index).astype(jnp.bfloat16)
                return carry

            lax.fori_loop(0, half_owned, body, 0, unroll=4)
            core_copy(chunk, place).start()

    def spread(chunk):
        refs = chunk_refs[chunk]
        low, high = spans[chunk]
        for place, owner in enumerate(order):
            core_copy(chunk, place).wait_recv()

            def body(index, carry):
                value = partial(chunk, owner, core, index) + refs["core_in"][place, index].astype(jnp.float32)
                if place < 3:
                    refs["row_out"][place, index] = value.astype(jnp.bfloat16)
                else:
                    own_part[index, 2 * low : 2 * high, :] = value
                return carry

            lax.fori_loop(0, half_owned, body, 0, unroll=4)
            if place == 0:

                @pl.when(is_end)
                def _():
                    row_copy(chunk, 3, 0, mate).start()

                @pl.when(is_middle)
                def _():
                    row_copy(chunk, 2, 0, opposite).start()

            elif place == 1:

                @pl.when(is_end)
                def _():
                    row_copy(chunk, 1, 1, cross).start()

            elif place == 2:
                row_copy(chunk, 0, 2, mate).start()

    def join(chunk):
        refs = chunk_refs[chunk]

        @pl.when(is_middle)
        def _():
            row_copy(chunk, 3, 0, mate).wait_recv()
            refs["row_out"][1] = (
                refs["row_out"][1].astype(jnp.float32) + refs["row_in"][3].astype(jnp.float32)
            ).astype(jnp.bfloat16)
            row_copy(chunk, 1, 1, cross).start()

    def settle(chunk):
        refs = chunk_refs[chunk]
        low, high = spans[chunk]
        row_copy(chunk, 0, 2, mate).wait_recv()
        row_copy(chunk, 1, 1, cross).wait_recv()

        def store(slots):
            value = own_part[:, 2 * low : 2 * high, :]
            for slot in range(slots):
                value = value + refs["row_in"][slot].astype(jnp.float32)
            refs["pieces"][me] = value.astype(jnp.bfloat16)

        @pl.when(is_end)
        def _():
            store(2)

        @pl.when(is_middle)
        def _():
            row_copy(chunk, 2, 0, opposite).wait_recv()
            store(3)

        for k in (1, 0, 2):
            layer_copy(chunk, k).start()

    def multiply(chunk):
        refs = chunk_refs[chunk]
        low, high = spans[chunk]
        size = 2 * (high - low)
        for k in range(3):
            layer_copy(chunk, k).wait_recv()
        for piece in range(4):
            side, which = piece // 2, piece % 2
            for index in range(half_owned):
                first = (which * half_owned + index) * points
                left[side * size : (side + 1) * size, first : first + points] = refs["pieces"][piece, index]
        for start in range(0, width, 256):
            stop = min(start + 256, width)
            total[4 * low : 4 * high, start:stop] = lax.dot_general(
                left[0 : 2 * size, :],
                fit[start:stop, :],
                (((1,), (1,)), ((), ())),
                preferred_element_type=jnp.float32,
            )

    def total_of(chunk, owner):
        low, high = spans[chunk]
        size = high - low
        return total[pl.ds(pl.multiple_of(4 * low + owner * size, size), size), 0:width]

    def deliver(chunk):
        refs = chunk_refs[chunk]
        padded = refs["product"].shape[2]
        if width < padded:
            shape = (3, refs["product"].shape[1], 128)
            refs["product"][:, :, padded - 128 :] = jnp.zeros(shape, jnp.bfloat16)

        def fill(place):
            refs["product"][place, :, 0:width] = total_of(chunk, order[place]).astype(jnp.bfloat16)

        @pl.when(is_end)
        def _():
            fill(0)
            end_copy(chunk, 3, 0, mate).start()
            fill(1)
            end_copy(chunk, 1, 1, cross).start()
            fill(2)
            end_copy(chunk, 0, 2, mate).start()

        @pl.when(is_middle)
        def _():
            fill(0)
            end_copy(chunk, 2, 0, opposite).start()
            fill(2)
            end_copy(chunk, 0, 2, mate).start()

    def pass_on(chunk):
        refs = chunk_refs[chunk]

        @pl.when(is_middle)
        def _():
            end_copy(chunk, 3, 0, mate).wait_recv()
            refs["product"][1, :, 0:width] = (
                total_of(chunk, cross) + refs["landed"][3, :, 0:width].astype(jnp.float32)
            ).astype(jnp.bfloat16)
            end_copy(chunk, 1, 1, cross).start()

    def finish(chunk):
        refs = chunk_refs[chunk]
        low, high = spans[chunk]
        end_copy(chunk, 0, 2, mate).wait_recv()
        end_copy(chunk, 1, 1, cross).wait_recv()

        def store(slots):
            value = total_of(chunk, row)
            for slot in range(slots):
                value = value + refs["landed"][slot, :, 0:width].astype(jnp.float32)
            out_ref[low:high, :] = value.astype(out_ref.dtype)

        @pl.when(is_end)
        def _():
            store(2)

        @pl.when(is_middle)
        def _():
            end_copy(chunk, 2, 0, opposite).wait_recv()
            store(3)

    chunks = len(spans)
    for chunk in range(chunks):
        begin(chunk)
        if chunk > 0:
            join(chunk - 1)
        share(chunk)
        spread(chunk)
        if chunk > 0:
            settle(chunk - 1)
        if chunk == 1:
            fit_copy.wait()
        if chunk > 1:
            multiply(chunk - 2)
            deliver(chunk - 2)
    join(chunks - 1)
    if chunks == 1:
        fit_copy.wait()
    if chunks > 1:
        multiply(chunks - 2)
        deliver(chunks - 2)
    settle(chunks - 1)
    for chunk in range(chunks - 1):
        pass_on(chunk)
    multiply(chunks - 1)
    deliver(chunks - 1)
    for chunk in range(chunks - 1):
        finish(chunk)
    pass_on(chunks - 1)
    finish(chunks - 1)

    meta_copy.wait_send()
    for copy in swaps:
        copy.wait_send()
    for chunk in range(chunks):
        for place in range(4):
            core_copy(chunk, place).wait_send()
        for k in range(3):
            layer_copy(chunk, k).wait_send()
        for copy_of in (row_copy, end_copy):
            copy_of(chunk, 0, 2, mate).wait_send()
            copy_of(chunk, 1, 1, cross).wait_send()

            @pl.when(is_end)
            def _():
                copy_of(chunk, 3, 0, mate).wait_send()

            @pl.when(is_middle)
            def _():
                copy_of(chunk, 2, 0, opposite).wait_send()


def local_fused(layers, table, fitting, owner, local_slice, block_index, weight_index):
    rows_dev, columns = layers.shape[1:]
    weights, points, block_rows = table.shape
    entries = owner.shape[1]
    peers = lax.axis_size("row")
    depth, width = fitting.shape
    owned = depth // points
    half = columns // 2
    out_rows = columns // peers
    padded = -(-width // 128) * 128
    pairs = rows_dev // points
    cuts = cuts_of(out_rows)
    spans = list(zip(cuts[:-1], cuts[1:]))
    bf16, f32 = jnp.bfloat16, jnp.float32
    dma = pltpu.SemaphoreType.DMA

    def chunk_scratch(low, high):
        size = high - low
        cols = 2 * size
        return {
            "swap_out": pltpu.VMEM((pairs, cols, points), bf16),
            "swap_in": pltpu.VMEM((pairs, cols, points), bf16),
            "core_out": pltpu.VMEM((4, owned // 2, cols, points), bf16),
            "core_in": pltpu.VMEM((4, owned // 2, cols, points), bf16),
            "row_out": pltpu.VMEM((3, owned // 2, cols, points), bf16),
            "row_in": pltpu.VMEM((4, owned // 2, cols, points), bf16),
            "pieces": pltpu.VMEM((4, owned // 2, cols, points), bf16),
            "product": pltpu.VMEM((3, size, padded), bf16),
            "landed": pltpu.VMEM((4, size, padded), bf16),
        }

    widest = 2 * max(high - low for low, high in spans)
    count = len(spans)
    vmem = pl.BlockSpec(memory_space=pltpu.VMEM)
    any_space = pl.BlockSpec(memory_space=pl.ANY)
    return pl.pallas_call(
        functools.partial(fused_kernel, peers, owned, spans),
        out_shape=jax.ShapeDtypeStruct((out_rows, width), bf16),
        in_specs=[any_space, vmem, vmem, vmem, vmem, vmem, any_space],
        out_specs=vmem,
        scratch_shapes=[
            pltpu.VMEM((rows_dev, half), bf16),
            pltpu.VMEM((rows_dev, half), bf16),
            pltpu.VMEM((pairs, half, points), bf16),
            pltpu.VMEM((2 * weights, points, points), bf16),
            pltpu.VMEM((entries + 1, half, points), f32),
            pltpu.VMEM((entries + 1, widest, points), f32),
            pltpu.VMEM((8, 128), jnp.int32),
            pltpu.SMEM((8, 128), jnp.int32),
            pltpu.SMEM((8, 128), jnp.int32),
            pltpu.VMEM((width, depth), bf16),
            pltpu.VMEM((2 * widest, depth), bf16),
            pltpu.VMEM((columns, padded), f32),
            pltpu.VMEM((owned // 2, half, points), f32),
            [chunk_scratch(low, high) for low, high in spans],
            dma((3,)),
            dma((3, 1)),
            dma((2, count)),
            dma((2, count, 4)),
            dma((2, count, 4)),
            dma((2, count, 3)),
            dma((2, count, 4)),
        ],
        compiler_params=pltpu.CompilerParams(collective_id=0, has_side_effects=True),
    )(
        layers[0],
        table.transpose(0, 2, 1),
        owner[:, :, 0],
        local_slice,
        block_index,
        weight_index,
        fitting.T,
    )


def cuts_of(out_rows):
    quarter = out_rows // 4
    return [0, quarter, 2 * quarter, out_rows]


def local(layers, table, fitting, owner, local_slice, block_index, weight_index):
    arguments = (layers, table, fitting, owner, local_slice, block_index, weight_index)
    entries, peers, group = owner.shape[1], lax.axis_size("row"), lax.axis_size("layer")
    _, points, block_rows = table.shape
    raw_rows = max(2, 2 * entries // peers) * block_rows
    reduced_rows = fitting.shape[0] // group
    slices = peers * fitting.shape[0] // points
    fits = points == 128 and block_rows == 64 and layers.shape[2] == 256
    fits = fits and entries <= 128 and slices <= 128
    if group == 4 and peers == 4 and raw_rows > reduced_rows and fits:
        return local_fused(*arguments)
    return local_rows(*arguments)


def solution(mesh):
    return jax.shard_map(
        local,
        mesh=mesh,
        in_specs=(
            P("layer", "row", "panel"),
            P(),
            P("row", "layer"),
            P("layer", "row", None),
            P("layer", "row"),
            P("layer", "row"),
            P("layer", "row"),
        ),
        out_specs=P(("panel", "row"), "layer"),
        check_vma=False,
    )
```

```python
import functools

import jax
import jax.numpy as jnp
from jax import lax
from jax.experimental import pallas as pl
from jax.experimental.pallas import tpu as pltpu

MESH = pl.DeviceIdType.MESH
from jax.sharding import PartitionSpec as P


def local_rows(layers, table, fitting, owner, local_slice, block_index, weight_index):
    rows_dev = layers.shape[1]
    columns = layers.shape[2]
    slice_rows = table.shape[1]
    block_rows = table.shape[2]
    entries = owner.shape[1]
    peer_count = lax.axis_size("row")
    capacity = max(2, 2 * entries // peer_count)
    slot_count = peer_count * capacity
    owned_slices = fitting.shape[0] // slice_rows
    owner_now = owner[0, :, 0]
    local_now = local_slice[0]
    owner_match = (owner_now[:, None] == jnp.arange(peer_count, dtype=jnp.int32)[None, :]).astype(
        jnp.int32
    )
    slot_rank = jnp.sum((jnp.cumsum(owner_match, axis=0) - 1) * owner_match, axis=1)
    target = owner_now * capacity + slot_rank
    placed = target[None, :] == jnp.arange(slot_count, dtype=jnp.int32)[:, None]
    filled = jnp.any(placed, axis=1)
    source = jnp.sum(jnp.where(placed, jnp.arange(entries, dtype=jnp.int32)[None, :], 0), axis=1)
    send_local = jnp.where(filled, local_now[source], -1).reshape(peer_count, capacity)
    grouped = layers[0].reshape(rows_dev // block_rows, block_rows, columns)
    picked = grouped[block_index[0][source]].reshape(peer_count, capacity, block_rows, columns)
    send_weight = weight_index[0][source].reshape(peer_count, capacity)
    got_rows, got_weight, got_local = (
        lax.all_to_all(picked, "row", split_axis=0, concat_axis=0, tiled=True),
        lax.all_to_all(send_weight, "row", split_axis=0, concat_axis=0, tiled=True),
        lax.all_to_all(send_local, "row", split_axis=0, concat_axis=0, tiled=True),
    )
    pupil_terms = jnp.einsum(
        "ksb,kbc->ksc",
        table[got_weight.reshape(-1)],
        got_rows.reshape(slot_count, block_rows, columns),
        preferred_element_type=jnp.float32,
    ).astype(jnp.bfloat16)
    selector = (
        jnp.arange(owned_slices, dtype=jnp.int32)[:, None] == got_local.reshape(-1)[None, :]
    ).astype(jnp.bfloat16)
    partial_pupil = jnp.dot(
        selector,
        pupil_terms.reshape(slot_count, slice_rows * columns),
        preferred_element_type=jnp.float32,
    ).reshape(owned_slices * slice_rows, columns)
    pupil_rounded = lax.psum(partial_pupil, "layer").astype(jnp.bfloat16)
    return lax.psum_scatter(
        lax.dot_general(
            pupil_rounded, fitting, (((0,), (0,)), ((), ())), preferred_element_type=jnp.float32
        ),
        "row",
        scatter_dimension=0,
        tiled=True,
    ).astype(jnp.bfloat16)


def index_table(owner, local_slice, block, weight, owned, weights, slices, out_ref):
    entries = owner.shape[1]
    square = (entries, entries)
    down = lax.broadcasted_iota(jnp.int32, square, 0)
    along = lax.broadcasted_iota(jnp.int32, square, 1)

    def upright(row):
        return jnp.sum(jnp.where(down == along, jnp.broadcast_to(row, square), 0), axis=1, keepdims=True)

    place = owner * owned + local_slice
    place_up = upright(place)
    place_row = jnp.broadcast_to(place, square)
    twin = (place_row == place_up) & (along < down)
    rank = jnp.sum(((place_row < place_up) | twin).astype(jnp.int32), axis=1, keepdims=True)
    follows = (jnp.sum(twin.astype(jnp.int32), axis=1, keepdims=True) > 0).astype(jnp.int32)
    code = upright(block * weights + weight)
    moved = rank == along
    code = jnp.sum(jnp.where(moved, jnp.broadcast_to(code, square), 0), axis=0, keepdims=True)
    follows = jnp.sum(jnp.where(moved, jnp.broadcast_to(follows, square), 0), axis=0, keepdims=True)
    names = lax.broadcasted_iota(jnp.int32, (entries, slices), 1)
    place_wide = jnp.broadcast_to(place_up, (entries, slices))
    until = jnp.sum((place_wide <= names).astype(jnp.int32), axis=0, keepdims=True)
    held = jnp.sum((place_wide == names).astype(jnp.int32), axis=0, keepdims=True)
    block = code // weights
    out_ref[0:1, 0:entries] = block // 2
    out_ref[1:2, 0:entries] = (block % 2) * weights + code % weights
    out_ref[2:3, 0:entries] = follows
    out_ref[3:4, 0:slices] = jnp.where(held > 0, until, 0)


def fused_kernel(
    peers, owned, chunks, groups,
    layers_hbm, table_hbm, owner_hbm, local_hbm, block_hbm, weight_hbm, fitting_hbm, out_ref,
    other_raw, own_raw, turned_ref, owner_ref, local_ref, block_ref, weight_ref,
    own_turned, wide_table, own_sums, got_sums, meta, own_index, got_index,
    fit, left, total, own_part, chunk_refs, group_refs,
    in_sem, meta_sem, swap_sem, core_sem, row_sem, layer_sem, end_sem,
):
    row = lax.axis_index("row")
    me = lax.axis_index("layer")
    core = lax.rem(me, 2)
    side = me // 2
    half = other_raw.shape[1]
    width = fit.shape[0]
    weights, block_rows, points = turned_ref.shape
    pairs = own_turned.shape[0]
    entries = owner_ref.shape[1]
    half_owned = owned // 2
    slices = peers * owned
    step_entries = 8 if entries % 8 == 0 else 1
    owner_width = half // 2
    mate = row + 1 - 2 * lax.rem(row, 2)
    cross = lax.rem(row + 2, peers)
    opposite = peers - 1 - row
    is_end = jnp.logical_or(row == 0, row == peers - 1)
    is_middle = jnp.logical_not(is_end)
    layer_peers = [lax.rem(me + k, 4) for k in range(1, 4)]
    partner = layer_peers[1]
    sibling = me + 1 - 2 * core
    order = (opposite, cross, mate, row)
    swapped = range(1, len(chunks))

    first_own = pl.multiple_of(side * half, half)
    first_other = pl.multiple_of((1 - side) * half, half)
    small_copies = [
        pltpu.make_async_copy(source, target, in_sem.at[4 + index])
        for index, (source, target) in enumerate(
            (
                (owner_hbm, owner_ref),
                (local_hbm, local_ref),
                (block_hbm, block_ref),
                (weight_hbm, weight_ref),
            )
        )
    ]
    other_copy = pltpu.make_async_copy(layers_hbm.at[:, pl.ds(first_other, half)], other_raw, in_sem.at[0])
    own_copy = pltpu.make_async_copy(layers_hbm.at[:, pl.ds(first_own, half)], own_raw, in_sem.at[1])
    table_copy = pltpu.make_async_copy(table_hbm, turned_ref, in_sem.at[2])
    fit_copy = pltpu.make_async_copy(fitting_hbm, fit, in_sem.at[3])
    for copy in small_copies:
        copy.start()
    other_copy.start()
    own_copy.start()
    table_copy.start()

    barrier = pltpu.get_barrier_semaphore()
    for peer in (mate, cross, opposite):
        pl.semaphore_signal(barrier, inc=1, device_id={"row": peer}, device_id_type=MESH)
    for peer in layer_peers:
        pl.semaphore_signal(barrier, inc=1, device_id={"layer": peer}, device_id_type=MESH)

    def remote(source, target, sems, where, axis, peer):
        return pltpu.make_async_remote_copy(
            src_ref=source,
            dst_ref=target,
            send_sem=sems.at[(0, *where)],
            recv_sem=sems.at[(1, *where)],
            device_id={axis: peer},
            device_id_type=MESH,
        )

    def turn(raw, targets, early):
        low, high = chunks[0]["parts"][0][1:]
        early_rows = pl.ds(pl.multiple_of(early * (high - low), high - low), high - low)

        def body(pair, carry):
            turned = raw[pl.ds(pl.multiple_of(pair * points, points), points), :].T
            for chunk, target, base in targets:
                for part, start, stop in chunks[chunk]["parts"]:
                    first = part * owner_width + start
                    target[pair, base : base + stop - start, :] = turned[first : first + stop - start]
                    base += stop - start
            own_turned[pair, early_rows, :] = turned[low:high]
            return carry

        lax.fori_loop(0, pairs, body, 0, unroll=4)

    def sum_terms(index_ref, rows_ref, sums_ref, size):
        def body(step, carry):
            terms = []
            for offset in range(step_entries):
                entry = step * step_entries + offset
                terms.append(
                    jnp.dot(
                        rows_ref[index_ref[0, entry]],
                        wide_table[index_ref[1, entry]],
                        preferred_element_type=jnp.float32,
                    )
                )
            running = sums_ref[step * step_entries, 0:size, :]
            for offset in range(step_entries):
                entry = step * step_entries + offset
                running = terms[offset] + index_ref[2, entry].astype(jnp.float32) * running
                sums_ref[entry + 1, 0:size, :] = running
            return carry

        lax.fori_loop(0, entries // step_entries, body, 0)

    def core_copy(chunk, place):
        refs = chunk_refs[chunk]
        return remote(
            refs["core_out"].at[place], refs["core_in"].at[place], core_sem, (chunk, place), "layer", sibling
        )

    def row_copy(chunk, slot, source, peer):
        refs = chunk_refs[chunk]
        return remote(
            refs["row_out"].at[source], refs["row_in"].at[slot], row_sem, (chunk, slot), "row", peer
        )

    def layer_copy(chunk, k):
        refs = chunk_refs[chunk]
        return remote(
            refs["pieces"].at[me], refs["pieces"].at[me], layer_sem, (chunk, k), "layer", layer_peers[k]
        )

    def end_copy(number, slot, source, peer):
        refs = group_refs[number]
        return remote(
            refs["product"].at[source], refs["landed"].at[slot], end_sem, (number, slot), "row", peer
        )

    def rows_of(chunk):
        base = chunks[chunk]["base"]
        return slice(base, base + chunks[chunk]["columns"])

    def partial(chunk, owner, which, index):
        name = owner * owned + which * half_owned + index
        value = own_sums[own_index[3, name], rows_of(chunk), :]
        if chunk > 0:
            value = value + got_sums[got_index[3, name], 0 : chunks[chunk]["columns"], :]
        return value

    def begin(chunk):
        swaps[chunk].wait_recv()
        sum_terms(got_index, chunk_refs[chunk]["swap_in"], got_sums, chunks[chunk]["columns"])

    def share(chunk):
        refs = chunk_refs[chunk]
        for place, owner in enumerate(order):

            def body(index, carry):
                refs["core_out"][place, index] = partial(chunk, owner, 1 - core, index).astype(jnp.bfloat16)
                return carry

            lax.fori_loop(0, half_owned, body, 0, unroll=4)
            core_copy(chunk, place).start()

    def spread(chunk):
        refs = chunk_refs[chunk]
        for place, owner in enumerate(order):
            core_copy(chunk, place).wait_recv()

            def body(index, carry):
                value = partial(chunk, owner, core, index) + refs["core_in"][place, index].astype(jnp.float32)
                if place < 3:
                    refs["row_out"][place, index] = value.astype(jnp.bfloat16)
                else:
                    own_part[index, rows_of(chunk), :] = value
                return carry

            lax.fori_loop(0, half_owned, body, 0, unroll=4)
            if place == 0:

                @pl.when(is_end)
                def _():
                    row_copy(chunk, 3, 0, mate).start()

                @pl.when(is_middle)
                def _():
                    row_copy(chunk, 2, 0, opposite).start()

            elif place == 1:

                @pl.when(is_end)
                def _():
                    row_copy(chunk, 1, 1, cross).start()

            elif place == 2:
                row_copy(chunk, 0, 2, mate).start()

    def join(chunk):
        refs = chunk_refs[chunk]

        @pl.when(is_middle)
        def _():
            row_copy(chunk, 3, 0, mate).wait_recv()
            refs["row_out"][1] = (
                refs["row_out"][1].astype(jnp.float32) + refs["row_in"][3].astype(jnp.float32)
            ).astype(jnp.bfloat16)
            row_copy(chunk, 1, 1, cross).start()

    def settle(chunk):
        refs = chunk_refs[chunk]
        row_copy(chunk, 0, 2, mate).wait_recv()
        row_copy(chunk, 1, 1, cross).wait_recv()

        def store(slots):
            value = own_part[:, rows_of(chunk), :]
            for slot in range(slots):
                value = value + refs["row_in"][slot].astype(jnp.float32)
            refs["pieces"][me] = value.astype(jnp.bfloat16)

        @pl.when(is_end)
        def _():
            store(2)

        @pl.when(is_middle)
        def _():
            row_copy(chunk, 2, 0, opposite).wait_recv()
            store(3)

        for k in (1, 0, 2):
            layer_copy(chunk, k).start()

    def multiply(number):
        low, high, members = groups[number]
        size = high - low
        for chunk in members:
            for k in range(3):
                layer_copy(chunk, k).wait_recv()
        for chunk in members:
            pieces = chunk_refs[chunk]["pieces"]
            for which in range(2):
                for index in range(half_owned):
                    first = (which * half_owned + index) * points
                    lanes = slice(first, first + points)
                    if chunk == 0:
                        value = pieces[which, index].astype(jnp.float32)
                        value = (value + pieces[2 + which, index].astype(jnp.float32)).astype(jnp.bfloat16)
                        left[0:size, lanes] = value[0:size]
                        left[2 * size : 3 * size, lanes] = value[size:]
                        continue
                    for far in range(2):
                        value = pieces[2 * far + which, index]
                        for place, (part, _, _) in enumerate(chunks[chunk]["parts"]):
                            target = (2 * far + part) * size
                            left[target : target + size, lanes] = value[place * size : (place + 1) * size]
        for start in range(0, width, 256):
            stop = min(start + 256, width)
            total[4 * low : 4 * high, start:stop] = lax.dot_general(
                left[0 : 4 * size, :],
                fit[start:stop, :],
                (((1,), (1,)), ((), ())),
                preferred_element_type=jnp.float32,
            )

    def total_of(number, owner):
        low, high, _ = groups[number]
        size = high - low
        return total[pl.ds(pl.multiple_of(4 * low + owner * size, size), size), 0:width]

    def deliver(number):
        product = group_refs[number]["product"]
        _, size, padded = product.shape
        if width < padded:
            product[:, :, padded - 128 :] = jnp.zeros((3, size, 128), jnp.bfloat16)

        def fill(place):
            product[place, :, 0:width] = total_of(number, order[place]).astype(jnp.bfloat16)

        @pl.when(is_end)
        def _():
            fill(0)
            end_copy(number, 3, 0, mate).start()
            fill(1)
            end_copy(number, 1, 1, cross).start()
            fill(2)
            end_copy(number, 0, 2, mate).start()

        @pl.when(is_middle)
        def _():
            fill(0)
            end_copy(number, 2, 0, opposite).start()
            fill(2)
            end_copy(number, 0, 2, mate).start()

    def pass_on(number):
        refs = group_refs[number]

        @pl.when(is_middle)
        def _():
            end_copy(number, 3, 0, mate).wait_recv()
            refs["product"][1, :, 0:width] = (
                total_of(number, cross) + refs["landed"][3, :, 0:width].astype(jnp.float32)
            ).astype(jnp.bfloat16)
            end_copy(number, 1, 1, cross).start()

    def finish(number):
        landed = group_refs[number]["landed"]
        low, high, _ = groups[number]
        end_copy(number, 0, 2, mate).wait_recv()
        end_copy(number, 1, 1, cross).wait_recv()

        def store(slots):
            value = total_of(number, row)
            for slot in range(slots):
                value = value + landed[slot, :, 0:width].astype(jnp.float32)
            out_ref[low:high, :] = value.astype(out_ref.dtype)

        @pl.when(is_end)
        def _():
            store(2)

        @pl.when(is_middle)
        def _():
            end_copy(number, 2, 0, opposite).wait_recv()
            store(3)

    for copy in small_copies:
        copy.wait()
    index_table(
        owner_ref[...], local_ref[...], block_ref[...], weight_ref[...], owned, weights, slices, meta
    )
    index_copy = pltpu.make_async_copy(meta, own_index, meta_sem.at[2, 0])
    index_copy.start()
    other_copy.wait()
    turn(other_raw, [(chunk, chunk_refs[chunk]["swap_out"], 0) for chunk in swapped], 1 - side)
    pl.semaphore_wait(barrier, peers - 1 + 3)
    meta_copy = remote(meta, got_index, meta_sem, (0,), "layer", partner)
    meta_copy.start()
    swaps = {
        chunk: remote(
            chunk_refs[chunk]["swap_out"], chunk_refs[chunk]["swap_in"], swap_sem, (chunk,), "layer", partner
        )
        for chunk in swapped
    }
    for copy in swaps.values():
        copy.start()
    fit_copy.start()
    own_copy.wait()
    turn(own_raw, [(chunk, own_turned, chunks[chunk]["base"]) for chunk in swapped], side)
    wide_table[...] = jnp.zeros_like(wide_table)
    table_copy.wait()
    for index in range(weights):
        wide_table[index, 0:block_rows, :] = turned_ref[index]
        wide_table[weights + index, block_rows:, :] = turned_ref[index]
    own_sums[0] = jnp.zeros(own_sums.shape[1:], own_sums.dtype)
    got_sums[0] = jnp.zeros(got_sums.shape[1:], got_sums.dtype)
    index_copy.wait()
    sum_terms(own_index, own_turned, own_sums, own_turned.shape[1])
    share(0)
    spread(0)
    meta_copy.wait_recv()
    begin(1)
    share(1)
    join(0)
    spread(1)
    begin(2)
    share(2)
    spread(2)
    join(1)
    settle(0)
    begin(3)
    share(3)
    spread(3)
    join(2)
    settle(1)
    begin(4)
    share(4)
    spread(4)
    join(3)
    settle(2)
    fit_copy.wait()
    multiply(0)
    join(4)
    deliver(0)
    settle(3)
    multiply(1)
    deliver(1)
    settle(4)
    pass_on(0)
    multiply(2)
    deliver(2)
    pass_on(1)
    multiply(3)
    deliver(3)
    pass_on(2)
    finish(0)
    finish(1)
    pass_on(3)
    finish(2)
    finish(3)

    meta_copy.wait_send()
    for copy in swaps.values():
        copy.wait_send()
    for chunk in range(len(chunks)):
        for place in range(4):
            core_copy(chunk, place).wait_send()
        for k in range(3):
            layer_copy(chunk, k).wait_send()

    def drain(copy_of, number):
        copy_of(number, 0, 2, mate).wait_send()
        copy_of(number, 1, 1, cross).wait_send()

        @pl.when(is_end)
        def _():
            copy_of(number, 3, 0, mate).wait_send()

        @pl.when(is_middle)
        def _():
            copy_of(number, 2, 0, opposite).wait_send()

    for chunk in range(len(chunks)):
        drain(row_copy, chunk)
    for number in range(len(groups)):
        drain(end_copy, number)


def plan_of(out_rows):
    cut = out_rows // 4
    marks = [cut * index for index in range(5)]
    spans = list(zip(marks[:-1], marks[1:]))
    low, high = spans[0]
    parts = [[(0, low, high)], [(1, low, high)]]
    parts += [[(0, start, stop), (1, start, stop)] for start, stop in spans[1:]]
    chunks, base = [], 0
    for number, part in enumerate(parts):
        columns = sum(stop - start for _, start, stop in part)
        if number == 0:
            columns = 2 * columns
        chunks.append({"parts": part, "columns": columns, "base": base})
        base += columns
    groups = [(low, high, (0, 1))]
    groups += [(start, stop, (number + 2,)) for number, (start, stop) in enumerate(spans[1:])]
    return chunks, groups, base


def local_fused(layers, table, fitting, owner, local_slice, block_index, weight_index):
    rows_dev, columns = layers.shape[1:]
    weights, points, block_rows = table.shape
    entries = owner.shape[1]
    peers = lax.axis_size("row")
    depth, width = fitting.shape
    owned = depth // points
    half = columns // 2
    out_rows = columns // peers
    padded = -(-width // 128) * 128
    pairs = rows_dev // points
    chunks, groups, held = plan_of(out_rows)
    bf16, f32 = jnp.bfloat16, jnp.float32
    dma = pltpu.SemaphoreType.DMA

    def chunk_scratch(number):
        cols = chunks[number]["columns"]
        slots = owned // 2
        refs = {
            "core_out": pltpu.VMEM((4, slots, cols, points), bf16),
            "core_in": pltpu.VMEM((4, slots, cols, points), bf16),
            "row_out": pltpu.VMEM((3, slots, cols, points), bf16),
            "row_in": pltpu.VMEM((4, slots, cols, points), bf16),
            "pieces": pltpu.VMEM((4, slots, cols, points), bf16),
        }
        if number > 0:
            refs["swap_out"] = pltpu.VMEM((pairs, cols, points), bf16)
            refs["swap_in"] = pltpu.VMEM((pairs, cols, points), bf16)
        return refs

    def group_scratch(number):
        low, high, _ = groups[number]
        return {
            "product": pltpu.VMEM((3, high - low, padded), bf16),
            "landed": pltpu.VMEM((4, high - low, padded), bf16),
        }

    widest = max(chunk["columns"] for chunk in chunks[1:])
    tallest = max(4 * (high - low) for low, high, _ in groups)
    vmem = pl.BlockSpec(memory_space=pltpu.VMEM)
    any_space = pl.BlockSpec(memory_space=pl.ANY)
    return pl.pallas_call(
        functools.partial(fused_kernel, peers, owned, chunks, groups),
        out_shape=jax.ShapeDtypeStruct((out_rows, width), bf16),
        in_specs=[any_space] * 7,
        out_specs=vmem,
        scratch_shapes=[
            pltpu.VMEM((rows_dev, half), bf16),
            pltpu.VMEM((rows_dev, half), bf16),
            pltpu.VMEM((weights, block_rows, points), bf16),
            pltpu.VMEM((1, entries), jnp.int32),
            pltpu.VMEM((1, entries), jnp.int32),
            pltpu.VMEM((1, entries), jnp.int32),
            pltpu.VMEM((1, entries), jnp.int32),
            pltpu.VMEM((pairs, held, points), bf16),
            pltpu.VMEM((2 * weights, points, points), bf16),
            pltpu.VMEM((entries + 1, held, points), f32),
            pltpu.VMEM((entries + 1, widest, points), f32),
            pltpu.VMEM((8, 128), jnp.int32),
            pltpu.SMEM((8, 128), jnp.int32),
            pltpu.SMEM((8, 128), jnp.int32),
            pltpu.VMEM((width, depth), bf16),
            pltpu.VMEM((tallest, depth), bf16),
            pltpu.VMEM((columns, padded), f32),
            pltpu.VMEM((owned // 2, held, points), f32),
            [chunk_scratch(number) for number in range(len(chunks))],
            [group_scratch(number) for number in range(len(groups))],
            dma((8,)),
            dma((3, 1)),
            dma((2, len(chunks))),
            dma((2, len(chunks), 4)),
            dma((2, len(chunks), 4)),
            dma((2, len(chunks), 3)),
            dma((2, len(groups), 4)),
        ],
        compiler_params=pltpu.CompilerParams(collective_id=0, has_side_effects=True),
    )(
        layers[0],
        table.transpose(0, 2, 1),
        owner[:, :, 0],
        local_slice,
        block_index,
        weight_index,
        fitting.T,
    )


def local(layers, table, fitting, owner, local_slice, block_index, weight_index):
    arguments = (layers, table, fitting, owner, local_slice, block_index, weight_index)
    entries, peers, group = owner.shape[1], lax.axis_size("row"), lax.axis_size("layer")
    _, points, block_rows = table.shape
    raw_rows = max(2, 2 * entries // peers) * block_rows
    reduced_rows = fitting.shape[0] // group
    slices = peers * fitting.shape[0] // points
    fits = points == 128 and block_rows == 64 and layers.shape[2] == 256
    fits = fits and entries <= 128 and slices <= 128
    if group == 4 and peers == 4 and raw_rows > reduced_rows and fits:
        return local_fused(*arguments)
    return local_rows(*arguments)


def solution(mesh):
    return jax.shard_map(
        local,
        mesh=mesh,
        in_specs=(
            P("layer", "row", "panel"),
            P(),
            P("row", "layer"),
            P("layer", "row", None),
            P("layer", "row"),
            P("layer", "row"),
            P("layer", "row"),
        ),
        out_specs=P(("panel", "row"), "layer"),
        check_vma=False,
    )
```

```python
import functools

import jax
import jax.numpy as jnp
from jax import lax
from jax.experimental import pallas as pl
from jax.experimental.pallas import tpu as pltpu

MESH = pl.DeviceIdType.MESH
from jax.sharding import PartitionSpec as P


def local_rows(layers, table, fitting, owner, local_slice, block_index, weight_index):
    rows_dev = layers.shape[1]
    columns = layers.shape[2]
    slice_rows = table.shape[1]
    block_rows = table.shape[2]
    entries = owner.shape[1]
    peer_count = lax.axis_size("row")
    capacity = max(2, 2 * entries // peer_count)
    slot_count = peer_count * capacity
    owned_slices = fitting.shape[0] // slice_rows
    owner_now = owner[0, :, 0]
    local_now = local_slice[0]
    owner_match = (owner_now[:, None] == jnp.arange(peer_count, dtype=jnp.int32)[None, :]).astype(
        jnp.int32
    )
    slot_rank = jnp.sum((jnp.cumsum(owner_match, axis=0) - 1) * owner_match, axis=1)
    target = owner_now * capacity + slot_rank
    placed = target[None, :] == jnp.arange(slot_count, dtype=jnp.int32)[:, None]
    filled = jnp.any(placed, axis=1)
    source = jnp.sum(jnp.where(placed, jnp.arange(entries, dtype=jnp.int32)[None, :], 0), axis=1)
    send_local = jnp.where(filled, local_now[source], -1).reshape(peer_count, capacity)
    grouped = layers[0].reshape(rows_dev // block_rows, block_rows, columns)
    picked = grouped[block_index[0][source]].reshape(peer_count, capacity, block_rows, columns)
    send_weight = weight_index[0][source].reshape(peer_count, capacity)
    got_rows, got_weight, got_local = (
        lax.all_to_all(picked, "row", split_axis=0, concat_axis=0, tiled=True),
        lax.all_to_all(send_weight, "row", split_axis=0, concat_axis=0, tiled=True),
        lax.all_to_all(send_local, "row", split_axis=0, concat_axis=0, tiled=True),
    )
    pupil_terms = jnp.einsum(
        "ksb,kbc->ksc",
        table[got_weight.reshape(-1)],
        got_rows.reshape(slot_count, block_rows, columns),
        preferred_element_type=jnp.float32,
    ).astype(jnp.bfloat16)
    selector = (
        jnp.arange(owned_slices, dtype=jnp.int32)[:, None] == got_local.reshape(-1)[None, :]
    ).astype(jnp.bfloat16)
    partial_pupil = jnp.dot(
        selector,
        pupil_terms.reshape(slot_count, slice_rows * columns),
        preferred_element_type=jnp.float32,
    ).reshape(owned_slices * slice_rows, columns)
    pupil_rounded = lax.psum(partial_pupil, "layer").astype(jnp.bfloat16)
    return lax.psum_scatter(
        lax.dot_general(
            pupil_rounded, fitting, (((0,), (0,)), ((), ())), preferred_element_type=jnp.float32
        ),
        "row",
        scatter_dimension=0,
        tiled=True,
    ).astype(jnp.bfloat16)


def index_table(owner, local_slice, block, weight, owned, weights, slices, out_ref):
    entries = owner.shape[1]
    square = (entries, entries)
    down = lax.broadcasted_iota(jnp.int32, square, 0)
    along = lax.broadcasted_iota(jnp.int32, square, 1)

    def upright(row):
        return jnp.sum(jnp.where(down == along, jnp.broadcast_to(row, square), 0), axis=1, keepdims=True)

    place = owner * owned + local_slice
    place_up = upright(place)
    place_row = jnp.broadcast_to(place, square)
    twin = (place_row == place_up) & (along < down)
    rank = jnp.sum(((place_row < place_up) | twin).astype(jnp.int32), axis=1, keepdims=True)
    follows = (jnp.sum(twin.astype(jnp.int32), axis=1, keepdims=True) > 0).astype(jnp.int32)
    code = upright(block * weights + weight)
    moved = rank == along
    code = jnp.sum(jnp.where(moved, jnp.broadcast_to(code, square), 0), axis=0, keepdims=True)
    follows = jnp.sum(jnp.where(moved, jnp.broadcast_to(follows, square), 0), axis=0, keepdims=True)
    names = lax.broadcasted_iota(jnp.int32, (entries, slices), 1)
    place_wide = jnp.broadcast_to(place_up, (entries, slices))
    until = jnp.sum((place_wide <= names).astype(jnp.int32), axis=0, keepdims=True)
    held = jnp.sum((place_wide == names).astype(jnp.int32), axis=0, keepdims=True)
    block = code // weights
    out_ref[0:1, 0:entries] = block // 2
    out_ref[1:2, 0:entries] = (block % 2) * weights + code % weights
    out_ref[2:3, 0:entries] = follows
    out_ref[3:4, 0:slices] = jnp.where(held > 0, until, 0)


def fused_kernel(
    peers, owned, chunks, groups,
    layers_hbm, table_hbm, owner_hbm, local_hbm, block_hbm, weight_hbm, fitting_hbm, out_hbm,
    other_raw, own_raw, turned_ref, owner_ref, local_ref, block_ref, weight_ref,
    own_turned, wide_table, own_sums, got_sums, meta, own_index, got_index,
    fit, left, total, own_part, result, chunk_refs, group_refs,
    in_sem, meta_sem, swap_sem, core_sem, row_sem, layer_sem, end_sem,
):
    row = lax.axis_index("row")
    me = lax.axis_index("layer")
    core = lax.rem(me, 2)
    side = me // 2
    half = other_raw.shape[1]
    width = fit.shape[0]
    weights, block_rows, points = turned_ref.shape
    pairs = own_turned.shape[0]
    entries = owner_ref.shape[1]
    half_owned = owned // 2
    slices = peers * owned
    step_entries = 8 if entries % 8 == 0 else 1
    owner_width = half // 2
    mate = row + 1 - 2 * lax.rem(row, 2)
    cross = lax.rem(row + 2, peers)
    opposite = peers - 1 - row
    is_end = jnp.logical_or(row == 0, row == peers - 1)
    is_middle = jnp.logical_not(is_end)
    layer_peers = [lax.rem(me + k, 4) for k in range(1, 4)]
    partner = layer_peers[1]
    sibling = me + 1 - 2 * core
    order = (opposite, cross, mate, row)
    swapped = range(1, len(chunks))

    first_own = pl.multiple_of(side * half, half)
    first_other = pl.multiple_of((1 - side) * half, half)
    small_copies = [
        pltpu.make_async_copy(source, target, in_sem.at[4 + index])
        for index, (source, target) in enumerate(
            (
                (owner_hbm, owner_ref),
                (local_hbm, local_ref),
                (block_hbm, block_ref),
                (weight_hbm, weight_ref),
            )
        )
    ]
    other_copy = pltpu.make_async_copy(layers_hbm.at[:, pl.ds(first_other, half)], other_raw, in_sem.at[0])
    own_copy = pltpu.make_async_copy(layers_hbm.at[:, pl.ds(first_own, half)], own_raw, in_sem.at[1])
    table_copy = pltpu.make_async_copy(table_hbm, turned_ref, in_sem.at[2])
    fit_copy = pltpu.make_async_copy(fitting_hbm, fit, in_sem.at[3])
    for copy in small_copies:
        copy.start()
    other_copy.start()
    own_copy.start()
    table_copy.start()

    barrier = pltpu.get_barrier_semaphore()
    for peer in (mate, cross, opposite):
        pl.semaphore_signal(barrier, inc=1, device_id={"row": peer}, device_id_type=MESH)
    for peer in layer_peers:
        pl.semaphore_signal(barrier, inc=1, device_id={"layer": peer}, device_id_type=MESH)

    def remote(source, target, sems, where, axis, peer):
        return pltpu.make_async_remote_copy(
            src_ref=source,
            dst_ref=target,
            send_sem=sems.at[(0, *where)],
            recv_sem=sems.at[(1, *where)],
            device_id={axis: peer},
            device_id_type=MESH,
        )

    def turn(raw, targets, early):
        low, high = chunks[0]["parts"][0][1:]
        early_rows = pl.ds(pl.multiple_of(early * (high - low), high - low), high - low)

        def body(pair, carry):
            turned = raw[pl.ds(pl.multiple_of(pair * points, points), points), :].T
            for chunk, target, base in targets:
                for part, start, stop in chunks[chunk]["parts"]:
                    first = part * owner_width + start
                    target[pair, base : base + stop - start, :] = turned[first : first + stop - start]
                    base += stop - start
            own_turned[pair, early_rows, :] = turned[low:high]
            return carry

        lax.fori_loop(0, pairs, body, 0, unroll=4)

    def sum_terms(index_ref, rows_ref, sums_ref, size):
        def body(step, carry):
            terms = []
            for offset in range(step_entries):
                entry = step * step_entries + offset
                terms.append(
                    jnp.dot(
                        rows_ref[index_ref[0, entry]],
                        wide_table[index_ref[1, entry]],
                        preferred_element_type=jnp.float32,
                    )
                )
            running = sums_ref[step * step_entries, 0:size, :]
            for offset in range(step_entries):
                entry = step * step_entries + offset
                running = terms[offset] + index_ref[2, entry].astype(jnp.float32) * running
                sums_ref[entry + 1, 0:size, :] = running
            return carry

        lax.fori_loop(0, entries // step_entries, body, 0)

    def core_copy(chunk, place):
        refs = chunk_refs[chunk]
        return remote(
            refs["core_out"].at[place], refs["core_in"].at[place], core_sem, (chunk, place), "layer", sibling
        )

    def row_copy(chunk, slot, source, peer):
        refs = chunk_refs[chunk]
        return remote(
            refs["row_out"].at[source], refs["row_in"].at[slot], row_sem, (chunk, slot), "row", peer
        )

    def layer_copy(chunk, k):
        refs = chunk_refs[chunk]
        return remote(
            refs["pieces"].at[me], refs["pieces"].at[me], layer_sem, (chunk, k), "layer", layer_peers[k]
        )

    def end_copy(number, slot, source, peer):
        refs = group_refs[number]
        return remote(
            refs["product"].at[source], refs["landed"].at[slot], end_sem, (number, slot), "row", peer
        )

    def out_copy(number):
        low, high, _ = groups[number]
        return pltpu.make_async_copy(
            result.at[low:high, :], out_hbm.at[low:high, :], in_sem.at[8 + number]
        )

    def rows_of(chunk):
        base = chunks[chunk]["base"]
        return slice(base, base + chunks[chunk]["columns"])

    def partial(chunk, owner, which, index):
        name = owner * owned + which * half_owned + index
        value = own_sums[own_index[3, name], rows_of(chunk), :]
        if chunk > 0:
            value = value + got_sums[got_index[3, name], 0 : chunks[chunk]["columns"], :]
        return value

    def begin(chunk):
        swaps[chunk].wait_recv()
        sum_terms(got_index, chunk_refs[chunk]["swap_in"], got_sums, chunks[chunk]["columns"])

    def share(chunk):
        refs = chunk_refs[chunk]
        for place, owner in enumerate(order):

            def body(index, carry):
                refs["core_out"][place, index] = partial(chunk, owner, 1 - core, index).astype(jnp.bfloat16)
                return carry

            lax.fori_loop(0, half_owned, body, 0, unroll=4)
            core_copy(chunk, place).start()

    def spread(chunk):
        refs = chunk_refs[chunk]
        for place, owner in enumerate(order):
            core_copy(chunk, place).wait_recv()

            def body(index, carry):
                value = partial(chunk, owner, core, index) + refs["core_in"][place, index].astype(jnp.float32)
                if place < 3:
                    refs["row_out"][place, index] = value.astype(jnp.bfloat16)
                else:
                    own_part[index, rows_of(chunk), :] = value
                return carry

            lax.fori_loop(0, half_owned, body, 0, unroll=4)
            if place < 2:

                @pl.when(is_end)
                def _():
                    row_copy(chunk, 3 - place, place, mate).start()

            elif place == 2:
                row_copy(chunk, 0, 2, mate).start()

    def join(chunk):
        refs = chunk_refs[chunk]

        def merge(place, slot):
            row_copy(chunk, slot, place, mate).wait_recv()
            refs["row_out"][place] = (
                refs["row_out"][place].astype(jnp.float32) + refs["row_in"][slot].astype(jnp.float32)
            ).astype(jnp.bfloat16)

        @pl.when(is_middle)
        def _():
            merge(1, 3)
            row_copy(chunk, 1, 1, cross).start()
            merge(0, 2)
            row_copy(chunk, 4, 0, opposite).start()

    def settle(chunk):
        refs = chunk_refs[chunk]
        row_copy(chunk, 0, 2, mate).wait_recv()

        def store(slot):
            value = own_part[:, rows_of(chunk), :]
            for part in (0, slot):
                value = value + refs["row_in"][part].astype(jnp.float32)
            refs["pieces"][me] = value.astype(jnp.bfloat16)

        @pl.when(is_end)
        def _():
            row_copy(chunk, 1, 1, cross).wait_recv()
            store(1)

        @pl.when(is_middle)
        def _():
            row_copy(chunk, 4, 0, opposite).wait_recv()
            store(4)

        for k in (1, 0, 2):
            layer_copy(chunk, k).start()

    def multiply(number):
        low, high, members = groups[number]
        size = high - low
        for chunk in members:
            for k in range(3):
                layer_copy(chunk, k).wait_recv()
        for chunk in members:
            pieces = chunk_refs[chunk]["pieces"]
            for which in range(2):
                for index in range(half_owned):
                    first = (which * half_owned + index) * points
                    lanes = slice(first, first + points)
                    if chunk == 0:
                        value = pieces[which, index].astype(jnp.float32)
                        value = (value + pieces[2 + which, index].astype(jnp.float32)).astype(jnp.bfloat16)
                        left[0:size, lanes] = value[0:size]
                        left[2 * size : 3 * size, lanes] = value[size:]
                        continue
                    for far in range(2):
                        value = pieces[2 * far + which, index]
                        for place, (part, _, _) in enumerate(chunks[chunk]["parts"]):
                            target = (2 * far + part) * size
                            left[target : target + size, lanes] = value[place * size : (place + 1) * size]
        for start in range(0, width, 256):
            stop = min(start + 256, width)
            total[4 * low : 4 * high, start:stop] = lax.dot_general(
                left[0 : 4 * size, :],
                fit[start:stop, :],
                (((1,), (1,)), ((), ())),
                preferred_element_type=jnp.float32,
            )

    def total_of(number, owner):
        low, high, _ = groups[number]
        size = high - low
        return total[pl.ds(pl.multiple_of(4 * low + owner * size, size), size), 0:width]

    def deliver(number):
        product = group_refs[number]["product"]
        _, size, padded = product.shape
        if width < padded:
            product[:, :, padded - 128 :] = jnp.zeros((3, size, 128), jnp.bfloat16)

        def fill(place):
            product[place, :, 0:width] = total_of(number, order[place]).astype(jnp.bfloat16)

        @pl.when(is_end)
        def _():
            for place in range(2):
                fill(place)
                end_copy(number, 3 - place, place, mate).start()

        fill(2)
        end_copy(number, 0, 2, mate).start()

    def pass_on(number):
        refs = group_refs[number]

        def merge(place, slot):
            end_copy(number, slot, place, mate).wait_recv()
            refs["product"][place, :, 0:width] = (
                total_of(number, order[place]) + refs["landed"][slot, :, 0:width].astype(jnp.float32)
            ).astype(jnp.bfloat16)

        @pl.when(is_middle)
        def _():
            merge(1, 3)
            end_copy(number, 1, 1, cross).start()
            merge(0, 2)
            end_copy(number, 4, 0, opposite).start()

    def finish(number):
        landed = group_refs[number]["landed"]
        low, high, _ = groups[number]
        end_copy(number, 0, 2, mate).wait_recv()

        def store(slot):
            value = total_of(number, row)
            for part in (0, slot):
                value = value + landed[part, :, 0:width].astype(jnp.float32)
            result[low:high, :] = value.astype(result.dtype)

        @pl.when(is_end)
        def _():
            end_copy(number, 1, 1, cross).wait_recv()
            store(1)

        @pl.when(is_middle)
        def _():
            end_copy(number, 4, 0, opposite).wait_recv()
            store(4)

        out_copy(number).start()

    for copy in small_copies:
        copy.wait()
    index_table(
        owner_ref[...], local_ref[...], block_ref[...], weight_ref[...], owned, weights, slices, meta
    )
    index_copy = pltpu.make_async_copy(meta, own_index, meta_sem.at[2, 0])
    index_copy.start()
    other_copy.wait()
    turn(other_raw, [(chunk, chunk_refs[chunk]["swap_out"], 0) for chunk in swapped], 1 - side)
    pl.semaphore_wait(barrier, peers - 1 + 3)
    meta_copy = remote(meta, got_index, meta_sem, (0,), "layer", partner)
    meta_copy.start()
    swaps = {
        chunk: remote(
            chunk_refs[chunk]["swap_out"], chunk_refs[chunk]["swap_in"], swap_sem, (chunk,), "layer", partner
        )
        for chunk in swapped
    }
    for copy in swaps.values():
        copy.start()
    own_copy.wait()
    turn(own_raw, [(chunk, own_turned, chunks[chunk]["base"]) for chunk in swapped], side)
    wide_table[...] = jnp.zeros_like(wide_table)
    table_copy.wait()
    for index in range(weights):
        wide_table[index, 0:block_rows, :] = turned_ref[index]
        wide_table[weights + index, block_rows:, :] = turned_ref[index]
    own_sums[0] = jnp.zeros(own_sums.shape[1:], own_sums.dtype)
    got_sums[0] = jnp.zeros(got_sums.shape[1:], got_sums.dtype)
    index_copy.wait()
    sum_terms(own_index, own_turned, own_sums, own_turned.shape[1])
    share(0)
    spread(0)
    meta_copy.wait_recv()
    begin(1)
    share(1)
    join(0)
    spread(1)
    fit_copy.start()
    begin(2)
    share(2)
    spread(2)
    join(1)
    begin(3)
    share(3)
    settle(0)
    spread(3)
    join(2)
    begin(4)
    share(4)
    spread(4)
    settle(1)
    join(3)
    settle(2)
    fit_copy.wait()
    multiply(0)
    join(4)
    deliver(0)
    settle(3)
    multiply(1)
    deliver(1)
    settle(4)
    pass_on(0)
    multiply(2)
    deliver(2)
    pass_on(1)
    multiply(3)
    deliver(3)
    pass_on(2)
    finish(0)
    finish(1)
    pass_on(3)
    finish(2)
    finish(3)

    meta_copy.wait_send()
    for copy in swaps.values():
        copy.wait_send()
    for chunk in range(len(chunks)):
        for place in range(4):
            core_copy(chunk, place).wait_send()
        for k in range(3):
            layer_copy(chunk, k).wait_send()

    def drain(copy_of, number):
        copy_of(number, 0, 2, mate).wait_send()

        @pl.when(is_end)
        def _():
            copy_of(number, 3, 0, mate).wait_send()
            copy_of(number, 2, 1, mate).wait_send()

        @pl.when(is_middle)
        def _():
            copy_of(number, 1, 1, cross).wait_send()
            copy_of(number, 4, 0, opposite).wait_send()

    for chunk in range(len(chunks)):
        drain(row_copy, chunk)
    for number in range(len(groups)):
        drain(end_copy, number)
        out_copy(number).wait()


def plan_of(out_rows):
    cut = out_rows // 4
    marks = [cut * index for index in range(5)]
    spans = list(zip(marks[:-1], marks[1:]))
    low, high = spans[0]
    parts = [[(0, low, high)], [(1, low, high)]]
    parts += [[(0, start, stop), (1, start, stop)] for start, stop in spans[1:]]
    chunks, base = [], 0
    for number, part in enumerate(parts):
        columns = sum(stop - start for _, start, stop in part)
        if number == 0:
            columns = 2 * columns
        chunks.append({"parts": part, "columns": columns, "base": base})
        base += columns
    groups = [(low, high, (0, 1))]
    groups += [(start, stop, (number + 2,)) for number, (start, stop) in enumerate(spans[1:])]
    return chunks, groups, base


def local_fused(layers, table, fitting, owner, local_slice, block_index, weight_index):
    rows_dev, columns = layers.shape[1:]
    weights, points, block_rows = table.shape
    entries = owner.shape[1]
    peers = lax.axis_size("row")
    depth, width = fitting.shape
    owned = depth // points
    half = columns // 2
    out_rows = columns // peers
    padded = -(-width // 128) * 128
    pairs = rows_dev // points
    chunks, groups, held = plan_of(out_rows)
    bf16, f32 = jnp.bfloat16, jnp.float32
    dma = pltpu.SemaphoreType.DMA

    def chunk_scratch(number):
        cols = chunks[number]["columns"]
        slots = owned // 2
        refs = {
            "core_out": pltpu.VMEM((4, slots, cols, points), bf16),
            "core_in": pltpu.VMEM((4, slots, cols, points), bf16),
            "row_out": pltpu.VMEM((3, slots, cols, points), bf16),
            "row_in": pltpu.VMEM((5, slots, cols, points), bf16),
            "pieces": pltpu.VMEM((4, slots, cols, points), bf16),
        }
        if number > 0:
            refs["swap_out"] = pltpu.VMEM((pairs, cols, points), bf16)
            refs["swap_in"] = pltpu.VMEM((pairs, cols, points), bf16)
        return refs

    def group_scratch(number):
        low, high, _ = groups[number]
        return {
            "product": pltpu.VMEM((3, high - low, padded), bf16),
            "landed": pltpu.VMEM((5, high - low, padded), bf16),
        }

    widest = max(chunk["columns"] for chunk in chunks[1:])
    tallest = max(4 * (high - low) for low, high, _ in groups)
    any_space = pl.BlockSpec(memory_space=pl.ANY)
    return pl.pallas_call(
        functools.partial(fused_kernel, peers, owned, chunks, groups),
        out_shape=jax.ShapeDtypeStruct((out_rows, width), bf16),
        in_specs=[any_space] * 7,
        out_specs=any_space,
        scratch_shapes=[
            pltpu.VMEM((rows_dev, half), bf16),
            pltpu.VMEM((rows_dev, half), bf16),
            pltpu.VMEM((weights, block_rows, points), bf16),
            pltpu.VMEM((1, entries), jnp.int32),
            pltpu.VMEM((1, entries), jnp.int32),
            pltpu.VMEM((1, entries), jnp.int32),
            pltpu.VMEM((1, entries), jnp.int32),
            pltpu.VMEM((pairs, held, points), bf16),
            pltpu.VMEM((2 * weights, points, points), bf16),
            pltpu.VMEM((entries + 1, held, points), f32),
            pltpu.VMEM((entries + 1, widest, points), f32),
            pltpu.VMEM((8, 128), jnp.int32),
            pltpu.SMEM((8, 128), jnp.int32),
            pltpu.SMEM((8, 128), jnp.int32),
            pltpu.VMEM((width, depth), bf16),
            pltpu.VMEM((tallest, depth), bf16),
            pltpu.VMEM((columns, padded), f32),
            pltpu.VMEM((owned // 2, held, points), f32),
            pltpu.VMEM((out_rows, width), bf16),
            [chunk_scratch(number) for number in range(len(chunks))],
            [group_scratch(number) for number in range(len(groups))],
            dma((8 + len(groups),)),
            dma((3, 1)),
            dma((2, len(chunks))),
            dma((2, len(chunks), 4)),
            dma((2, len(chunks), 5)),
            dma((2, len(chunks), 3)),
            dma((2, len(groups), 5)),
        ],
        compiler_params=pltpu.CompilerParams(collective_id=0, has_side_effects=True),
    )(
        layers[0],
        table.transpose(0, 2, 1),
        owner[:, :, 0],
        local_slice,
        block_index,
        weight_index,
        fitting.T,
    )


def local(layers, table, fitting, owner, local_slice, block_index, weight_index):
    arguments = (layers, table, fitting, owner, local_slice, block_index, weight_index)
    entries, peers, group = owner.shape[1], lax.axis_size("row"), lax.axis_size("layer")
    _, points, block_rows = table.shape
    raw_rows = max(2, 2 * entries // peers) * block_rows
    reduced_rows = fitting.shape[0] // group
    slices = peers * fitting.shape[0] // points
    fits = points == 128 and block_rows == 64 and layers.shape[2] == 256
    fits = fits and entries <= 128 and slices <= 128
    if group == 4 and peers == 4 and raw_rows > reduced_rows and fits:
        return local_fused(*arguments)
    return local_rows(*arguments)


def solution(mesh):
    return jax.shard_map(
        local,
        mesh=mesh,
        in_specs=(
            P("layer", "row", "panel"),
            P(),
            P("row", "layer"),
            P("layer", "row", None),
            P("layer", "row"),
            P("layer", "row"),
            P("layer", "row"),
        ),
        out_specs=P(("panel", "row"), "layer"),
        check_vma=False,
    )
```

```python
import functools

import jax
import jax.numpy as jnp
from jax import lax
from jax.experimental import pallas as pl
from jax.experimental.pallas import tpu as pltpu

MESH = pl.DeviceIdType.MESH
from jax.sharding import PartitionSpec as P


def local_rows(layers, table, fitting, owner, local_slice, block_index, weight_index):
    rows_dev = layers.shape[1]
    columns = layers.shape[2]
    slice_rows = table.shape[1]
    block_rows = table.shape[2]
    entries = owner.shape[1]
    peer_count = lax.axis_size("row")
    capacity = max(2, 2 * entries // peer_count)
    slot_count = peer_count * capacity
    owned_slices = fitting.shape[0] // slice_rows
    owner_now = owner[0, :, 0]
    local_now = local_slice[0]
    owner_match = (owner_now[:, None] == jnp.arange(peer_count, dtype=jnp.int32)[None, :]).astype(
        jnp.int32
    )
    slot_rank = jnp.sum((jnp.cumsum(owner_match, axis=0) - 1) * owner_match, axis=1)
    target = owner_now * capacity + slot_rank
    placed = target[None, :] == jnp.arange(slot_count, dtype=jnp.int32)[:, None]
    filled = jnp.any(placed, axis=1)
    source = jnp.sum(jnp.where(placed, jnp.arange(entries, dtype=jnp.int32)[None, :], 0), axis=1)
    send_local = jnp.where(filled, local_now[source], -1).reshape(peer_count, capacity)
    grouped = layers[0].reshape(rows_dev // block_rows, block_rows, columns)
    picked = grouped[block_index[0][source]].reshape(peer_count, capacity, block_rows, columns)
    send_weight = weight_index[0][source].reshape(peer_count, capacity)
    got_rows, got_weight, got_local = (
        lax.all_to_all(picked, "row", split_axis=0, concat_axis=0, tiled=True),
        lax.all_to_all(send_weight, "row", split_axis=0, concat_axis=0, tiled=True),
        lax.all_to_all(send_local, "row", split_axis=0, concat_axis=0, tiled=True),
    )
    pupil_terms = jnp.einsum(
        "ksb,kbc->ksc",
        table[got_weight.reshape(-1)],
        got_rows.reshape(slot_count, block_rows, columns),
        preferred_element_type=jnp.float32,
    ).astype(jnp.bfloat16)
    selector = (
        jnp.arange(owned_slices, dtype=jnp.int32)[:, None] == got_local.reshape(-1)[None, :]
    ).astype(jnp.bfloat16)
    partial_pupil = jnp.dot(
        selector,
        pupil_terms.reshape(slot_count, slice_rows * columns),
        preferred_element_type=jnp.float32,
    ).reshape(owned_slices * slice_rows, columns)
    pupil_rounded = lax.psum(partial_pupil, "layer").astype(jnp.bfloat16)
    return lax.psum_scatter(
        lax.dot_general(
            pupil_rounded, fitting, (((0,), (0,)), ((), ())), preferred_element_type=jnp.float32
        ),
        "row",
        scatter_dimension=0,
        tiled=True,
    ).astype(jnp.bfloat16)


def index_table(owner, local_slice, block, weight, owned, weights, slices, out_ref):
    entries = owner.shape[1]
    square = (entries, entries)
    down = lax.broadcasted_iota(jnp.int32, square, 0)
    along = lax.broadcasted_iota(jnp.int32, square, 1)

    def upright(row):
        return jnp.sum(jnp.where(down == along, jnp.broadcast_to(row, square), 0), axis=1, keepdims=True)

    place = owner * owned + local_slice
    place_up = upright(place)
    place_row = jnp.broadcast_to(place, square)
    twin = (place_row == place_up) & (along < down)
    rank = jnp.sum(((place_row < place_up) | twin).astype(jnp.int32), axis=1, keepdims=True)
    follows = (jnp.sum(twin.astype(jnp.int32), axis=1, keepdims=True) > 0).astype(jnp.int32)
    code = upright(block * weights + weight)
    moved = rank == along
    code = jnp.sum(jnp.where(moved, jnp.broadcast_to(code, square), 0), axis=0, keepdims=True)
    follows = jnp.sum(jnp.where(moved, jnp.broadcast_to(follows, square), 0), axis=0, keepdims=True)
    names = lax.broadcasted_iota(jnp.int32, (entries, slices), 1)
    place_wide = jnp.broadcast_to(place_up, (entries, slices))
    until = jnp.sum((place_wide <= names).astype(jnp.int32), axis=0, keepdims=True)
    held = jnp.sum((place_wide == names).astype(jnp.int32), axis=0, keepdims=True)
    block = code // weights
    out_ref[0:1, 0:entries] = block // 2
    out_ref[1:2, 0:entries] = (block % 2) * weights + code % weights
    out_ref[2:3, 0:entries] = follows
    out_ref[3:4, 0:slices] = jnp.where(held > 0, until, 0)


def fused_kernel(
    peers, owned, chunks, groups, units,
    layers_hbm, table_hbm, owner_hbm, local_hbm, block_hbm, weight_hbm, fitting_hbm, result,
    other_raw, own_raw, turned_ref, owner_ref, local_ref, block_ref, weight_ref,
    own_turned, wide_table, own_sums, got_sums, meta, own_index, got_index,
    fit, left, total, own_part, chunk_refs, unit_refs,
    in_sem, meta_sem, swap_sem, core_sem, row_send, row_recv, layer_send, layer_recv, end_send, end_recv,
):
    row = lax.axis_index("row")
    me = lax.axis_index("layer")
    core = lax.rem(me, 2)
    side = me // 2
    half = other_raw.shape[1]
    width = fit.shape[0]
    weights, block_rows, points = turned_ref.shape
    pairs = own_turned.shape[0]
    entries = owner_ref.shape[1]
    half_owned = owned // 2
    slices = peers * owned
    step_entries = 8 if entries % 8 == 0 else 1
    owner_width = half // 2
    mate = row + 1 - 2 * lax.rem(row, 2)
    cross = lax.rem(row + 2, peers)
    opposite = peers - 1 - row
    is_end = jnp.logical_or(row == 0, row == peers - 1)
    is_middle = jnp.logical_not(is_end)
    layer_peers = [lax.rem(me + k, 4) for k in range(1, 4)]
    partner = layer_peers[1]
    sibling = me + 1 - 2 * core
    order = (opposite, cross, mate, row)
    swapped = range(1, len(chunks))

    first_own = pl.multiple_of(side * half, half)
    first_other = pl.multiple_of((1 - side) * half, half)
    small_copies = [
        pltpu.make_async_copy(source, target, in_sem.at[4 + index])
        for index, (source, target) in enumerate(
            (
                (owner_hbm, owner_ref),
                (local_hbm, local_ref),
                (block_hbm, block_ref),
                (weight_hbm, weight_ref),
            )
        )
    ]
    other_copy = pltpu.make_async_copy(layers_hbm.at[:, pl.ds(first_other, half)], other_raw, in_sem.at[0])
    own_copy = pltpu.make_async_copy(layers_hbm.at[:, pl.ds(first_own, half)], own_raw, in_sem.at[1])
    table_copy = pltpu.make_async_copy(table_hbm, turned_ref, in_sem.at[2])
    fit_copy = pltpu.make_async_copy(fitting_hbm, fit, in_sem.at[3])
    for copy in small_copies:
        copy.start()
    other_copy.start()
    own_copy.start()
    table_copy.start()

    barrier = pltpu.get_barrier_semaphore()
    for peer in (mate, 2 - row // 2):
        pl.semaphore_signal(barrier, inc=1, device_id={"row": peer}, device_id_type=MESH)
    for peer in layer_peers:
        pl.semaphore_signal(barrier, inc=1, device_id={"layer": peer}, device_id_type=MESH)

    def remote(source, target, send, recv, axis, peer):
        return pltpu.make_async_remote_copy(
            src_ref=source,
            dst_ref=target,
            send_sem=send,
            recv_sem=recv,
            device_id={axis: peer},
            device_id_type=MESH,
        )

    def all_of(ref, sem):
        return remote(ref, ref, sem, sem, "layer", partner)

    def turn(raw, targets, early):
        low, high = chunks[0]["parts"][0][1:]
        early_rows = pl.ds(pl.multiple_of(early * (high - low), high - low), high - low)

        def body(pair, carry):
            turned = raw[pl.ds(pl.multiple_of(pair * points, points), points), :].T
            for chunk, target, base in targets:
                for part, start, stop in chunks[chunk]["parts"]:
                    first = part * owner_width + start
                    target[pair, base : base + stop - start, :] = turned[first : first + stop - start]
                    base += stop - start
            own_turned[pair, early_rows, :] = turned[low:high]
            return carry

        lax.fori_loop(0, pairs, body, 0, unroll=4)

    def sum_terms(index_ref, rows_ref, sums_ref, low, high):
        def body(step, carry):
            terms = []
            for offset in range(step_entries):
                entry = step * step_entries + offset
                terms.append(
                    jnp.dot(
                        rows_ref[index_ref[0, entry], low:high, :],
                        wide_table[index_ref[1, entry]],
                        preferred_element_type=jnp.float32,
                    )
                )
            running = sums_ref[step * step_entries, low:high, :]
            for offset in range(step_entries):
                entry = step * step_entries + offset
                running = terms[offset] + index_ref[2, entry].astype(jnp.float32) * running
                sums_ref[entry + 1, low:high, :] = running
            return carry

        lax.fori_loop(0, entries // step_entries, body, 0)

    def core_copy(chunk):
        refs = chunk_refs[chunk]
        sems = (core_sem.at[0, chunk], core_sem.at[1, chunk])
        return remote(refs["core_out"], refs["core_in"], *sems, "layer", sibling)

    def row_copy(chunk, slot, source, peer):
        refs = chunk_refs[chunk]
        sems = (row_send.at[chunk], row_recv.at[chunk, max(slot, 1) - 1])
        return remote(refs["row_out"].at[source], refs["row_in"].at[slot], *sems, "row", peer)

    def layer_copy(chunk, k):
        pieces = chunk_refs[chunk]["pieces"]
        sems = (layer_send.at[chunk], layer_recv.at[chunk])
        return remote(pieces.at[me], pieces.at[me], *sems, "layer", layer_peers[k])

    def end_copy(unit, slot, source, peer):
        refs = unit_refs[unit]
        sems = (end_send.at[unit], end_recv.at[unit, max(slot, 1) - 1])
        return remote(refs["product"].at[source], refs["landed"].at[slot], *sems, "row", peer)

    def rows_of(chunk):
        base = chunks[chunk]["base"]
        return slice(base, base + chunks[chunk]["columns"])

    def partial(chunk, owner, which, index):
        name = owner * owned + which * half_owned + index
        value = own_sums[own_index[3, name], rows_of(chunk), :]
        if chunk > 0:
            value = value + got_sums[got_index[3, name], 0 : chunks[chunk]["columns"], :]
        return value

    def begin(chunk):
        swaps[chunk].wait_recv()
        sum_terms(got_index, chunk_refs[chunk]["swap_in"], got_sums, 0, chunks[chunk]["columns"])

    def share(chunk):
        refs = chunk_refs[chunk]
        for place, owner in enumerate(order):

            def body(index, carry):
                refs["core_out"][place, index] = partial(chunk, owner, 1 - core, index).astype(jnp.bfloat16)
                return carry

            lax.fori_loop(0, half_owned, body, 0, unroll=4)
        core_copy(chunk).start()

    def spread(chunk):
        refs = chunk_refs[chunk]
        core_copy(chunk).wait_recv()
        for place, owner in enumerate(order):

            def body(index, carry):
                value = partial(chunk, owner, core, index) + refs["core_in"][place, index].astype(jnp.float32)
                if place < 3:
                    refs["row_out"][place, index] = value.astype(jnp.bfloat16)
                else:
                    own_part[index, rows_of(chunk), :] = value
                return carry

            lax.fori_loop(0, half_owned, body, 0, unroll=4)
            if place < 2:

                @pl.when(is_end)
                def _():
                    row_copy(chunk, 2 + place, place, mate).start()

            elif place == 2:
                row_copy(chunk, 0, 2, mate).start()

    def join(chunk, place):
        refs = chunk_refs[chunk]
        slot = 3 - place

        @pl.when(is_middle)
        def _():
            row_copy(chunk, slot, place, mate).wait_recv()
            refs["row_out"][place] = (
                refs["row_out"][place].astype(jnp.float32) + refs["row_in"][slot].astype(jnp.float32)
            ).astype(jnp.bfloat16)
            row_copy(chunk, 1, place, order[place]).start()

    def settle(chunk):
        refs = chunk_refs[chunk]
        all_of(refs["row_in"].at[0:2], row_recv.at[chunk, 0]).wait_recv()
        value = own_part[:, rows_of(chunk), :]
        for slot in range(2):
            value = value + refs["row_in"][slot].astype(jnp.float32)
        refs["pieces"][me] = value.astype(jnp.bfloat16)
        for k in (1, 0, 2):
            layer_copy(chunk, k).start()

    def gather(number):
        low, high, members = groups[number]
        size = high - low
        for chunk in members:
            pieces = chunk_refs[chunk]["pieces"]
            all_of(pieces.at[0:3], layer_recv.at[chunk]).wait_recv()
            for which in range(2):
                for index in range(half_owned):
                    first = (which * half_owned + index) * points
                    lanes = slice(first, first + points)
                    if chunk == 0:
                        value = pieces[which, index].astype(jnp.float32)
                        value = (value + pieces[2 + which, index].astype(jnp.float32)).astype(jnp.bfloat16)
                        left[0:size, lanes] = value[0:size]
                        left[2 * size : 3 * size, lanes] = value[size:]
                        continue
                    for far in range(2):
                        value = pieces[2 * far + which, index]
                        for place, (part, _, _) in enumerate(chunks[chunk]["parts"]):
                            target = (2 * far + part) * size
                            left[target : target + size, lanes] = value[place * size : (place + 1) * size]

    def multiply(unit):
        number, begins, ends = units[unit]
        low, high, _ = groups[number]
        for start in range(begins, ends, 256):
            stop = min(start + 256, ends)
            total[4 * low : 4 * high, start:stop] = lax.dot_general(
                left[0 : 4 * (high - low), :],
                fit[start:stop, :],
                (((1,), (1,)), ((), ())),
                preferred_element_type=jnp.float32,
            )

    def total_of(unit, owner):
        number, begins, ends = units[unit]
        low, high, _ = groups[number]
        size = high - low
        return total[pl.ds(pl.multiple_of(4 * low + owner * size, size), size), begins:ends]

    def deliver(unit):
        product = unit_refs[unit]["product"]
        _, begins, ends = units[unit]
        _, size, padded = product.shape
        if ends - begins < padded:
            product[:, :, padded - 128 :] = jnp.zeros((3, size, 128), jnp.bfloat16)

        def fill(place):
            product[place, :, 0 : ends - begins] = total_of(unit, order[place]).astype(jnp.bfloat16)

        @pl.when(is_end)
        def _():
            for place in range(2):
                fill(place)
                end_copy(unit, 2 + place, place, mate).start()

        fill(2)
        end_copy(unit, 0, 2, mate).start()

    def pass_on(unit):
        product, landed = unit_refs[unit]["product"], unit_refs[unit]["landed"]
        _, begins, ends = units[unit]
        lanes = slice(0, ends - begins)

        @pl.when(is_middle)
        def _():
            for place in (1, 0):
                slot = 3 - place
                end_copy(unit, slot, place, mate).wait_recv()
                product[place, :, lanes] = (
                    total_of(unit, order[place]) + landed[slot, :, lanes].astype(jnp.float32)
                ).astype(jnp.bfloat16)
                end_copy(unit, 1, place, order[place]).start()

    def finish(unit):
        landed = unit_refs[unit]["landed"]
        number, begins, ends = units[unit]
        low, high, _ = groups[number]
        all_of(landed.at[0:2], end_recv.at[unit, 0]).wait_recv()
        value = total_of(unit, row)
        for slot in range(2):
            value = value + landed[slot, :, 0 : ends - begins].astype(jnp.float32)
        result[low:high, begins:ends] = value.astype(result.dtype)

    for copy in small_copies:
        copy.wait()
    index_table(
        owner_ref[...], local_ref[...], block_ref[...], weight_ref[...], owned, weights, slices, meta
    )
    index_copy = pltpu.make_async_copy(meta, own_index, meta_sem.at[2])
    index_copy.start()
    other_copy.wait()
    turn(other_raw, [(chunk, chunk_refs[chunk]["swap_out"], 0) for chunk in swapped], 1 - side)
    pl.semaphore_wait(barrier, 4 + 2 * lax.rem((row + 1) // 2, 2))
    meta_copy = remote(meta, got_index, meta_sem.at[0], meta_sem.at[1], "layer", partner)
    meta_copy.start()
    swaps = {
        chunk: remote(
            chunk_refs[chunk]["swap_out"],
            chunk_refs[chunk]["swap_in"],
            swap_sem.at[0, chunk - 1],
            swap_sem.at[1, chunk - 1],
            "layer",
            partner,
        )
        for chunk in swapped
    }
    for copy in swaps.values():
        copy.start()
    own_copy.wait()
    turn(own_raw, [(chunk, own_turned, chunks[chunk]["base"]) for chunk in swapped], side)
    wide_table[...] = jnp.zeros_like(wide_table)
    table_copy.wait()
    for index in range(weights):
        wide_table[index, 0:block_rows, :] = turned_ref[index]
        wide_table[weights + index, block_rows:, :] = turned_ref[index]
    own_sums[0] = jnp.zeros(own_sums.shape[1:], own_sums.dtype)
    got_sums[0] = jnp.zeros(got_sums.shape[1:], got_sums.dtype)
    index_copy.wait()
    early_rows = chunks[0]["columns"]
    sum_terms(own_index, own_turned, own_sums, 0, early_rows)
    share(0)
    spread(0)
    sum_terms(own_index, own_turned, own_sums, early_rows, own_turned.shape[1])
    meta_copy.wait_recv()
    begin(1)
    share(1)
    join(0, 1)
    spread(1)
    join(0, 0)
    fit_copy.start()
    begin(2)
    share(2)
    join(1, 1)
    spread(2)
    join(1, 0)
    begin(3)
    share(3)
    settle(0)
    spread(3)
    join(2, 1)
    settle(1)
    begin(4)
    share(4)
    join(2, 0)
    spread(4)
    join(3, 1)
    settle(2)
    fit_copy.wait()
    gather(0)
    multiply(0)
    join(3, 0)
    deliver(0)
    join(4, 1)
    join(4, 0)
    settle(3)
    gather(1)
    multiply(1)
    deliver(1)
    settle(4)
    pass_on(0)
    gather(2)
    multiply(2)
    deliver(2)
    pass_on(1)
    gather(3)
    multiply(3)
    deliver(3)
    multiply(4)
    deliver(4)
    pass_on(2)
    finish(0)
    finish(1)
    pass_on(3)
    pass_on(4)
    finish(2)
    finish(3)
    finish(4)

    meta_copy.wait_send()
    for copy in swaps.values():
        copy.wait_send()
    for chunk, refs in enumerate(chunk_refs):
        core_copy(chunk).wait_send()
        all_of(refs["row_out"], row_send.at[chunk]).wait_send()
        all_of(refs["pieces"].at[0:3], layer_send.at[chunk]).wait_send()
    for unit, refs in enumerate(unit_refs):
        all_of(refs["product"], end_send.at[unit]).wait_send()


def plan_of(out_rows, width):
    cut = out_rows // 4
    marks = [cut * index for index in range(5)]
    spans = list(zip(marks[:-1], marks[1:]))
    low, high = spans[0]
    parts = [[(0, low, high)], [(1, low, high)]]
    parts += [[(0, start, stop), (1, start, stop)] for start, stop in spans[1:]]
    chunks, base = [], 0
    for number, part in enumerate(parts):
        columns = sum(stop - start for _, start, stop in part)
        if number == 0:
            columns = 2 * columns
        chunks.append({"parts": part, "columns": columns, "base": base})
        base += columns
    groups = [(low, high, (0, 1))]
    groups += [(start, stop, (number + 2,)) for number, (start, stop) in enumerate(spans[1:])]
    middle = width // 512 * 256
    units = [(number, 0, width) for number in range(len(groups) - 1)]
    units += [(len(groups) - 1, 0, middle), (len(groups) - 1, middle, width)]
    return chunks, groups, units, base


def local_fused(layers, table, fitting, owner, local_slice, block_index, weight_index):
    rows_dev, columns = layers.shape[1:]
    weights, points, block_rows = table.shape
    entries = owner.shape[1]
    peers = lax.axis_size("row")
    depth, width = fitting.shape
    owned = depth // points
    half = columns // 2
    out_rows = columns // peers
    pairs = rows_dev // points
    chunks, groups, units, held = plan_of(out_rows, width)
    bf16, f32 = jnp.bfloat16, jnp.float32
    dma = pltpu.SemaphoreType.DMA

    def chunk_scratch(number):
        cols = chunks[number]["columns"]
        slots = owned // 2
        refs = {
            "core_out": pltpu.VMEM((4, slots, cols, points), bf16),
            "core_in": pltpu.VMEM((4, slots, cols, points), bf16),
            "row_out": pltpu.VMEM((3, slots, cols, points), bf16),
            "row_in": pltpu.VMEM((4, slots, cols, points), bf16),
            "pieces": pltpu.VMEM((4, slots, cols, points), bf16),
        }
        if number > 0:
            refs["swap_out"] = pltpu.VMEM((pairs, cols, points), bf16)
            refs["swap_in"] = pltpu.VMEM((pairs, cols, points), bf16)
        return refs

    def unit_scratch(unit):
        number, begins, ends = unit
        low, high, _ = groups[number]
        padded = -(-(ends - begins) // 128) * 128
        return {
            "product": pltpu.VMEM((3, high - low, padded), bf16),
            "landed": pltpu.VMEM((4, high - low, padded), bf16),
        }

    widest = max(chunk["columns"] for chunk in chunks[1:])
    tallest = max(4 * (high - low) for low, high, _ in groups)
    hbm = pl.BlockSpec(memory_space=pltpu.HBM)
    vmem = pl.BlockSpec(memory_space=pltpu.VMEM)
    return pl.pallas_call(
        functools.partial(fused_kernel, peers, owned, chunks, groups, units),
        out_shape=pltpu.VMEM((out_rows, width), bf16),
        in_specs=[hbm] * 7,
        out_specs=vmem,
        scratch_shapes=[
            pltpu.VMEM((rows_dev, half), bf16),
            pltpu.VMEM((rows_dev, half), bf16),
            pltpu.VMEM((weights, block_rows, points), bf16),
            pltpu.VMEM((1, entries), jnp.int32),
            pltpu.VMEM((1, entries), jnp.int32),
            pltpu.VMEM((1, entries), jnp.int32),
            pltpu.VMEM((1, entries), jnp.int32),
            pltpu.VMEM((pairs, held, points), bf16),
            pltpu.VMEM((2 * weights, points, points), bf16),
            pltpu.VMEM((entries + 1, held, points), f32),
            pltpu.VMEM((entries + 1, widest, points), f32),
            pltpu.VMEM((8, 128), jnp.int32),
            pltpu.SMEM((8, 128), jnp.int32),
            pltpu.SMEM((8, 128), jnp.int32),
            pltpu.VMEM((width, depth), bf16),
            pltpu.VMEM((tallest, depth), bf16),
            pltpu.VMEM((columns, width), f32),
            pltpu.VMEM((owned // 2, held, points), f32),
            [chunk_scratch(number) for number in range(len(chunks))],
            [unit_scratch(unit) for unit in units],
            dma((8,)),
            dma((3,)),
            dma((2, len(chunks) - 1)),
            dma((2, len(chunks))),
            dma((len(chunks),)),
            dma((len(chunks), 3)),
            dma((len(chunks),)),
            dma((len(chunks),)),
            dma((len(units),)),
            dma((len(units), 3)),
        ],
        compiler_params=pltpu.CompilerParams(
            collective_id=0, has_side_effects=True
        ),
    )(
        layers[0],
        table.transpose(0, 2, 1),
        owner[:, :, 0],
        local_slice,
        block_index,
        weight_index,
        fitting.T,
    )


def local(layers, table, fitting, owner, local_slice, block_index, weight_index):
    arguments = (layers, table, fitting, owner, local_slice, block_index, weight_index)
    entries, peers, group = owner.shape[1], lax.axis_size("row"), lax.axis_size("layer")
    _, points, block_rows = table.shape
    raw_rows = max(2, 2 * entries // peers) * block_rows
    reduced_rows = fitting.shape[0] // group
    slices = peers * fitting.shape[0] // points
    fits = points == 128 and block_rows == 64 and layers.shape[2] == 256
    fits = fits and entries <= 128 and slices <= 128
    if group == 4 and peers == 4 and raw_rows > reduced_rows and fits:
        return local_fused(*arguments)
    return local_rows(*arguments)


def solution(mesh):
    return jax.shard_map(
        local,
        mesh=mesh,
        in_specs=(
            P("layer", "row", "panel"),
            P(),
            P("row", "layer"),
            P("layer", "row", None),
            P("layer", "row"),
            P("layer", "row"),
            P("layer", "row"),
        ),
        out_specs=P(("panel", "row"), "layer"),
        check_vma=False,
    )
```

```python
import functools

import jax
import jax.numpy as jnp
from jax import lax
from jax.experimental import pallas as pl
from jax.experimental.pallas import tpu as pltpu

MESH = pl.DeviceIdType.MESH
from jax.sharding import PartitionSpec as P


def local_rows(layers, table, fitting, owner, local_slice, block_index, weight_index):
    rows_dev = layers.shape[1]
    columns = layers.shape[2]
    slice_rows = table.shape[1]
    block_rows = table.shape[2]
    entries = owner.shape[1]
    peer_count = lax.axis_size("row")
    capacity = max(2, 2 * entries // peer_count)
    slot_count = peer_count * capacity
    owned_slices = fitting.shape[0] // slice_rows
    owner_now = owner[0, :, 0]
    local_now = local_slice[0]
    owner_match = (owner_now[:, None] == jnp.arange(peer_count, dtype=jnp.int32)[None, :]).astype(
        jnp.int32
    )
    slot_rank = jnp.sum((jnp.cumsum(owner_match, axis=0) - 1) * owner_match, axis=1)
    target = owner_now * capacity + slot_rank
    placed = target[None, :] == jnp.arange(slot_count, dtype=jnp.int32)[:, None]
    filled = jnp.any(placed, axis=1)
    source = jnp.sum(jnp.where(placed, jnp.arange(entries, dtype=jnp.int32)[None, :], 0), axis=1)
    send_local = jnp.where(filled, local_now[source], -1).reshape(peer_count, capacity)
    grouped = layers[0].reshape(rows_dev // block_rows, block_rows, columns)
    picked = grouped[block_index[0][source]].reshape(peer_count, capacity, block_rows, columns)
    send_weight = weight_index[0][source].reshape(peer_count, capacity)
    got_rows, got_weight, got_local = (
        lax.all_to_all(picked, "row", split_axis=0, concat_axis=0, tiled=True),
        lax.all_to_all(send_weight, "row", split_axis=0, concat_axis=0, tiled=True),
        lax.all_to_all(send_local, "row", split_axis=0, concat_axis=0, tiled=True),
    )
    pupil_terms = jnp.einsum(
        "ksb,kbc->ksc",
        table[got_weight.reshape(-1)],
        got_rows.reshape(slot_count, block_rows, columns),
        preferred_element_type=jnp.float32,
    ).astype(jnp.bfloat16)
    selector = (
        jnp.arange(owned_slices, dtype=jnp.int32)[:, None] == got_local.reshape(-1)[None, :]
    ).astype(jnp.bfloat16)
    partial_pupil = jnp.dot(
        selector,
        pupil_terms.reshape(slot_count, slice_rows * columns),
        preferred_element_type=jnp.float32,
    ).reshape(owned_slices * slice_rows, columns)
    pupil_rounded = lax.psum(partial_pupil, "layer").astype(jnp.bfloat16)
    return lax.psum_scatter(
        lax.dot_general(
            pupil_rounded, fitting, (((0,), (0,)), ((), ())), preferred_element_type=jnp.float32
        ),
        "row",
        scatter_dimension=0,
        tiled=True,
    ).astype(jnp.bfloat16)


def index_table(owner, local_slice, block, weight, owned, weights, slices, out_ref):
    entries = owner.shape[1]
    square = (entries, entries)
    down = lax.broadcasted_iota(jnp.int32, square, 0)
    along = lax.broadcasted_iota(jnp.int32, square, 1)

    def upright(row):
        return jnp.sum(jnp.where(down == along, jnp.broadcast_to(row, square), 0), axis=1, keepdims=True)

    place = owner * owned + local_slice
    place_up = upright(place)
    place_row = jnp.broadcast_to(place, square)
    twin = (place_row == place_up) & (along < down)
    rank = jnp.sum(((place_row < place_up) | twin).astype(jnp.int32), axis=1, keepdims=True)
    follows = (jnp.sum(twin.astype(jnp.int32), axis=1, keepdims=True) > 0).astype(jnp.int32)
    code = upright(block * weights + weight)
    moved = rank == along
    code = jnp.sum(jnp.where(moved, jnp.broadcast_to(code, square), 0), axis=0, keepdims=True)
    follows = jnp.sum(jnp.where(moved, jnp.broadcast_to(follows, square), 0), axis=0, keepdims=True)
    names = lax.broadcasted_iota(jnp.int32, (entries, slices), 1)
    place_wide = jnp.broadcast_to(place_up, (entries, slices))
    until = jnp.sum((place_wide <= names).astype(jnp.int32), axis=0, keepdims=True)
    held = jnp.sum((place_wide == names).astype(jnp.int32), axis=0, keepdims=True)
    block = code // weights
    out_ref[0:1, 0:entries] = block // 2
    out_ref[1:2, 0:entries] = (block % 2) * weights + code % weights
    out_ref[2:3, 0:entries] = follows
    out_ref[3:4, 0:slices] = jnp.where(held > 0, until, 0)


def fused_kernel(
    peers, owned, chunks, groups, units,
    layers_hbm, table_hbm, owner_hbm, local_hbm, block_hbm, weight_hbm, fitting_hbm, result,
    other_raw, own_raw, turned_ref, owner_ref, local_ref, block_ref, weight_ref,
    own_turned, wide_table, own_sums, got_sums, meta, own_index, got_index,
    fit, left, total, own_part, chunk_refs, unit_refs,
    in_sem, meta_sem, swap_sem, core_sem, row_send, row_recv, layer_send, layer_recv, end_send, end_recv,
):
    row = lax.axis_index("row")
    me = lax.axis_index("layer")
    core = lax.rem(me, 2)
    side = me // 2
    half = other_raw.shape[1]
    width = fit.shape[0]
    weights, block_rows, points = turned_ref.shape
    pairs = own_turned.shape[0]
    entries = owner_ref.shape[1]
    half_owned = owned // 2
    slices = peers * owned
    step_entries = 8 if entries % 8 == 0 else 1
    owner_width = half // 2
    mate = row + 1 - 2 * lax.rem(row, 2)
    cross = lax.rem(row + 2, peers)
    opposite = peers - 1 - row
    is_end = jnp.logical_or(row == 0, row == peers - 1)
    is_middle = jnp.logical_not(is_end)
    layer_peers = [lax.rem(me + k, 4) for k in range(1, 4)]
    partner = layer_peers[1]
    sibling = me + 1 - 2 * core
    order = (opposite, cross, mate, row)
    swapped = range(1, len(chunks))
    late_chunks = (len(chunks) - 2, len(chunks) - 1)

    first_own = pl.multiple_of(side * half, half)
    first_other = pl.multiple_of((1 - side) * half, half)
    small_copies = [
        pltpu.make_async_copy(source, target, in_sem.at[4 + index])
        for index, (source, target) in enumerate(
            (
                (owner_hbm, owner_ref),
                (local_hbm, local_ref),
                (block_hbm, block_ref),
                (weight_hbm, weight_ref),
            )
        )
    ]
    other_copy = pltpu.make_async_copy(layers_hbm.at[:, pl.ds(first_other, half)], other_raw, in_sem.at[0])
    own_copy = pltpu.make_async_copy(layers_hbm.at[:, pl.ds(first_own, half)], own_raw, in_sem.at[1])
    table_copy = pltpu.make_async_copy(table_hbm, turned_ref, in_sem.at[2])
    fit_copy = pltpu.make_async_copy(fitting_hbm, fit, in_sem.at[3])
    for copy in small_copies:
        copy.start()
    other_copy.start()
    own_copy.start()
    table_copy.start()

    barrier = pltpu.get_barrier_semaphore()
    for peer in (mate, 2 - row // 2):
        pl.semaphore_signal(barrier, inc=1, device_id={"row": peer}, device_id_type=MESH)
    for peer in layer_peers:
        pl.semaphore_signal(barrier, inc=1, device_id={"layer": peer}, device_id_type=MESH)

    def remote(source, target, send, recv, axis, peer):
        return pltpu.make_async_remote_copy(
            src_ref=source,
            dst_ref=target,
            send_sem=send,
            recv_sem=recv,
            device_id={axis: peer},
            device_id_type=MESH,
        )

    def all_of(ref, sem):
        return remote(ref, ref, sem, sem, "layer", partner)

    def turn(raw, targets, early):
        low, high = chunks[0]["parts"][0][1:]
        early_rows = pl.ds(pl.multiple_of(early * (high - low), high - low), high - low)

        def body(pair, carry):
            turned = raw[pl.ds(pl.multiple_of(pair * points, points), points), :].T
            for chunk, target, base in targets:
                for part, start, stop in chunks[chunk]["parts"]:
                    first = part * owner_width + start
                    target[pair, base : base + stop - start, :] = turned[first : first + stop - start]
                    base += stop - start
            own_turned[pair, early_rows, :] = turned[low:high]
            return carry

        lax.fori_loop(0, pairs, body, 0, unroll=4)

    def sum_terms(index_ref, rows_ref, sums_ref, low, high):
        def body(step, carry):
            terms = []
            for offset in range(step_entries):
                entry = step * step_entries + offset
                terms.append(
                    jnp.dot(
                        rows_ref[index_ref[0, entry], low:high, :],
                        wide_table[index_ref[1, entry]],
                        preferred_element_type=jnp.float32,
                    )
                )
            running = sums_ref[step * step_entries, low:high, :]
            for offset in range(step_entries):
                entry = step * step_entries + offset
                running = terms[offset] + index_ref[2, entry].astype(jnp.float32) * running
                sums_ref[entry + 1, low:high, :] = running
            return carry

        lax.fori_loop(0, entries // step_entries, body, 0)

    def core_copy(chunk):
        refs = chunk_refs[chunk]
        sems = (core_sem.at[0, chunk], core_sem.at[1, chunk])
        return remote(refs["core_out"], refs["core_in"], *sems, "layer", sibling)

    def row_copy(chunk, slot, source, peer):
        refs = chunk_refs[chunk]
        sems = (row_send.at[chunk], row_recv.at[chunk, max(slot, 1) - 1])
        return remote(refs["row_out"].at[source], refs["row_in"].at[slot], *sems, "row", peer)

    def layer_copy(chunk, k):
        pieces = chunk_refs[chunk]["pieces"]
        sems = (layer_send.at[chunk], layer_recv.at[chunk])
        return remote(pieces.at[me], pieces.at[me], *sems, "layer", layer_peers[k])

    def end_copy(unit, slot, source, peer):
        refs = unit_refs[unit]
        sems = (end_send.at[unit], end_recv.at[unit, max(slot, 1) - 1])
        return remote(refs["product"].at[source], refs["landed"].at[slot], *sems, "row", peer)

    def rows_of(chunk):
        base = chunks[chunk]["base"]
        return slice(base, base + chunks[chunk]["columns"])

    def partial(chunk, owner, which, index):
        name = owner * owned + which * half_owned + index
        value = own_sums[own_index[3, name], rows_of(chunk), :]
        if chunk > 0:
            value = value + got_sums[got_index[3, name], 0 : chunks[chunk]["columns"], :]
        return value

    def begin(chunk):
        swaps[chunk].wait_recv()
        sum_terms(got_index, chunk_refs[chunk]["swap_in"], got_sums, 0, chunks[chunk]["columns"])

    def share(chunk):
        refs = chunk_refs[chunk]
        for place, owner in enumerate(order):

            def body(index, carry):
                refs["core_out"][place, index] = partial(chunk, owner, 1 - core, index).astype(jnp.bfloat16)
                return carry

            lax.fori_loop(0, half_owned, body, 0, unroll=4)
        core_copy(chunk).start()

    def spread(chunk):
        refs = chunk_refs[chunk]
        core_copy(chunk).wait_recv()
        for place, owner in enumerate(order):

            def body(index, carry):
                value = partial(chunk, owner, core, index) + refs["core_in"][place, index].astype(jnp.float32)
                if place < 3:
                    refs["row_out"][place, index] = value.astype(jnp.bfloat16)
                else:
                    own_part[index, rows_of(chunk), :] = value
                return carry

            lax.fori_loop(0, half_owned, body, 0, unroll=4)
            if place < 2:

                @pl.when(is_end)
                def _():
                    row_copy(chunk, 2 + place, place, mate).start()

            elif place == 2 and chunk not in late_chunks:
                row_copy(chunk, 0, 2, mate).start()
        if chunk == late_chunks[-1]:
            for late in late_chunks:
                row_copy(late, 0, 2, mate).start()

    def join(chunk, place):
        refs = chunk_refs[chunk]
        slot = 3 - place

        @pl.when(is_middle)
        def _():
            row_copy(chunk, slot, place, mate).wait_recv()
            refs["row_out"][place] = (
                refs["row_out"][place].astype(jnp.float32) + refs["row_in"][slot].astype(jnp.float32)
            ).astype(jnp.bfloat16)
            row_copy(chunk, 1, place, order[place]).start()

    def settle(chunk, when=None):
        refs = chunk_refs[chunk]

        def run():
            all_of(refs["row_in"].at[0:2], row_recv.at[chunk, 0]).wait_recv()
            value = own_part[:, rows_of(chunk), :]
            for slot in range(2):
                value = value + refs["row_in"][slot].astype(jnp.float32)
            refs["pieces"][me] = value.astype(jnp.bfloat16)
            for k in (1, 0, 2):
                layer_copy(chunk, k).start()

        if when is None:
            run()
        else:
            pl.when(when)(run)

    def gather(number):
        low, high, members = groups[number]
        size = high - low
        for chunk in members:
            pieces = chunk_refs[chunk]["pieces"]
            all_of(pieces.at[0:3], layer_recv.at[chunk]).wait_recv()
            for which in range(2):
                for index in range(half_owned):
                    first = (which * half_owned + index) * points
                    lanes = slice(first, first + points)
                    if chunk == 0:
                        value = pieces[which, index].astype(jnp.float32)
                        value = (value + pieces[2 + which, index].astype(jnp.float32)).astype(jnp.bfloat16)
                        left[0:size, lanes] = value[0:size]
                        left[2 * size : 3 * size, lanes] = value[size:]
                        continue
                    for far in range(2):
                        value = pieces[2 * far + which, index]
                        for place, (part, _, _) in enumerate(chunks[chunk]["parts"]):
                            target = (2 * far + part) * size
                            left[target : target + size, lanes] = value[place * size : (place + 1) * size]

    def multiply(unit):
        number, begins, ends = units[unit]
        low, high, _ = groups[number]
        for start in range(begins, ends, 256):
            stop = min(start + 256, ends)
            total[4 * low : 4 * high, start:stop] = lax.dot_general(
                left[0 : 4 * (high - low), :],
                fit[start:stop, :],
                (((1,), (1,)), ((), ())),
                preferred_element_type=jnp.float32,
            )

    def total_of(unit, owner):
        number, begins, ends = units[unit]
        low, high, _ = groups[number]
        size = high - low
        return total[pl.ds(pl.multiple_of(4 * low + owner * size, size), size), begins:ends]

    def fill(unit):
        product = unit_refs[unit]["product"]
        _, begins, ends = units[unit]
        _, size, padded = product.shape
        if ends - begins < padded:
            product[:, :, padded - 128 :] = jnp.zeros((3, size, 128), jnp.bfloat16)

        def put(place):
            product[place, :, 0 : ends - begins] = total_of(unit, order[place]).astype(jnp.bfloat16)

        for place in range(2):
            pl.when(is_end)(functools.partial(put, place))
        put(2)

    def send_far(unit, place):
        @pl.when(is_end)
        def _():
            end_copy(unit, 2 + place, place, mate).start()

    def send_mate(unit):
        end_copy(unit, 0, 2, mate).start()

    def pass_on(unit, place):
        product, landed = unit_refs[unit]["product"], unit_refs[unit]["landed"]
        _, begins, ends = units[unit]
        lanes = slice(0, ends - begins)
        slot = 3 - place

        @pl.when(is_middle)
        def _():
            end_copy(unit, slot, place, mate).wait_recv()
            product[place, :, lanes] = (
                total_of(unit, order[place]) + landed[slot, :, lanes].astype(jnp.float32)
            ).astype(jnp.bfloat16)
            end_copy(unit, 1, place, order[place]).start()

    def finish(unit):
        landed = unit_refs[unit]["landed"]
        number, begins, ends = units[unit]
        low, high, _ = groups[number]
        all_of(landed.at[0:2], end_recv.at[unit, 0]).wait_recv()
        value = total_of(unit, row)
        for slot in range(2):
            value = value + landed[slot, :, 0 : ends - begins].astype(jnp.float32)
        result[low:high, begins:ends] = value.astype(result.dtype)

    for copy in small_copies:
        copy.wait()
    index_table(
        owner_ref[...], local_ref[...], block_ref[...], weight_ref[...], owned, weights, slices, meta
    )
    index_copy = pltpu.make_async_copy(meta, own_index, meta_sem.at[2])
    index_copy.start()
    other_copy.wait()
    turn(other_raw, [(chunk, chunk_refs[chunk]["swap_out"], 0) for chunk in swapped], 1 - side)
    pl.semaphore_wait(barrier, 4 + 2 * lax.rem((row + 1) // 2, 2))
    meta_copy = remote(meta, got_index, meta_sem.at[0], meta_sem.at[1], "layer", partner)
    meta_copy.start()
    swaps = {
        chunk: remote(
            chunk_refs[chunk]["swap_out"],
            chunk_refs[chunk]["swap_in"],
            swap_sem.at[0, chunk - 1],
            swap_sem.at[1, chunk - 1],
            "layer",
            partner,
        )
        for chunk in swapped
    }
    for copy in swaps.values():
        copy.start()
    own_copy.wait()
    turn(own_raw, [(chunk, own_turned, chunks[chunk]["base"]) for chunk in swapped], side)
    wide_table[...] = jnp.zeros_like(wide_table)
    table_copy.wait()
    for index in range(weights):
        wide_table[index, 0:block_rows, :] = turned_ref[index]
        wide_table[weights + index, block_rows:, :] = turned_ref[index]
    own_sums[0] = jnp.zeros(own_sums.shape[1:], own_sums.dtype)
    got_sums[0] = jnp.zeros(got_sums.shape[1:], got_sums.dtype)
    index_copy.wait()
    early_rows = chunks[0]["columns"]
    sum_terms(own_index, own_turned, own_sums, 0, early_rows)
    share(0)
    spread(0)
    sum_terms(own_index, own_turned, own_sums, early_rows, own_turned.shape[1])
    meta_copy.wait_recv()
    begin(1)
    share(1)
    join(0, 1)
    spread(1)
    join(0, 0)
    fit_copy.start()
    begin(2)
    share(2)
    spread(2)
    join(1, 1)
    join(1, 0)
    begin(3)
    share(3)
    settle(0)
    spread(3)
    join(2, 1)
    begin(4)
    share(4)
    join(2, 0)
    settle(1)
    spread(4)
    join(3, 1)
    settle(2)
    join(3, 0)
    join(4, 1)
    join(4, 0)
    fit_copy.wait()
    settle(3, is_middle)
    gather(0)
    multiply(0)
    fill(0)
    send_far(0, 0)
    send_far(0, 1)
    send_mate(0)
    settle(3, is_end)
    settle(4, is_middle)
    gather(1)
    multiply(1)
    fill(1)
    send_far(1, 0)
    send_far(1, 1)
    send_mate(1)
    settle(4, is_end)
    pass_on(0, 1)
    pass_on(0, 0)
    gather(2)
    multiply(2)
    fill(2)
    send_far(2, 0)
    pass_on(1, 1)
    pass_on(1, 0)
    gather(3)
    multiply(3)
    fill(3)
    send_far(3, 0)
    send_far(2, 1)
    pass_on(2, 1)
    multiply(4)
    fill(4)
    send_far(4, 0)
    send_far(3, 1)
    send_far(4, 1)
    send_mate(2)
    send_mate(3)
    send_mate(4)
    pass_on(3, 1)
    finish(0)
    pass_on(2, 0)
    pass_on(4, 1)
    finish(1)
    pass_on(3, 0)
    pass_on(4, 0)
    finish(2)
    finish(3)
    finish(4)

    meta_copy.wait_send()
    for copy in swaps.values():
        copy.wait_send()
    for chunk, refs in enumerate(chunk_refs):
        core_copy(chunk).wait_send()
        all_of(refs["row_out"], row_send.at[chunk]).wait_send()
        all_of(refs["pieces"].at[0:3], layer_send.at[chunk]).wait_send()
    for unit, refs in enumerate(unit_refs):
        all_of(refs["product"], end_send.at[unit]).wait_send()


def plan_of(out_rows, width):
    cut = out_rows // 4
    marks = [cut * index for index in range(5)]
    spans = list(zip(marks[:-1], marks[1:]))
    low, high = spans[0]
    parts = [[(0, low, high)], [(1, low, high)]]
    parts += [[(0, start, stop), (1, start, stop)] for start, stop in spans[1:]]
    chunks, base = [], 0
    for number, part in enumerate(parts):
        columns = sum(stop - start for _, start, stop in part)
        if number == 0:
            columns = 2 * columns
        chunks.append({"parts": part, "columns": columns, "base": base})
        base += columns
    groups = [(low, high, (0, 1))]
    groups += [(start, stop, (number + 2,)) for number, (start, stop) in enumerate(spans[1:])]
    middle = width // 512 * 256
    units = [(number, 0, width) for number in range(len(groups) - 1)]
    units += [(len(groups) - 1, 0, middle), (len(groups) - 1, middle, width)]
    return chunks, groups, units, base


def local_fused(layers, table, fitting, owner, local_slice, block_index, weight_index):
    rows_dev, columns = layers.shape[1:]
    weights, points, block_rows = table.shape
    entries = owner.shape[1]
    peers = lax.axis_size("row")
    depth, width = fitting.shape
    owned = depth // points
    half = columns // 2
    out_rows = columns // peers
    pairs = rows_dev // points
    chunks, groups, units, held = plan_of(out_rows, width)
    bf16, f32 = jnp.bfloat16, jnp.float32
    dma = pltpu.SemaphoreType.DMA

    def chunk_scratch(number):
        cols = chunks[number]["columns"]
        slots = owned // 2
        refs = {
            "core_out": pltpu.VMEM((4, slots, cols, points), bf16),
            "core_in": pltpu.VMEM((4, slots, cols, points), bf16),
            "row_out": pltpu.VMEM((3, slots, cols, points), bf16),
            "row_in": pltpu.VMEM((4, slots, cols, points), bf16),
            "pieces": pltpu.VMEM((4, slots, cols, points), bf16),
        }
        if number > 0:
            refs["swap_out"] = pltpu.VMEM((pairs, cols, points), bf16)
            refs["swap_in"] = pltpu.VMEM((pairs, cols, points), bf16)
        return refs

    def unit_scratch(unit):
        number, begins, ends = unit
        low, high, _ = groups[number]
        padded = -(-(ends - begins) // 128) * 128
        return {
            "product": pltpu.VMEM((3, high - low, padded), bf16),
            "landed": pltpu.VMEM((4, high - low, padded), bf16),
        }

    widest = max(chunk["columns"] for chunk in chunks[1:])
    tallest = max(4 * (high - low) for low, high, _ in groups)
    hbm = pl.BlockSpec(memory_space=pltpu.HBM)
    vmem = pl.BlockSpec(memory_space=pltpu.VMEM)
    return pl.pallas_call(
        functools.partial(fused_kernel, peers, owned, chunks, groups, units),
        out_shape=pltpu.VMEM((out_rows, width), bf16),
        in_specs=[hbm] * 7,
        out_specs=vmem,
        scratch_shapes=[
            pltpu.VMEM((rows_dev, half), bf16),
            pltpu.VMEM((rows_dev, half), bf16),
            pltpu.VMEM((weights, block_rows, points), bf16),
            pltpu.VMEM((1, entries), jnp.int32),
            pltpu.VMEM((1, entries), jnp.int32),
            pltpu.VMEM((1, entries), jnp.int32),
            pltpu.VMEM((1, entries), jnp.int32),
            pltpu.VMEM((pairs, held, points), bf16),
            pltpu.VMEM((2 * weights, points, points), bf16),
            pltpu.VMEM((entries + 1, held, points), f32),
            pltpu.VMEM((entries + 1, widest, points), f32),
            pltpu.VMEM((8, 128), jnp.int32),
            pltpu.SMEM((8, 128), jnp.int32),
            pltpu.SMEM((8, 128), jnp.int32),
            pltpu.VMEM((width, depth), bf16),
            pltpu.VMEM((tallest, depth), bf16),
            pltpu.VMEM((columns, width), f32),
            pltpu.VMEM((owned // 2, held, points), f32),
            [chunk_scratch(number) for number in range(len(chunks))],
            [unit_scratch(unit) for unit in units],
            dma((8,)),
            dma((3,)),
            dma((2, len(chunks) - 1)),
            dma((2, len(chunks))),
            dma((len(chunks),)),
            dma((len(chunks), 3)),
            dma((len(chunks),)),
            dma((len(chunks),)),
            dma((len(units),)),
            dma((len(units), 3)),
        ],
        compiler_params=pltpu.CompilerParams(
            collective_id=0, has_side_effects=True
        ),
    )(
        layers[0],
        table.transpose(0, 2, 1),
        owner[:, :, 0],
        local_slice,
        block_index,
        weight_index,
        fitting.T,
    )


def local(layers, table, fitting, owner, local_slice, block_index, weight_index):
    arguments = (layers, table, fitting, owner, local_slice, block_index, weight_index)
    entries, peers, group = owner.shape[1], lax.axis_size("row"), lax.axis_size("layer")
    _, points, block_rows = table.shape
    raw_rows = max(2, 2 * entries // peers) * block_rows
    reduced_rows = fitting.shape[0] // group
    slices = peers * fitting.shape[0] // points
    fits = points == 128 and block_rows == 64 and layers.shape[2] == 256
    fits = fits and entries <= 128 and slices <= 128
    if group == 4 and peers == 4 and raw_rows > reduced_rows and fits:
        return local_fused(*arguments)
    return local_rows(*arguments)


def solution(mesh):
    return jax.shard_map(
        local,
        mesh=mesh,
        in_specs=(
            P("layer", "row", "panel"),
            P(),
            P("row", "layer"),
            P("layer", "row", None),
            P("layer", "row"),
            P("layer", "row"),
            P("layer", "row"),
        ),
        out_specs=P(("panel", "row"), "layer"),
        check_vma=False,
    )
```

```python
import functools

import jax
import jax.numpy as jnp
from jax import lax
from jax.experimental import pallas as pl
from jax.experimental.pallas import tpu as pltpu

MESH = pl.DeviceIdType.MESH
from jax.sharding import PartitionSpec as P


def local_rows(layers, table, fitting, owner, local_slice, block_index, weight_index):
    rows_dev = layers.shape[1]
    columns = layers.shape[2]
    slice_rows = table.shape[1]
    block_rows = table.shape[2]
    entries = owner.shape[1]
    peer_count = lax.axis_size("row")
    capacity = max(2, 2 * entries // peer_count)
    slot_count = peer_count * capacity
    owned_slices = fitting.shape[0] // slice_rows
    owner_now = owner[0, :, 0]
    local_now = local_slice[0]
    owner_match = (owner_now[:, None] == jnp.arange(peer_count, dtype=jnp.int32)[None, :]).astype(
        jnp.int32
    )
    slot_rank = jnp.sum((jnp.cumsum(owner_match, axis=0) - 1) * owner_match, axis=1)
    target = owner_now * capacity + slot_rank
    placed = target[None, :] == jnp.arange(slot_count, dtype=jnp.int32)[:, None]
    filled = jnp.any(placed, axis=1)
    source = jnp.sum(jnp.where(placed, jnp.arange(entries, dtype=jnp.int32)[None, :], 0), axis=1)
    send_local = jnp.where(filled, local_now[source], -1).reshape(peer_count, capacity)
    grouped = layers[0].reshape(rows_dev // block_rows, block_rows, columns)
    picked = grouped[block_index[0][source]].reshape(peer_count, capacity, block_rows, columns)
    send_weight = weight_index[0][source].reshape(peer_count, capacity)
    got_rows, got_weight, got_local = (
        lax.all_to_all(picked, "row", split_axis=0, concat_axis=0, tiled=True),
        lax.all_to_all(send_weight, "row", split_axis=0, concat_axis=0, tiled=True),
        lax.all_to_all(send_local, "row", split_axis=0, concat_axis=0, tiled=True),
    )
    pupil_terms = jnp.einsum(
        "ksb,kbc->ksc",
        table[got_weight.reshape(-1)],
        got_rows.reshape(slot_count, block_rows, columns),
        preferred_element_type=jnp.float32,
    ).astype(jnp.bfloat16)
    selector = (
        jnp.arange(owned_slices, dtype=jnp.int32)[:, None] == got_local.reshape(-1)[None, :]
    ).astype(jnp.bfloat16)
    partial_pupil = jnp.dot(
        selector,
        pupil_terms.reshape(slot_count, slice_rows * columns),
        preferred_element_type=jnp.float32,
    ).reshape(owned_slices * slice_rows, columns)
    pupil_rounded = lax.psum(partial_pupil, "layer").astype(jnp.bfloat16)
    return lax.psum_scatter(
        lax.dot_general(
            pupil_rounded, fitting, (((0,), (0,)), ((), ())), preferred_element_type=jnp.float32
        ),
        "row",
        scatter_dimension=0,
        tiled=True,
    ).astype(jnp.bfloat16)


def index_table(owner, local_slice, block, weight, owned, weights, slices, out_ref):
    entries = owner.shape[1]
    square = (entries, entries)
    down = lax.broadcasted_iota(jnp.int32, square, 0)
    along = lax.broadcasted_iota(jnp.int32, square, 1)

    def upright(row):
        return jnp.sum(jnp.where(down == along, jnp.broadcast_to(row, square), 0), axis=1, keepdims=True)

    place = owner * owned + local_slice
    place_up = upright(place)
    place_row = jnp.broadcast_to(place, square)
    twin = (place_row == place_up) & (along < down)
    rank = jnp.sum(((place_row < place_up) | twin).astype(jnp.int32), axis=1, keepdims=True)
    follows = (jnp.sum(twin.astype(jnp.int32), axis=1, keepdims=True) > 0).astype(jnp.int32)
    code = upright(block * weights + weight)
    moved = rank == along
    code = jnp.sum(jnp.where(moved, jnp.broadcast_to(code, square), 0), axis=0, keepdims=True)
    follows = jnp.sum(jnp.where(moved, jnp.broadcast_to(follows, square), 0), axis=0, keepdims=True)
    names = lax.broadcasted_iota(jnp.int32, (entries, slices), 1)
    place_wide = jnp.broadcast_to(place_up, (entries, slices))
    until = jnp.sum((place_wide <= names).astype(jnp.int32), axis=0, keepdims=True)
    held = jnp.sum((place_wide == names).astype(jnp.int32), axis=0, keepdims=True)
    block = code // weights
    out_ref[0:1, 0:entries] = block // 2
    out_ref[1:2, 0:entries] = (block % 2) * weights + code % weights
    out_ref[2:3, 0:entries] = follows
    out_ref[3:4, 0:slices] = jnp.where(held > 0, until, 0)


def fused_kernel(
    peers, owned, chunks, groups, units,
    layers_hbm, table_hbm, owner_hbm, local_hbm, block_hbm, weight_hbm, fitting_hbm, result,
    other_raw, own_raw, turned_ref, owner_ref, local_ref, block_ref, weight_ref,
    own_turned, wide_table, own_sums, got_sums, meta, own_index, got_index,
    fit, left, total, own_part, chunk_refs, unit_refs,
    in_sem, meta_sem, swap_sem, core_sem, row_send, row_recv, layer_send, layer_recv, end_send, end_recv,
):
    row = lax.axis_index("row")
    me = lax.axis_index("layer")
    core = lax.rem(me, 2)
    side = me // 2
    half = other_raw.shape[1]
    width = fit.shape[0]
    weights, block_rows, points = turned_ref.shape
    pairs = own_turned.shape[0]
    entries = owner_ref.shape[1]
    half_owned = owned // 2
    slices = peers * owned
    step_entries = next(size for size in (32, 16, 8, 1) if entries % size == 0)
    owner_width = half // 2
    mate = row + 1 - 2 * lax.rem(row, 2)
    cross = lax.rem(row + 2, peers)
    opposite = peers - 1 - row
    is_end = jnp.logical_or(row == 0, row == peers - 1)
    is_middle = jnp.logical_not(is_end)
    layer_peers = [lax.rem(me + k, 4) for k in range(1, 4)]
    partner = layer_peers[1]
    sibling = me + 1 - 2 * core
    order = (opposite, cross, mate, row)
    swapped = range(1, len(chunks))
    late_chunks = (len(chunks) - 2, len(chunks) - 1)

    first_own = pl.multiple_of(side * half, half)
    first_other = pl.multiple_of((1 - side) * half, half)
    small_copies = [
        pltpu.make_async_copy(source, target, in_sem.at[4 + index])
        for index, (source, target) in enumerate(
            (
                (owner_hbm, owner_ref),
                (local_hbm, local_ref),
                (block_hbm, block_ref),
                (weight_hbm, weight_ref),
            )
        )
    ]
    other_copy = pltpu.make_async_copy(layers_hbm.at[:, pl.ds(first_other, half)], other_raw, in_sem.at[0])
    own_copy = pltpu.make_async_copy(layers_hbm.at[:, pl.ds(first_own, half)], own_raw, in_sem.at[1])
    table_copy = pltpu.make_async_copy(table_hbm, turned_ref, in_sem.at[2])
    fit_copy = pltpu.make_async_copy(fitting_hbm, fit, in_sem.at[3])
    for copy in small_copies:
        copy.start()
    other_copy.start()
    own_copy.start()
    table_copy.start()

    barrier = pltpu.get_barrier_semaphore()
    for peer in (mate, 2 - row // 2):
        pl.semaphore_signal(barrier, inc=1, device_id={"row": peer}, device_id_type=MESH)
    for peer in layer_peers:
        pl.semaphore_signal(barrier, inc=1, device_id={"layer": peer}, device_id_type=MESH)

    def remote(source, target, send, recv, axis, peer):
        return pltpu.make_async_remote_copy(
            src_ref=source,
            dst_ref=target,
            send_sem=send,
            recv_sem=recv,
            device_id={axis: peer},
            device_id_type=MESH,
        )

    def all_of(ref, sem):
        return remote(ref, ref, sem, sem, "layer", partner)

    def turn(raw, targets, early):
        low, high = chunks[0]["parts"][0][1:]
        early_rows = pl.ds(pl.multiple_of(early * (high - low), high - low), high - low)

        def body(pair, carry):
            turned = raw[pl.ds(pl.multiple_of(pair * points, points), points), :].T
            for chunk, target, base in targets:
                for part, start, stop in chunks[chunk]["parts"]:
                    first = part * owner_width + start
                    target[pair, base : base + stop - start, :] = turned[first : first + stop - start]
                    base += stop - start
            own_turned[pair, early_rows, :] = turned[low:high]
            return carry

        lax.fori_loop(0, pairs, body, 0, unroll=4)

    def sum_terms(index_ref, rows_ref, sums_ref, low, high):
        def body(step, carry):
            terms = []
            for offset in range(step_entries):
                entry = step * step_entries + offset
                terms.append(
                    jnp.dot(
                        rows_ref[index_ref[0, entry], low:high, :],
                        wide_table[index_ref[1, entry]],
                        preferred_element_type=jnp.float32,
                    )
                )
            running = sums_ref[step * step_entries, low:high, :]
            for offset in range(step_entries):
                entry = step * step_entries + offset
                running = terms[offset] + index_ref[2, entry].astype(jnp.float32) * running
                sums_ref[entry + 1, low:high, :] = running
            return carry

        lax.fori_loop(0, entries // step_entries, body, 0)

    def core_copy(chunk, place):
        refs = chunk_refs[chunk]
        source, target = refs["core_out"], refs["core_in"]
        if chunk == 0:
            source, target = source.at[place], target.at[place]
        index = place if chunk == 0 else chunk + 3
        return remote(source, target, core_sem.at[0, index], core_sem.at[1, index], "layer", sibling)

    def row_copy(chunk, slot, source, peer):
        refs = chunk_refs[chunk]
        sems = (row_send.at[chunk], row_recv.at[chunk, max(slot, 1) - 1])
        return remote(refs["row_out"].at[source], refs["row_in"].at[slot], *sems, "row", peer)

    def layer_copy(chunk, k):
        pieces = chunk_refs[chunk]["pieces"]
        sems = (layer_send.at[chunk], layer_recv.at[chunk])
        return remote(pieces.at[me], pieces.at[me], *sems, "layer", layer_peers[k])

    def end_copy(unit, slot, source, peer):
        refs = unit_refs[unit]
        sems = (end_send.at[unit], end_recv.at[unit, max(slot, 1) - 1])
        return remote(refs["product"].at[source], refs["landed"].at[slot], *sems, "row", peer)

    def rows_of(chunk):
        base = chunks[chunk]["base"]
        return slice(base, base + chunks[chunk]["columns"])

    def partial(chunk, owner, which, index):
        name = owner * owned + which * half_owned + index
        value = own_sums[own_index[3, name], rows_of(chunk), :]
        if chunk > 0:
            value = value + got_sums[got_index[3, name], 0 : chunks[chunk]["columns"], :]
        return value

    def begin(chunk):
        swaps[chunk].wait_recv()
        sum_terms(got_index, chunk_refs[chunk]["swap_in"], got_sums, 0, chunks[chunk]["columns"])

    def share(chunk):
        refs = chunk_refs[chunk]
        for place, owner in enumerate(order):

            def body(index, carry):
                refs["core_out"][place, index] = partial(chunk, owner, 1 - core, index).astype(jnp.bfloat16)
                return carry

            lax.fori_loop(0, half_owned, body, 0, unroll=4)
            if chunk == 0 or place == 3:
                core_copy(chunk, place).start()

    def spread(chunk):
        refs = chunk_refs[chunk]
        for place, owner in enumerate(order):
            if chunk == 0 or place == 0:
                core_copy(chunk, place).wait_recv()

            def body(index, carry):
                value = partial(chunk, owner, core, index) + refs["core_in"][place, index].astype(jnp.float32)
                if place < 3:
                    refs["row_out"][place, index] = value.astype(jnp.bfloat16)
                else:
                    own_part[index, rows_of(chunk), :] = value
                return carry

            lax.fori_loop(0, half_owned, body, 0, unroll=4)
            if place < 2:

                @pl.when(is_end)
                def _():
                    row_copy(chunk, 2 + place, place, mate).start()

            elif place == 2:

                @pl.when(is_middle if chunk in late_chunks else True)
                def _():
                    row_copy(chunk, 0, 2, mate).start()

        if chunk == late_chunks[-1]:

            @pl.when(is_end)
            def _():
                for late in late_chunks:
                    row_copy(late, 0, 2, mate).start()

    def join(chunk, place):
        refs = chunk_refs[chunk]
        slot = 3 - place

        @pl.when(is_middle)
        def _():
            row_copy(chunk, slot, place, mate).wait_recv()
            refs["row_out"][place] = (
                refs["row_out"][place].astype(jnp.float32) + refs["row_in"][slot].astype(jnp.float32)
            ).astype(jnp.bfloat16)
            row_copy(chunk, 1, place, order[place]).start()

    def settle(chunk, when=None):
        refs = chunk_refs[chunk]

        def run():
            all_of(refs["row_in"].at[0:2], row_recv.at[chunk, 0]).wait_recv()
            value = own_part[:, rows_of(chunk), :]
            for slot in range(2):
                value = value + refs["row_in"][slot].astype(jnp.float32)
            refs["pieces"][me] = value.astype(jnp.bfloat16)
            for k in (1, 0, 2):
                layer_copy(chunk, k).start()

        if when is None:
            run()
        else:
            pl.when(when)(run)

    def gather(number):
        low, high, members = groups[number]
        size = high - low
        for chunk in members:
            pieces = chunk_refs[chunk]["pieces"]
            all_of(pieces.at[0:3], layer_recv.at[chunk]).wait_recv()
            for which in range(2):
                for index in range(half_owned):
                    first = (which * half_owned + index) * points
                    lanes = slice(first, first + points)
                    if chunk == 0:
                        value = pieces[which, index].astype(jnp.float32)
                        value = (value + pieces[2 + which, index].astype(jnp.float32)).astype(jnp.bfloat16)
                        left[0:size, lanes] = value[0:size]
                        left[2 * size : 3 * size, lanes] = value[size:]
                        continue
                    for far in range(2):
                        value = pieces[2 * far + which, index]
                        for place, (part, _, _) in enumerate(chunks[chunk]["parts"]):
                            target = (2 * far + part) * size
                            left[target : target + size, lanes] = value[place * size : (place + 1) * size]

    def multiply(unit):
        number, begins, ends = units[unit]
        low, high, _ = groups[number]
        for start in range(begins, ends, 256):
            stop = min(start + 256, ends)
            total[4 * low : 4 * high, start:stop] = lax.dot_general(
                left[0 : 4 * (high - low), :],
                fit[start:stop, :],
                (((1,), (1,)), ((), ())),
                preferred_element_type=jnp.float32,
            )

    def total_of(unit, owner):
        number, begins, ends = units[unit]
        low, high, _ = groups[number]
        size = high - low
        return total[pl.ds(pl.multiple_of(4 * low + owner * size, size), size), begins:ends]

    def fill(unit):
        product = unit_refs[unit]["product"]
        _, begins, ends = units[unit]
        _, size, padded = product.shape
        if ends - begins < padded:
            product[:, :, padded - 128 :] = jnp.zeros((3, size, 128), jnp.bfloat16)

        def put(place):
            product[place, :, 0 : ends - begins] = total_of(unit, order[place]).astype(jnp.bfloat16)

        for place in range(2):
            pl.when(is_end)(functools.partial(put, place))
        put(2)

    def send_far(unit, place):
        @pl.when(is_end)
        def _():
            end_copy(unit, 2 + place, place, mate).start()

    def send_mate(unit, when=True):
        @pl.when(when)
        def _():
            end_copy(unit, 0, 2, mate).start()

    def pass_on(unit, place):
        product, landed = unit_refs[unit]["product"], unit_refs[unit]["landed"]
        _, begins, ends = units[unit]
        lanes = slice(0, ends - begins)
        slot = 3 - place

        @pl.when(is_middle)
        def _():
            end_copy(unit, slot, place, mate).wait_recv()
            product[place, :, lanes] = (
                total_of(unit, order[place]) + landed[slot, :, lanes].astype(jnp.float32)
            ).astype(jnp.bfloat16)
            end_copy(unit, 1, place, order[place]).start()

    def finish(unit):
        landed = unit_refs[unit]["landed"]
        number, begins, ends = units[unit]
        low, high, _ = groups[number]
        all_of(landed.at[0:2], end_recv.at[unit, 0]).wait_recv()
        value = total_of(unit, row)
        for slot in range(2):
            value = value + landed[slot, :, 0 : ends - begins].astype(jnp.float32)
        result[low:high, begins:ends] = value.astype(result.dtype)

    wide_table[...] = jnp.zeros_like(wide_table)
    own_sums[0] = jnp.zeros(own_sums.shape[1:], own_sums.dtype)
    got_sums[0] = jnp.zeros(got_sums.shape[1:], got_sums.dtype)
    for copy in small_copies:
        copy.wait()
    index_table(
        owner_ref[...], local_ref[...], block_ref[...], weight_ref[...], owned, weights, slices, meta
    )
    index_copy = pltpu.make_async_copy(meta, own_index, meta_sem.at[2])
    index_copy.start()
    other_copy.wait()
    turn(other_raw, [(chunk, chunk_refs[chunk]["swap_out"], 0) for chunk in swapped], 1 - side)
    pl.semaphore_wait(barrier, 4 + 2 * lax.rem((row + 1) // 2, 2))
    meta_copy = remote(meta, got_index, meta_sem.at[0], meta_sem.at[1], "layer", partner)
    meta_copy.start()
    swaps = {
        chunk: remote(
            chunk_refs[chunk]["swap_out"],
            chunk_refs[chunk]["swap_in"],
            swap_sem.at[0, chunk - 1],
            swap_sem.at[1, chunk - 1],
            "layer",
            partner,
        )
        for chunk in swapped
    }
    swaps[1].start()
    own_copy.wait()
    turn(own_raw, [(chunk, own_turned, chunks[chunk]["base"]) for chunk in swapped], side)
    table_copy.wait()
    for index in range(weights):
        wide_table[index, 0:block_rows, :] = turned_ref[index]
        wide_table[weights + index, block_rows:, :] = turned_ref[index]
    index_copy.wait()
    early_rows = chunks[0]["columns"]
    sum_terms(own_index, own_turned, own_sums, 0, early_rows)
    share(0)
    for chunk in swapped[1:]:
        swaps[chunk].start()
    spread(0)
    sum_terms(own_index, own_turned, own_sums, early_rows, own_turned.shape[1])
    meta_copy.wait_recv()
    begin(1)
    share(1)
    join(0, 1)
    spread(1)
    join(0, 0)
    fit_copy.start()
    begin(2)
    share(2)
    spread(2)
    join(1, 1)
    join(1, 0)
    begin(3)
    share(3)
    settle(0)
    spread(3)
    join(2, 1)
    begin(4)
    share(4)
    join(2, 0)
    settle(1)
    spread(4)
    join(3, 1)
    settle(2)
    join(3, 0)
    join(4, 1)
    join(4, 0)
    fit_copy.wait()
    settle(3, is_middle)
    gather(0)
    multiply(0)
    fill(0)
    send_far(0, 0)
    send_far(0, 1)
    send_mate(0)
    settle(3, is_end)
    settle(4, is_middle)
    gather(1)
    multiply(1)
    fill(1)
    send_far(1, 0)
    send_far(1, 1)
    send_mate(1)
    settle(4, is_end)
    pass_on(0, 1)
    pass_on(0, 0)
    gather(2)
    multiply(2)
    fill(2)
    send_mate(2, is_middle)
    send_far(2, 0)
    pass_on(1, 1)
    pass_on(1, 0)
    gather(3)
    multiply(3)
    fill(3)
    send_mate(3, is_middle)
    send_far(3, 0)
    pass_on(2, 1)
    multiply(4)
    fill(4)
    send_mate(4, is_middle)
    send_far(4, 0)
    send_far(2, 1)
    send_far(3, 1)
    send_far(4, 1)
    send_mate(2, is_end)
    send_mate(3, is_end)
    send_mate(4, is_end)
    pass_on(3, 1)
    pass_on(4, 1)
    finish(0)
    pass_on(2, 0)
    finish(1)
    pass_on(3, 0)
    pass_on(4, 0)
    finish(2)
    finish(3)
    finish(4)

    meta_copy.wait_send()
    for copy in swaps.values():
        copy.wait_send()
    for chunk, refs in enumerate(chunk_refs):
        for place in range(4 if chunk == 0 else 1):
            core_copy(chunk, place).wait_send()
        all_of(refs["row_out"], row_send.at[chunk]).wait_send()
        all_of(refs["pieces"].at[0:3], layer_send.at[chunk]).wait_send()
    for unit, refs in enumerate(unit_refs):
        all_of(refs["product"], end_send.at[unit]).wait_send()


def plan_of(out_rows, width):
    cut = out_rows // 4
    marks = [cut * index for index in range(5)]
    spans = list(zip(marks[:-1], marks[1:]))
    low, high = spans[0]
    parts = [[(0, low, high)], [(1, low, high)]]
    parts += [[(0, start, stop), (1, start, stop)] for start, stop in spans[1:]]
    chunks, base = [], 0
    for number, part in enumerate(parts):
        columns = sum(stop - start for _, start, stop in part)
        if number == 0:
            columns = 2 * columns
        chunks.append({"parts": part, "columns": columns, "base": base})
        base += columns
    groups = [(low, high, (0, 1))]
    groups += [(start, stop, (number + 2,)) for number, (start, stop) in enumerate(spans[1:])]
    middle = width // 512 * 256
    units = [(number, 0, width) for number in range(len(groups) - 1)]
    units += [(len(groups) - 1, 0, middle), (len(groups) - 1, middle, width)]
    return chunks, groups, units, base


def local_fused(layers, table, fitting, owner, local_slice, block_index, weight_index):
    rows_dev, columns = layers.shape[1:]
    weights, points, block_rows = table.shape
    entries = owner.shape[1]
    peers = lax.axis_size("row")
    depth, width = fitting.shape
    owned = depth // points
    half = columns // 2
    out_rows = columns // peers
    pairs = rows_dev // points
    chunks, groups, units, held = plan_of(out_rows, width)
    bf16, f32 = jnp.bfloat16, jnp.float32
    dma = pltpu.SemaphoreType.DMA

    def chunk_scratch(number):
        cols = chunks[number]["columns"]
        slots = owned // 2
        refs = {
            "core_out": pltpu.VMEM((4, slots, cols, points), bf16),
            "core_in": pltpu.VMEM((4, slots, cols, points), bf16),
            "row_out": pltpu.VMEM((3, slots, cols, points), bf16),
            "row_in": pltpu.VMEM((4, slots, cols, points), bf16),
            "pieces": pltpu.VMEM((4, slots, cols, points), bf16),
        }
        if number > 0:
            refs["swap_out"] = pltpu.VMEM((pairs, cols, points), bf16)
            refs["swap_in"] = pltpu.VMEM((pairs, cols, points), bf16)
        return refs

    def unit_scratch(unit):
        number, begins, ends = unit
        low, high, _ = groups[number]
        padded = -(-(ends - begins) // 128) * 128
        return {
            "product": pltpu.VMEM((3, high - low, padded), bf16),
            "landed": pltpu.VMEM((4, high - low, padded), bf16),
        }

    widest = max(chunk["columns"] for chunk in chunks[1:])
    tallest = max(4 * (high - low) for low, high, _ in groups)
    hbm = pl.BlockSpec(memory_space=pltpu.HBM)
    vmem = pl.BlockSpec(memory_space=pltpu.VMEM)
    return pl.pallas_call(
        functools.partial(fused_kernel, peers, owned, chunks, groups, units),
        out_shape=pltpu.VMEM((out_rows, width), bf16),
        in_specs=[hbm] * 7,
        out_specs=vmem,
        scratch_shapes=[
            pltpu.VMEM((rows_dev, half), bf16),
            pltpu.VMEM((rows_dev, half), bf16),
            pltpu.VMEM((weights, block_rows, points), bf16),
            pltpu.VMEM((1, entries), jnp.int32),
            pltpu.VMEM((1, entries), jnp.int32),
            pltpu.VMEM((1, entries), jnp.int32),
            pltpu.VMEM((1, entries), jnp.int32),
            pltpu.VMEM((pairs, held, points), bf16),
            pltpu.VMEM((2 * weights, points, points), bf16),
            pltpu.VMEM((entries + 1, held, points), f32),
            pltpu.VMEM((entries + 1, widest, points), f32),
            pltpu.VMEM((8, 128), jnp.int32),
            pltpu.SMEM((8, 128), jnp.int32),
            pltpu.SMEM((8, 128), jnp.int32),
            pltpu.VMEM((width, depth), bf16),
            pltpu.VMEM((tallest, depth), bf16),
            pltpu.VMEM((columns, width), f32),
            pltpu.VMEM((owned // 2, held, points), f32),
            [chunk_scratch(number) for number in range(len(chunks))],
            [unit_scratch(unit) for unit in units],
            dma((8,)),
            dma((3,)),
            dma((2, len(chunks) - 1)),
            dma((2, len(chunks) + 3)),
            dma((len(chunks),)),
            dma((len(chunks), 3)),
            dma((len(chunks),)),
            dma((len(chunks),)),
            dma((len(units),)),
            dma((len(units), 3)),
        ],
        compiler_params=pltpu.CompilerParams(
            collective_id=0, has_side_effects=True
        ),
    )(
        layers[0],
        table.transpose(0, 2, 1),
        owner[:, :, 0],
        local_slice,
        block_index,
        weight_index,
        fitting.T,
    )


def local(layers, table, fitting, owner, local_slice, block_index, weight_index):
    arguments = (layers, table, fitting, owner, local_slice, block_index, weight_index)
    entries, peers, group = owner.shape[1], lax.axis_size("row"), lax.axis_size("layer")
    _, points, block_rows = table.shape
    raw_rows = max(2, 2 * entries // peers) * block_rows
    reduced_rows = fitting.shape[0] // group
    slices = peers * fitting.shape[0] // points
    fits = points == 128 and block_rows == 64 and layers.shape[2] == 256
    fits = fits and entries <= 128 and slices <= 128
    if group == 4 and peers == 4 and raw_rows > reduced_rows and fits:
        return local_fused(*arguments)
    return local_rows(*arguments)


def solution(mesh):
    return jax.shard_map(
        local,
        mesh=mesh,
        in_specs=(
            P("layer", "row", "panel"),
            P(),
            P("row", "layer"),
            P("layer", "row", None),
            P("layer", "row"),
            P("layer", "row"),
            P("layer", "row"),
        ),
        out_specs=P(("panel", "row"), "layer"),
        check_vma=False,
    )
```

```python
import functools

import jax
import jax.numpy as jnp
from jax import lax
from jax.experimental import pallas as pl
from jax.experimental.pallas import tpu as pltpu

MESH = pl.DeviceIdType.MESH
from jax.sharding import PartitionSpec as P


def local_rows(layers, table, fitting, owner, local_slice, block_index, weight_index):
    rows_dev = layers.shape[1]
    columns = layers.shape[2]
    slice_rows = table.shape[1]
    block_rows = table.shape[2]
    entries = owner.shape[1]
    peer_count = lax.axis_size("row")
    capacity = max(2, 2 * entries // peer_count)
    slot_count = peer_count * capacity
    owned_slices = fitting.shape[0] // slice_rows
    owner_now = owner[0, :, 0]
    local_now = local_slice[0]
    owner_match = (owner_now[:, None] == jnp.arange(peer_count, dtype=jnp.int32)[None, :]).astype(
        jnp.int32
    )
    slot_rank = jnp.sum((jnp.cumsum(owner_match, axis=0) - 1) * owner_match, axis=1)
    target = owner_now * capacity + slot_rank
    placed = target[None, :] == jnp.arange(slot_count, dtype=jnp.int32)[:, None]
    filled = jnp.any(placed, axis=1)
    source = jnp.sum(jnp.where(placed, jnp.arange(entries, dtype=jnp.int32)[None, :], 0), axis=1)
    send_local = jnp.where(filled, local_now[source], -1).reshape(peer_count, capacity)
    grouped = layers[0].reshape(rows_dev // block_rows, block_rows, columns)
    picked = grouped[block_index[0][source]].reshape(peer_count, capacity, block_rows, columns)
    send_weight = weight_index[0][source].reshape(peer_count, capacity)
    got_rows, got_weight, got_local = (
        lax.all_to_all(picked, "row", split_axis=0, concat_axis=0, tiled=True),
        lax.all_to_all(send_weight, "row", split_axis=0, concat_axis=0, tiled=True),
        lax.all_to_all(send_local, "row", split_axis=0, concat_axis=0, tiled=True),
    )
    pupil_terms = jnp.einsum(
        "ksb,kbc->ksc",
        table[got_weight.reshape(-1)],
        got_rows.reshape(slot_count, block_rows, columns),
        preferred_element_type=jnp.float32,
    ).astype(jnp.bfloat16)
    selector = (
        jnp.arange(owned_slices, dtype=jnp.int32)[:, None] == got_local.reshape(-1)[None, :]
    ).astype(jnp.bfloat16)
    partial_pupil = jnp.dot(
        selector,
        pupil_terms.reshape(slot_count, slice_rows * columns),
        preferred_element_type=jnp.float32,
    ).reshape(owned_slices * slice_rows, columns)
    pupil_rounded = lax.psum(partial_pupil, "layer").astype(jnp.bfloat16)
    return lax.psum_scatter(
        lax.dot_general(
            pupil_rounded, fitting, (((0,), (0,)), ((), ())), preferred_element_type=jnp.float32
        ),
        "row",
        scatter_dimension=0,
        tiled=True,
    ).astype(jnp.bfloat16)


def index_table(owner, local_slice, block, weight, owned, weights, slices, out_ref):
    entries = owner.shape[1]
    square = (entries, entries)
    down = lax.broadcasted_iota(jnp.int32, square, 0)
    along = lax.broadcasted_iota(jnp.int32, square, 1)

    def upright(row):
        return jnp.sum(jnp.where(down == along, jnp.broadcast_to(row, square), 0), axis=1, keepdims=True)

    place = owner * owned + local_slice
    place_up = upright(place)
    place_row = jnp.broadcast_to(place, square)
    twin = (place_row == place_up) & (along < down)
    rank = jnp.sum(((place_row < place_up) | twin).astype(jnp.int32), axis=1, keepdims=True)
    follows = (jnp.sum(twin.astype(jnp.int32), axis=1, keepdims=True) > 0).astype(jnp.int32)
    code = upright(block * weights + weight)
    moved = rank == along
    code = jnp.sum(jnp.where(moved, jnp.broadcast_to(code, square), 0), axis=0, keepdims=True)
    follows = jnp.sum(jnp.where(moved, jnp.broadcast_to(follows, square), 0), axis=0, keepdims=True)
    names = lax.broadcasted_iota(jnp.int32, (entries, slices), 1)
    place_wide = jnp.broadcast_to(place_up, (entries, slices))
    until = jnp.sum((place_wide <= names).astype(jnp.int32), axis=0, keepdims=True)
    held = jnp.sum((place_wide == names).astype(jnp.int32), axis=0, keepdims=True)
    block = code // weights
    out_ref[0:1, 0:entries] = block // 2
    out_ref[1:2, 0:entries] = (block % 2) * weights + code % weights
    out_ref[2:3, 0:entries] = follows
    out_ref[3:4, 0:slices] = jnp.where(held > 0, until, 0)


def fused_kernel(
    peers, owned, chunks, groups, units, split_chunks,
    layers_hbm, table_hbm, owner_hbm, local_hbm, block_hbm, weight_hbm, fitting_hbm, result,
    other_raw, own_raw, turned_ref, owner_ref, local_ref, block_ref, weight_ref,
    own_turned, wide_table, own_sums, got_sums, meta, own_index, got_index,
    fit, left, total, own_part, chunk_refs, unit_refs,
    in_sem, meta_sem, swap_sem, core_sem, row_send, row_recv, layer_send, layer_recv, end_send, end_recv,
):
    row = lax.axis_index("row")
    me = lax.axis_index("layer")
    core = lax.rem(me, 2)
    side = me // 2
    half = other_raw.shape[1]
    width = fit.shape[0]
    weights, block_rows, points = turned_ref.shape
    pairs = own_turned.shape[0]
    entries = owner_ref.shape[1]
    half_owned = owned // 2
    slices = peers * owned
    step_entries = next(size for size in (32, 16, 8, 1) if entries % size == 0)
    owner_width = half // 2
    mate = row + 1 - 2 * lax.rem(row, 2)
    cross = lax.rem(row + 2, peers)
    opposite = peers - 1 - row
    is_end = jnp.logical_or(row == 0, row == peers - 1)
    is_middle = jnp.logical_not(is_end)
    layer_peers = [lax.rem(me + k, 4) for k in range(1, 4)]
    partner = layer_peers[1]
    sibling = me + 1 - 2 * core
    order = (opposite, cross, mate, row)
    swapped = range(1, len(chunks))
    late_chunks = (len(chunks) - 2, len(chunks) - 1)

    first_own = pl.multiple_of(side * half, half)
    first_other = pl.multiple_of((1 - side) * half, half)
    small_copies = [
        pltpu.make_async_copy(source, target, in_sem.at[4 + index])
        for index, (source, target) in enumerate(
            (
                (owner_hbm, owner_ref),
                (local_hbm, local_ref),
                (block_hbm, block_ref),
                (weight_hbm, weight_ref),
            )
        )
    ]
    split_rows = other_raw.shape[0] // 2
    other_copies = [
        pltpu.make_async_copy(
            layers_hbm.at[part * split_rows : (part + 1) * split_rows, pl.ds(first_other, half)],
            other_raw.at[part * split_rows : (part + 1) * split_rows, :],
            in_sem.at[8 * part],
        )
        for part in range(2)
    ]
    own_copy = pltpu.make_async_copy(layers_hbm.at[:, pl.ds(first_own, half)], own_raw, in_sem.at[1])
    table_copy = pltpu.make_async_copy(table_hbm, turned_ref, in_sem.at[2])
    fit_copy = pltpu.make_async_copy(fitting_hbm, fit, in_sem.at[3])
    for copy in small_copies:
        copy.start()
    for copy in other_copies:
        copy.start()
    own_copy.start()
    table_copy.start()

    barrier = pltpu.get_barrier_semaphore()
    for peer in (mate, 2 - row // 2):
        pl.semaphore_signal(barrier, inc=1, device_id={"row": peer}, device_id_type=MESH)
    for peer in layer_peers:
        pl.semaphore_signal(barrier, inc=1, device_id={"layer": peer}, device_id_type=MESH)

    def remote(source, target, send, recv, axis, peer):
        return pltpu.make_async_remote_copy(
            src_ref=source,
            dst_ref=target,
            send_sem=send,
            recv_sem=recv,
            device_id={axis: peer},
            device_id_type=MESH,
        )

    def all_of(ref, sem):
        return remote(ref, ref, sem, sem, "layer", partner)

    def turn(raw, targets, which, start_pair, stop_pair):
        low, high = chunks[0]["parts"][0][1:]
        early_rows = pl.ds(pl.multiple_of(which * (high - low), high - low), high - low)

        def body(pair, carry):
            turned = raw[pl.ds(pl.multiple_of(pair * points, points), points), :].T
            for chunk, target, base in targets:
                for part, start, stop in chunks[chunk]["parts"]:
                    first = part * owner_width + start
                    target[pair, base : base + stop - start, :] = turned[first : first + stop - start]
                    base += stop - start
            own_turned[pair, early_rows, :] = turned[low:high]
            return carry

        lax.fori_loop(start_pair, stop_pair, body, 0, unroll=4)

    def sum_terms(index_ref, rows_ref, sums_ref, low, high):
        def body(step, carry):
            terms = []
            for offset in range(step_entries):
                entry = step * step_entries + offset
                terms.append(
                    jnp.dot(
                        rows_ref[index_ref[0, entry], low:high, :],
                        wide_table[index_ref[1, entry]],
                        preferred_element_type=jnp.float32,
                    )
                )
            running = sums_ref[step * step_entries, low:high, :]
            for offset in range(step_entries):
                entry = step * step_entries + offset
                running = terms[offset] + index_ref[2, entry].astype(jnp.float32) * running
                sums_ref[entry + 1, low:high, :] = running
            return carry

        lax.fori_loop(0, entries // step_entries, body, 0)

    def core_copy(chunk, place):
        refs = chunk_refs[chunk]
        source, target = refs["core_out"], refs["core_in"]
        if chunk < split_chunks:
            source, target = source.at[place], target.at[place]
        index = 4 * chunk + place if chunk < split_chunks else chunk + 3 * split_chunks
        return remote(source, target, core_sem.at[0, index], core_sem.at[1, index], "layer", sibling)

    def row_copy(chunk, slot, source, peer):
        refs = chunk_refs[chunk]
        sems = (row_send.at[chunk], row_recv.at[chunk, max(slot, 1) - 1])
        return remote(refs["row_out"].at[source], refs["row_in"].at[slot], *sems, "row", peer)

    def layer_copy(chunk, k):
        pieces = chunk_refs[chunk]["pieces"]
        sems = (layer_send.at[chunk], layer_recv.at[chunk])
        return remote(pieces.at[me], pieces.at[me], *sems, "layer", layer_peers[k])

    def end_copy(unit, slot, source, peer):
        refs = unit_refs[unit]
        sems = (end_send.at[unit], end_recv.at[unit, max(slot, 1) - 1])
        return remote(refs["product"].at[source], refs["landed"].at[slot], *sems, "row", peer)

    def rows_of(chunk):
        base = chunks[chunk]["base"]
        return slice(base, base + chunks[chunk]["columns"])

    def partial(chunk, owner, which, index):
        name = owner * owned + which * half_owned + index
        value = own_sums[own_index[3, name], rows_of(chunk), :]
        if chunk > 0:
            value = value + got_sums[got_index[3, name], 0 : chunks[chunk]["columns"], :]
        return value

    def begin(chunk):
        swaps[chunk].wait_recv()
        sum_terms(got_index, chunk_refs[chunk]["swap_in"], got_sums, 0, chunks[chunk]["columns"])

    def share(chunk):
        refs = chunk_refs[chunk]
        for place, owner in enumerate(order):

            def body(index, carry):
                refs["core_out"][place, index] = partial(chunk, owner, 1 - core, index).astype(jnp.bfloat16)
                return carry

            lax.fori_loop(0, half_owned, body, 0, unroll=4)
            if chunk < split_chunks or place == 3:
                core_copy(chunk, place if chunk < split_chunks else 0).start()

    def spread(chunk):
        refs = chunk_refs[chunk]
        for place, owner in enumerate(order):
            if chunk < split_chunks or place == 0:
                core_copy(chunk, place).wait_recv()

            def body(index, carry):
                value = partial(chunk, owner, core, index) + refs["core_in"][place, index].astype(jnp.float32)
                if place < 3:
                    refs["row_out"][place, index] = value.astype(jnp.bfloat16)
                else:
                    own_part[index, rows_of(chunk), :] = value
                return carry

            lax.fori_loop(0, half_owned, body, 0, unroll=4)
            if place < 2:

                @pl.when(is_end)
                def _():
                    row_copy(chunk, 2 + place, place, mate).start()

            elif place == 2:

                @pl.when(is_middle if chunk in late_chunks else True)
                def _():
                    row_copy(chunk, 0, 2, mate).start()

        if chunk == late_chunks[-1]:

            @pl.when(is_end)
            def _():
                for late in late_chunks:
                    row_copy(late, 0, 2, mate).start()

    def join(chunk, place):
        refs = chunk_refs[chunk]
        slot = 3 - place

        @pl.when(is_middle)
        def _():
            row_copy(chunk, slot, place, mate).wait_recv()
            refs["row_out"][place] = (
                refs["row_out"][place].astype(jnp.float32) + refs["row_in"][slot].astype(jnp.float32)
            ).astype(jnp.bfloat16)
            row_copy(chunk, 1, place, order[place]).start()

    def settle(chunk, when=None):
        refs = chunk_refs[chunk]

        def run():
            all_of(refs["row_in"].at[0:2], row_recv.at[chunk, 0]).wait_recv()
            value = own_part[:, rows_of(chunk), :]
            for slot in range(2):
                value = value + refs["row_in"][slot].astype(jnp.float32)
            refs["pieces"][me] = value.astype(jnp.bfloat16)
            for k in (1, 0, 2):
                layer_copy(chunk, k).start()

        if when is None:
            run()
        else:
            pl.when(when)(run)

    def gather(number):
        low, high, members = groups[number]
        size = high - low
        for chunk in members:
            pieces = chunk_refs[chunk]["pieces"]
            all_of(pieces.at[0:3], layer_recv.at[chunk]).wait_recv()
            for which in range(2):
                for index in range(half_owned):
                    first = (which * half_owned + index) * points
                    lanes = slice(first, first + points)
                    if chunk == 0:
                        value = pieces[which, index].astype(jnp.float32)
                        value = (value + pieces[2 + which, index].astype(jnp.float32)).astype(jnp.bfloat16)
                        left[0:size, lanes] = value[0:size]
                        left[2 * size : 3 * size, lanes] = value[size:]
                        continue
                    for far in range(2):
                        value = pieces[2 * far + which, index]
                        for place, (part, _, _) in enumerate(chunks[chunk]["parts"]):
                            target = (2 * far + part) * size
                            left[target : target + size, lanes] = value[place * size : (place + 1) * size]

    def multiply(unit):
        number, begins, ends = units[unit]
        low, high, _ = groups[number]
        for start in range(begins, ends, 256):
            stop = min(start + 256, ends)
            total[4 * low : 4 * high, start:stop] = lax.dot_general(
                left[0 : 4 * (high - low), :],
                fit[start:stop, :],
                (((1,), (1,)), ((), ())),
                preferred_element_type=jnp.float32,
            )

    def total_of(unit, owner):
        number, begins, ends = units[unit]
        low, high, _ = groups[number]
        size = high - low
        return total[pl.ds(pl.multiple_of(4 * low + owner * size, size), size), begins:ends]

    def fill(unit):
        product = unit_refs[unit]["product"]
        _, begins, ends = units[unit]
        _, size, padded = product.shape
        if ends - begins < padded:
            product[:, :, padded - 128 :] = jnp.zeros((3, size, 128), jnp.bfloat16)

        def put(place):
            product[place, :, 0 : ends - begins] = total_of(unit, order[place]).astype(jnp.bfloat16)

        for place in range(2):
            pl.when(is_end)(functools.partial(put, place))
        put(2)

    def send_far(unit, place):
        @pl.when(is_end)
        def _():
            end_copy(unit, 2 + place, place, mate).start()

    def send_mate(unit, when=True):
        @pl.when(when)
        def _():
            end_copy(unit, 0, 2, mate).start()

    def pass_on(unit, place):
        product, landed = unit_refs[unit]["product"], unit_refs[unit]["landed"]
        _, begins, ends = units[unit]
        lanes = slice(0, ends - begins)
        slot = 3 - place

        @pl.when(is_middle)
        def _():
            end_copy(unit, slot, place, mate).wait_recv()
            product[place, :, lanes] = (
                total_of(unit, order[place]) + landed[slot, :, lanes].astype(jnp.float32)
            ).astype(jnp.bfloat16)
            end_copy(unit, 1, place, order[place]).start()

    def finish(unit):
        landed = unit_refs[unit]["landed"]
        number, begins, ends = units[unit]
        low, high, _ = groups[number]
        all_of(landed.at[0:2], end_recv.at[unit, 0]).wait_recv()
        value = total_of(unit, row)
        for slot in range(2):
            value = value + landed[slot, :, 0 : ends - begins].astype(jnp.float32)
        result[low:high, begins:ends] = value.astype(result.dtype)

    wide_table[...] = jnp.zeros_like(wide_table)
    own_sums[0] = jnp.zeros(own_sums.shape[1:], own_sums.dtype)
    got_sums[0] = jnp.zeros(got_sums.shape[1:], got_sums.dtype)
    for copy in small_copies:
        copy.wait()
    index_table(
        owner_ref[...], local_ref[...], block_ref[...], weight_ref[...], owned, weights, slices, meta
    )
    index_copy = pltpu.make_async_copy(meta, own_index, meta_sem.at[2])
    index_copy.start()
    swap_targets = [(chunk, chunk_refs[chunk]["swap_out"], 0) for chunk in swapped]
    for part, copy in enumerate(other_copies):
        copy.wait()
        turn(other_raw, swap_targets, 1 - side, part * pairs // 2, (part + 1) * pairs // 2)
    pl.semaphore_wait(barrier, 4 + 2 * lax.rem((row + 1) // 2, 2))
    meta_copy = remote(meta, got_index, meta_sem.at[0], meta_sem.at[1], "layer", partner)
    meta_copy.start()
    swaps = {
        chunk: remote(
            chunk_refs[chunk]["swap_out"],
            chunk_refs[chunk]["swap_in"],
            swap_sem.at[0, chunk - 1],
            swap_sem.at[1, chunk - 1],
            "layer",
            partner,
        )
        for chunk in swapped
    }
    swaps[1].start()
    own_copy.wait()
    turn(own_raw, [(chunk, own_turned, chunks[chunk]["base"]) for chunk in swapped], side, 0, pairs)
    table_copy.wait()
    for index in range(weights):
        wide_table[index, 0:block_rows, :] = turned_ref[index]
        wide_table[weights + index, block_rows:, :] = turned_ref[index]
    index_copy.wait()
    early_rows = chunks[0]["columns"]
    sum_terms(own_index, own_turned, own_sums, 0, early_rows)
    share(0)
    swaps[2].start()
    spread(0)
    sum_terms(own_index, own_turned, own_sums, early_rows, own_turned.shape[1])
    meta_copy.wait_recv()
    begin(1)
    swaps[3].start()
    share(1)
    join(0, 1)
    spread(1)
    join(0, 0)
    fit_copy.start()
    begin(2)
    swaps[4].start()
    share(2)
    spread(2)
    join(1, 1)
    join(1, 0)
    begin(3)
    share(3)
    settle(0)
    spread(3)
    join(2, 1)
    begin(4)
    share(4)
    join(2, 0)
    settle(1)
    spread(4)
    join(3, 1)
    settle(2)
    join(3, 0)
    join(4, 1)
    join(4, 0)
    fit_copy.wait()
    settle(3, is_middle)
    gather(0)
    multiply(0)
    fill(0)
    send_far(0, 0)
    send_far(0, 1)
    send_mate(0)
    settle(3, is_end)
    settle(4, is_middle)
    gather(1)
    multiply(1)
    fill(1)
    send_far(1, 0)
    send_far(1, 1)
    send_mate(1)
    settle(4, is_end)
    pass_on(0, 1)
    pass_on(0, 0)
    gather(2)
    multiply(2)
    fill(2)
    send_mate(2, is_middle)
    send_far(2, 0)
    pass_on(1, 1)
    pass_on(1, 0)
    gather(3)
    multiply(3)
    fill(3)
    send_mate(3, is_middle)
    send_far(3, 0)
    pass_on(2, 1)
    multiply(4)
    fill(4)
    send_mate(4, is_middle)
    send_far(4, 0)
    send_far(2, 1)
    send_far(3, 1)
    send_far(4, 1)
    send_mate(2, is_end)
    send_mate(3, is_end)
    send_mate(4, is_end)
    pass_on(3, 1)
    pass_on(4, 1)
    finish(0)
    pass_on(2, 0)
    finish(1)
    pass_on(3, 0)
    pass_on(4, 0)
    finish(2)
    finish(3)
    finish(4)

    meta_copy.wait_send()
    for copy in swaps.values():
        copy.wait_send()
    for chunk, refs in enumerate(chunk_refs):
        for place in range(4 if chunk < split_chunks else 1):
            core_copy(chunk, place).wait_send()
        all_of(refs["row_out"], row_send.at[chunk]).wait_send()
        all_of(refs["pieces"].at[0:3], layer_send.at[chunk]).wait_send()
    for unit, refs in enumerate(unit_refs):
        all_of(refs["product"], end_send.at[unit]).wait_send()


def plan_of(out_rows, width):
    cut = out_rows // 4
    marks = [cut * index for index in range(5)]
    spans = list(zip(marks[:-1], marks[1:]))
    low, high = spans[0]
    parts = [[(0, low, high)], [(1, low, high)]]
    parts += [[(0, start, stop), (1, start, stop)] for start, stop in spans[1:]]
    chunks, base = [], 0
    for number, part in enumerate(parts):
        columns = sum(stop - start for _, start, stop in part)
        if number == 0:
            columns = 2 * columns
        chunks.append({"parts": part, "columns": columns, "base": base})
        base += columns
    groups = [(low, high, (0, 1))]
    groups += [(start, stop, (number + 2,)) for number, (start, stop) in enumerate(spans[1:])]
    middle = width * 3 // 1024 * 256
    units = [(number, 0, width) for number in range(len(groups) - 1)]
    units += [(len(groups) - 1, 0, middle), (len(groups) - 1, middle, width)]
    return chunks, groups, units, base


def local_fused(layers, table, fitting, owner, local_slice, block_index, weight_index):
    rows_dev, columns = layers.shape[1:]
    weights, points, block_rows = table.shape
    entries = owner.shape[1]
    peers = lax.axis_size("row")
    depth, width = fitting.shape
    owned = depth // points
    half = columns // 2
    out_rows = columns // peers
    pairs = rows_dev // points
    chunks, groups, units, held = plan_of(out_rows, width)
    split_chunks = 1
    bf16, f32 = jnp.bfloat16, jnp.float32
    dma = pltpu.SemaphoreType.DMA

    def chunk_scratch(number):
        cols = chunks[number]["columns"]
        slots = owned // 2
        refs = {
            "core_out": pltpu.VMEM((4, slots, cols, points), bf16),
            "core_in": pltpu.VMEM((4, slots, cols, points), bf16),
            "row_out": pltpu.VMEM((3, slots, cols, points), bf16),
            "row_in": pltpu.VMEM((4, slots, cols, points), bf16),
            "pieces": pltpu.VMEM((4, slots, cols, points), bf16),
        }
        if number > 0:
            refs["swap_out"] = pltpu.VMEM((pairs, cols, points), bf16)
            refs["swap_in"] = pltpu.VMEM((pairs, cols, points), bf16)
        return refs

    def unit_scratch(unit):
        number, begins, ends = unit
        low, high, _ = groups[number]
        padded = -(-(ends - begins) // 128) * 128
        return {
            "product": pltpu.VMEM((3, high - low, padded), bf16),
            "landed": pltpu.VMEM((4, high - low, padded), bf16),
        }

    widest = max(chunk["columns"] for chunk in chunks[1:])
    tallest = max(4 * (high - low) for low, high, _ in groups)
    hbm = pl.BlockSpec(memory_space=pltpu.HBM)
    vmem = pl.BlockSpec(memory_space=pltpu.VMEM)
    return pl.pallas_call(
        functools.partial(fused_kernel, peers, owned, chunks, groups, units, split_chunks),
        out_shape=pltpu.VMEM((out_rows, width), bf16),
        in_specs=[hbm] * 7,
        out_specs=vmem,
        scratch_shapes=[
            pltpu.VMEM((rows_dev, half), bf16),
            pltpu.VMEM((rows_dev, half), bf16),
            pltpu.VMEM((weights, block_rows, points), bf16),
            pltpu.VMEM((1, entries), jnp.int32),
            pltpu.VMEM((1, entries), jnp.int32),
            pltpu.VMEM((1, entries), jnp.int32),
            pltpu.VMEM((1, entries), jnp.int32),
            pltpu.VMEM((pairs, held, points), bf16),
            pltpu.VMEM((2 * weights, points, points), bf16),
            pltpu.VMEM((entries + 1, held, points), f32),
            pltpu.VMEM((entries + 1, widest, points), f32),
            pltpu.VMEM((8, 128), jnp.int32),
            pltpu.SMEM((8, 128), jnp.int32),
            pltpu.SMEM((8, 128), jnp.int32),
            pltpu.VMEM((width, depth), bf16),
            pltpu.VMEM((tallest, depth), bf16),
            pltpu.VMEM((columns, width), f32),
            pltpu.VMEM((owned // 2, held, points), f32),
            [chunk_scratch(number) for number in range(len(chunks))],
            [unit_scratch(unit) for unit in units],
            dma((9,)),
            dma((3,)),
            dma((2, len(chunks) - 1)),
            dma((2, len(chunks) + 3 * split_chunks)),
            dma((len(chunks),)),
            dma((len(chunks), 3)),
            dma((len(chunks),)),
            dma((len(chunks),)),
            dma((len(units),)),
            dma((len(units), 3)),
        ],
        compiler_params=pltpu.CompilerParams(
            collective_id=0, has_side_effects=True
        ),
    )(
        layers[0],
        table.transpose(0, 2, 1),
        owner[:, :, 0],
        local_slice,
        block_index,
        weight_index,
        fitting.T,
    )


def local(layers, table, fitting, owner, local_slice, block_index, weight_index):
    arguments = (layers, table, fitting, owner, local_slice, block_index, weight_index)
    entries, peers, group = owner.shape[1], lax.axis_size("row"), lax.axis_size("layer")
    _, points, block_rows = table.shape
    raw_rows = max(2, 2 * entries // peers) * block_rows
    reduced_rows = fitting.shape[0] // group
    slices = peers * fitting.shape[0] // points
    fits = points == 128 and block_rows == 64 and layers.shape[2] == 256
    fits = fits and entries <= 128 and slices <= 128
    if group == 4 and peers == 4 and raw_rows > reduced_rows and fits:
        return local_fused(*arguments)
    return local_rows(*arguments)


def solution(mesh):
    return jax.shard_map(
        local,
        mesh=mesh,
        in_specs=(
            P("layer", "row", "panel"),
            P(),
            P("row", "layer"),
            P("layer", "row", None),
            P("layer", "row"),
            P("layer", "row"),
            P("layer", "row"),
        ),
        out_specs=P(("panel", "row"), "layer"),
        check_vma=False,
    )
```

```python
import functools

import jax
import jax.numpy as jnp
from jax import lax
from jax.experimental import pallas as pl
from jax.experimental.pallas import tpu as pltpu

MESH = pl.DeviceIdType.MESH
from jax.sharding import PartitionSpec as P


def local_rows(layers, table, fitting, owner, local_slice, block_index, weight_index):
    rows_dev = layers.shape[1]
    columns = layers.shape[2]
    slice_rows = table.shape[1]
    block_rows = table.shape[2]
    entries = owner.shape[1]
    peer_count = lax.axis_size("row")
    capacity = max(2, 2 * entries // peer_count)
    slot_count = peer_count * capacity
    owned_slices = fitting.shape[0] // slice_rows
    owner_now = owner[0, :, 0]
    local_now = local_slice[0]
    owner_match = (owner_now[:, None] == jnp.arange(peer_count, dtype=jnp.int32)[None, :]).astype(
        jnp.int32
    )
    slot_rank = jnp.sum((jnp.cumsum(owner_match, axis=0) - 1) * owner_match, axis=1)
    target = owner_now * capacity + slot_rank
    placed = target[None, :] == jnp.arange(slot_count, dtype=jnp.int32)[:, None]
    filled = jnp.any(placed, axis=1)
    source = jnp.sum(jnp.where(placed, jnp.arange(entries, dtype=jnp.int32)[None, :], 0), axis=1)
    send_local = jnp.where(filled, local_now[source], -1).reshape(peer_count, capacity)
    grouped = layers[0].reshape(rows_dev // block_rows, block_rows, columns)
    picked = grouped[block_index[0][source]].reshape(peer_count, capacity, block_rows, columns)
    send_weight = weight_index[0][source].reshape(peer_count, capacity)
    got_rows, got_weight, got_local = (
        lax.all_to_all(picked, "row", split_axis=0, concat_axis=0, tiled=True),
        lax.all_to_all(send_weight, "row", split_axis=0, concat_axis=0, tiled=True),
        lax.all_to_all(send_local, "row", split_axis=0, concat_axis=0, tiled=True),
    )
    pupil_terms = jnp.einsum(
        "ksb,kbc->ksc",
        table[got_weight.reshape(-1)],
        got_rows.reshape(slot_count, block_rows, columns),
        preferred_element_type=jnp.float32,
    ).astype(jnp.bfloat16)
    selector = (
        jnp.arange(owned_slices, dtype=jnp.int32)[:, None] == got_local.reshape(-1)[None, :]
    ).astype(jnp.bfloat16)
    partial_pupil = jnp.dot(
        selector,
        pupil_terms.reshape(slot_count, slice_rows * columns),
        preferred_element_type=jnp.float32,
    ).reshape(owned_slices * slice_rows, columns)
    pupil_rounded = lax.psum(partial_pupil, "layer").astype(jnp.bfloat16)
    return lax.psum_scatter(
        lax.dot_general(
            pupil_rounded, fitting, (((0,), (0,)), ((), ())), preferred_element_type=jnp.float32
        ),
        "row",
        scatter_dimension=0,
        tiled=True,
    ).astype(jnp.bfloat16)


def index_table(owner, local_slice, block, weight, owned, weights, slices, out_ref):
    entries = owner.shape[1]
    square = (entries, entries)
    down = lax.broadcasted_iota(jnp.int32, square, 0)
    along = lax.broadcasted_iota(jnp.int32, square, 1)

    def upright(row):
        return jnp.sum(jnp.where(down == along, jnp.broadcast_to(row, square), 0), axis=1, keepdims=True)

    place = owner * owned + local_slice
    place_up = upright(place)
    place_row = jnp.broadcast_to(place, square)
    twin = (place_row == place_up) & (along < down)
    rank = jnp.sum(((place_row < place_up) | twin).astype(jnp.int32), axis=1, keepdims=True)
    follows = (jnp.sum(twin.astype(jnp.int32), axis=1, keepdims=True) > 0).astype(jnp.int32)
    code = upright(block * weights + weight)
    moved = rank == along
    code = jnp.sum(jnp.where(moved, jnp.broadcast_to(code, square), 0), axis=0, keepdims=True)
    follows = jnp.sum(jnp.where(moved, jnp.broadcast_to(follows, square), 0), axis=0, keepdims=True)
    names = lax.broadcasted_iota(jnp.int32, (entries, slices), 1)
    place_wide = jnp.broadcast_to(place_up, (entries, slices))
    until = jnp.sum((place_wide <= names).astype(jnp.int32), axis=0, keepdims=True)
    held = jnp.sum((place_wide == names).astype(jnp.int32), axis=0, keepdims=True)
    block = code // weights
    out_ref[0:1, 0:entries] = block // 2
    out_ref[1:2, 0:entries] = (block % 2) * weights + code % weights
    out_ref[2:3, 0:entries] = follows
    out_ref[3:4, 0:slices] = jnp.where(held > 0, until, 0)


def fused_kernel(
    peers, owned, chunks, groups, units, split_chunks,
    layers_hbm, table_hbm, owner_hbm, local_hbm, block_hbm, weight_hbm, fitting_hbm, result,
    other_raw, own_raw, turned_ref, owner_ref, local_ref, block_ref, weight_ref,
    own_turned, wide_table, own_sums, got_sums, meta, own_index, got_index,
    fit, left, total, own_part, chunk_refs, unit_refs,
    in_sem, meta_sem, swap_sem, core_sem, row_send, row_recv, layer_send, layer_recv, end_send, end_recv,
):
    row = lax.axis_index("row")
    me = lax.axis_index("layer")
    core = lax.rem(me, 2)
    side = me // 2
    half = other_raw.shape[1]
    width = fit.shape[0]
    weights, block_rows, points = turned_ref.shape
    pairs = own_turned.shape[0]
    entries = owner_ref.shape[1]
    half_owned = owned // 2
    slices = peers * owned
    step_entries = next(size for size in (32, 16, 8, 1) if entries % size == 0)
    owner_width = half // 2
    mate = row + 1 - 2 * lax.rem(row, 2)
    cross = lax.rem(row + 2, peers)
    opposite = peers - 1 - row
    is_end = jnp.logical_or(row == 0, row == peers - 1)
    is_middle = jnp.logical_not(is_end)
    layer_peers = [lax.rem(me + k, 4) for k in range(1, 4)]
    partner = layer_peers[1]
    sibling = me + 1 - 2 * core
    order = (opposite, cross, mate, row)
    swapped = range(1, len(chunks))
    late_chunks = (len(chunks) - 2, len(chunks) - 1)

    first_own = pl.multiple_of(side * half, half)
    first_other = pl.multiple_of((1 - side) * half, half)
    small_copies = [
        pltpu.make_async_copy(source, target, in_sem.at[4 + index])
        for index, (source, target) in enumerate(
            (
                (owner_hbm, owner_ref),
                (local_hbm, local_ref),
                (block_hbm, block_ref),
                (weight_hbm, weight_ref),
            )
        )
    ]
    split_rows = other_raw.shape[0] // 2
    other_copies = [
        pltpu.make_async_copy(
            layers_hbm.at[part * split_rows : (part + 1) * split_rows, pl.ds(first_other, half)],
            other_raw.at[part * split_rows : (part + 1) * split_rows, :],
            in_sem.at[8 * part],
        )
        for part in range(2)
    ]
    own_copy = pltpu.make_async_copy(layers_hbm.at[:, pl.ds(first_own, half)], own_raw, in_sem.at[1])
    table_copy = pltpu.make_async_copy(table_hbm, turned_ref, in_sem.at[2])
    fit_copy = pltpu.make_async_copy(fitting_hbm, fit, in_sem.at[3])
    for copy in small_copies:
        copy.start()
    for copy in other_copies:
        copy.start()
    own_copy.start()
    table_copy.start()

    barrier = pltpu.get_barrier_semaphore()
    for peer in (mate, 2 - row // 2):
        pl.semaphore_signal(barrier, inc=1, device_id={"row": peer}, device_id_type=MESH)
    for peer in layer_peers:
        pl.semaphore_signal(barrier, inc=1, device_id={"layer": peer}, device_id_type=MESH)

    def remote(source, target, send, recv, axis, peer):
        return pltpu.make_async_remote_copy(
            src_ref=source,
            dst_ref=target,
            send_sem=send,
            recv_sem=recv,
            device_id={axis: peer},
            device_id_type=MESH,
        )

    def all_of(ref, sem):
        return remote(ref, ref, sem, sem, "layer", partner)

    def turn(raw, targets, which, start_pair, stop_pair):
        low, high = chunks[0]["parts"][0][1:]
        early_rows = pl.ds(pl.multiple_of(which * (high - low), high - low), high - low)

        def body(pair, carry):
            turned = raw[pl.ds(pl.multiple_of(pair * points, points), points), :].T
            for chunk, target, base in targets:
                for part, start, stop in chunks[chunk]["parts"]:
                    first = part * owner_width + start
                    target[pair, base : base + stop - start, :] = turned[first : first + stop - start]
                    base += stop - start
            own_turned[pair, early_rows, :] = turned[low:high]
            return carry

        lax.fori_loop(start_pair, stop_pair, body, 0, unroll=4)

    def sum_terms(index_ref, rows_ref, sums_ref, low, high):
        def body(step, carry):
            terms = []
            for offset in range(step_entries):
                entry = step * step_entries + offset
                terms.append(
                    jnp.dot(
                        rows_ref[index_ref[0, entry], low:high, :],
                        wide_table[index_ref[1, entry]],
                        preferred_element_type=jnp.float32,
                    )
                )
            running = sums_ref[step * step_entries, low:high, :]
            for offset in range(step_entries):
                entry = step * step_entries + offset
                running = terms[offset] + index_ref[2, entry].astype(jnp.float32) * running
                sums_ref[entry + 1, low:high, :] = running
            return carry

        lax.fori_loop(0, entries // step_entries, body, 0)

    def core_copy(chunk, place):
        refs = chunk_refs[chunk]
        source, target = refs["core_out"], refs["core_in"]
        if chunk < split_chunks:
            source, target = source.at[place], target.at[place]
        index = 4 * chunk + place if chunk < split_chunks else chunk + 3 * split_chunks
        return remote(source, target, core_sem.at[0, index], core_sem.at[1, index], "layer", sibling)

    def row_copy(chunk, slot, source, peer):
        refs = chunk_refs[chunk]
        sems = (row_send.at[chunk], row_recv.at[chunk, max(slot, 1) - 1])
        return remote(refs["row_out"].at[source], refs["row_in"].at[slot], *sems, "row", peer)

    def layer_copy(chunk, k):
        pieces = chunk_refs[chunk]["pieces"]
        sems = (layer_send.at[chunk], layer_recv.at[chunk])
        return remote(pieces.at[me], pieces.at[me], *sems, "layer", layer_peers[k])

    def end_copy(unit, slot, source, peer):
        refs = unit_refs[unit]
        sems = (end_send.at[unit], end_recv.at[unit, max(slot, 1) - 1])
        return remote(refs["product"].at[source], refs["landed"].at[slot], *sems, "row", peer)

    def rows_of(chunk):
        base = chunks[chunk]["base"]
        return slice(base, base + chunks[chunk]["columns"])

    def partial(chunk, owner, which, index):
        name = owner * owned + which * half_owned + index
        value = own_sums[own_index[3, name], rows_of(chunk), :]
        if chunk > 0:
            value = value + got_sums[got_index[3, name], 0 : chunks[chunk]["columns"], :]
        return value

    def begin(chunk):
        swaps[chunk].wait_recv()
        sum_terms(got_index, chunk_refs[chunk]["swap_in"], got_sums, 0, chunks[chunk]["columns"])

    def share(chunk):
        refs = chunk_refs[chunk]
        for place, owner in enumerate(order):

            def body(index, carry):
                refs["core_out"][place, index] = partial(chunk, owner, 1 - core, index).astype(jnp.bfloat16)
                return carry

            lax.fori_loop(0, half_owned, body, 0, unroll=4)
            if chunk < split_chunks or place == 3:
                core_copy(chunk, place if chunk < split_chunks else 0).start()

    def spread(chunk):
        refs = chunk_refs[chunk]
        for place, owner in enumerate(order):
            if chunk < split_chunks or place == 0:
                core_copy(chunk, place).wait_recv()

            def body(index, carry):
                value = partial(chunk, owner, core, index) + refs["core_in"][place, index].astype(jnp.float32)
                if place < 3:
                    refs["row_out"][place, index] = value.astype(jnp.bfloat16)
                else:
                    own_part[index, rows_of(chunk), :] = value
                return carry

            lax.fori_loop(0, half_owned, body, 0, unroll=4)
            if place < 2:

                @pl.when(is_end)
                def _():
                    row_copy(chunk, 2 + place, place, mate).start()

            elif place == 2:

                @pl.when(is_middle if chunk in late_chunks else True)
                def _():
                    row_copy(chunk, 0, 2, mate).start()

        if chunk == late_chunks[-1]:

            @pl.when(is_end)
            def _():
                for late in late_chunks:
                    row_copy(late, 0, 2, mate).start()

    def join(chunk, place):
        refs = chunk_refs[chunk]
        slot = 3 - place

        @pl.when(is_middle)
        def _():
            row_copy(chunk, slot, place, mate).wait_recv()
            refs["row_out"][place] = (
                refs["row_out"][place].astype(jnp.float32) + refs["row_in"][slot].astype(jnp.float32)
            ).astype(jnp.bfloat16)
            row_copy(chunk, 1, place, order[place]).start()

    def settle(chunk, when=None):
        refs = chunk_refs[chunk]

        def run():
            all_of(refs["row_in"].at[0:2], row_recv.at[chunk, 0]).wait_recv()
            value = own_part[:, rows_of(chunk), :]
            for slot in range(2):
                value = value + refs["row_in"][slot].astype(jnp.float32)
            refs["pieces"][me] = value.astype(jnp.bfloat16)
            for k in (1, 0, 2):
                layer_copy(chunk, k).start()

        if when is None:
            run()
        else:
            pl.when(when)(run)

    def gather(number):
        low, high, members = groups[number]
        size = high - low
        for chunk in members:
            pieces = chunk_refs[chunk]["pieces"]
            all_of(pieces.at[0:3], layer_recv.at[chunk]).wait_recv()
            for which in range(2):
                for index in range(half_owned):
                    first = (which * half_owned + index) * points
                    lanes = slice(first, first + points)
                    if chunk == 0:
                        value = pieces[which, index].astype(jnp.float32)
                        value = (value + pieces[2 + which, index].astype(jnp.float32)).astype(jnp.bfloat16)
                        left[0:size, lanes] = value[0:size]
                        left[2 * size : 3 * size, lanes] = value[size:]
                        continue
                    for far in range(2):
                        value = pieces[2 * far + which, index]
                        for place, (part, _, _) in enumerate(chunks[chunk]["parts"]):
                            target = (2 * far + part) * size
                            left[target : target + size, lanes] = value[place * size : (place + 1) * size]

    def multiply(unit, half=None):
        number, begins, ends = units[unit]
        low, high, _ = groups[number]
        middle = begins + (ends - begins) // 512 * 256
        if half is not None:
            begins, ends = ((begins, middle), (middle, ends))[half]
        for start in range(begins, ends, 256):
            stop = min(start + 256, ends)
            total[4 * low : 4 * high, start:stop] = lax.dot_general(
                left[0 : 4 * (high - low), :],
                fit[start:stop, :],
                (((1,), (1,)), ((), ())),
                preferred_element_type=jnp.float32,
            )

    def total_of(unit, owner):
        number, begins, ends = units[unit]
        low, high, _ = groups[number]
        size = high - low
        return total[pl.ds(pl.multiple_of(4 * low + owner * size, size), size), begins:ends]

    def fill(unit):
        product = unit_refs[unit]["product"]
        _, begins, ends = units[unit]
        _, size, padded = product.shape
        if ends - begins < padded:
            product[:, :, padded - 128 :] = jnp.zeros((3, size, 128), jnp.bfloat16)

        def put(place):
            product[place, :, 0 : ends - begins] = total_of(unit, order[place]).astype(jnp.bfloat16)

        for place in range(2):
            pl.when(is_end)(functools.partial(put, place))
        put(2)

    def send_far(unit, place):
        @pl.when(is_end)
        def _():
            end_copy(unit, 2 + place, place, mate).start()

    def send_mate(unit, when=True):
        @pl.when(when)
        def _():
            end_copy(unit, 0, 2, mate).start()

    def pass_on(unit, place):
        product, landed = unit_refs[unit]["product"], unit_refs[unit]["landed"]
        _, begins, ends = units[unit]
        lanes = slice(0, ends - begins)
        slot = 3 - place

        @pl.when(is_middle)
        def _():
            end_copy(unit, slot, place, mate).wait_recv()
            product[place, :, lanes] = (
                total_of(unit, order[place]) + landed[slot, :, lanes].astype(jnp.float32)
            ).astype(jnp.bfloat16)
            end_copy(unit, 1, place, order[place]).start()

    def finish(unit):
        landed = unit_refs[unit]["landed"]
        number, begins, ends = units[unit]
        low, high, _ = groups[number]
        all_of(landed.at[0:2], end_recv.at[unit, 0]).wait_recv()
        value = total_of(unit, row)
        for slot in range(2):
            value = value + landed[slot, :, 0 : ends - begins].astype(jnp.float32)
        result[low:high, begins:ends] = value.astype(result.dtype)

    wide_table[...] = jnp.zeros_like(wide_table)
    own_sums[0] = jnp.zeros(own_sums.shape[1:], own_sums.dtype)
    got_sums[0] = jnp.zeros(got_sums.shape[1:], got_sums.dtype)
    for copy in small_copies:
        copy.wait()
    index_table(
        owner_ref[...], local_ref[...], block_ref[...], weight_ref[...], owned, weights, slices, meta
    )
    index_copy = pltpu.make_async_copy(meta, own_index, meta_sem.at[2])
    index_copy.start()
    swap_targets = [(chunk, chunk_refs[chunk]["swap_out"], 0) for chunk in swapped]
    for part, copy in enumerate(other_copies):
        copy.wait()
        turn(other_raw, swap_targets, 1 - side, part * pairs // 2, (part + 1) * pairs // 2)
    pl.semaphore_wait(barrier, 4 + 2 * lax.rem((row + 1) // 2, 2))
    meta_copy = remote(meta, got_index, meta_sem.at[0], meta_sem.at[1], "layer", partner)
    meta_copy.start()
    swaps = {
        chunk: remote(
            chunk_refs[chunk]["swap_out"],
            chunk_refs[chunk]["swap_in"],
            swap_sem.at[0, chunk - 1],
            swap_sem.at[1, chunk - 1],
            "layer",
            partner,
        )
        for chunk in swapped
    }
    swaps[1].start()
    own_copy.wait()
    turn(own_raw, [(chunk, own_turned, chunks[chunk]["base"]) for chunk in swapped], side, 0, pairs)
    table_copy.wait()
    for index in range(weights):
        wide_table[index, 0:block_rows, :] = turned_ref[index]
        wide_table[weights + index, block_rows:, :] = turned_ref[index]
    index_copy.wait()
    early_rows = chunks[0]["columns"]
    sum_terms(own_index, own_turned, own_sums, 0, early_rows)
    share(0)
    swaps[2].start()
    spread(0)
    sum_terms(own_index, own_turned, own_sums, early_rows, own_turned.shape[1])
    meta_copy.wait_recv()
    begin(1)
    swaps[3].start()
    share(1)
    join(0, 1)
    spread(1)
    join(0, 0)
    fit_copy.start()
    begin(2)
    swaps[4].start()
    share(2)
    spread(2)
    join(1, 1)
    join(1, 0)
    begin(3)
    share(3)
    settle(0)
    spread(3)
    join(2, 1)
    begin(4)
    share(4)
    join(2, 0)
    settle(1)
    spread(4)
    join(3, 1)
    settle(2)
    join(3, 0)
    fit_copy.wait()
    gather(0)
    multiply(0, 0)
    join(4, 1)
    multiply(0, 1)
    join(4, 0)
    settle(3, is_middle)
    fill(0)
    send_far(0, 0)
    send_far(0, 1)
    send_mate(0)
    settle(3, is_end)
    gather(1)
    multiply(1, 0)
    settle(4, is_middle)
    multiply(1, 1)
    fill(1)
    send_far(1, 0)
    send_far(1, 1)
    send_mate(1)
    settle(4, is_end)
    pass_on(0, 1)
    pass_on(0, 0)
    gather(2)
    multiply(2)
    fill(2)
    send_mate(2, is_middle)
    send_far(2, 0)
    pass_on(1, 1)
    pass_on(1, 0)
    gather(3)
    multiply(3)
    fill(3)
    send_mate(3, is_middle)
    send_far(3, 0)
    pass_on(2, 1)
    multiply(4)
    fill(4)
    send_mate(4, is_middle)
    send_far(4, 0)
    send_far(2, 1)
    send_far(3, 1)
    send_far(4, 1)
    send_mate(2, is_end)
    send_mate(3, is_end)
    send_mate(4, is_end)
    pass_on(3, 1)
    pass_on(4, 1)
    finish(0)
    pass_on(2, 0)
    finish(1)
    pass_on(3, 0)
    pass_on(4, 0)
    finish(2)
    finish(3)
    finish(4)

    meta_copy.wait_send()
    for copy in swaps.values():
        copy.wait_send()
    for chunk, refs in enumerate(chunk_refs):
        for place in range(4 if chunk < split_chunks else 1):
            core_copy(chunk, place).wait_send()
        all_of(refs["row_out"], row_send.at[chunk]).wait_send()
        all_of(refs["pieces"].at[0:3], layer_send.at[chunk]).wait_send()
    for unit, refs in enumerate(unit_refs):
        all_of(refs["product"], end_send.at[unit]).wait_send()


def plan_of(out_rows, width):
    cut = out_rows // 4
    marks = [cut * index for index in range(5)]
    spans = list(zip(marks[:-1], marks[1:]))
    low, high = spans[0]
    parts = [[(0, low, high)], [(1, low, high)]]
    parts += [[(0, start, stop), (1, start, stop)] for start, stop in spans[1:]]
    chunks, base = [], 0
    for number, part in enumerate(parts):
        columns = sum(stop - start for _, start, stop in part)
        if number == 0:
            columns = 2 * columns
        chunks.append({"parts": part, "columns": columns, "base": base})
        base += columns
    groups = [(low, high, (0, 1))]
    groups += [(start, stop, (number + 2,)) for number, (start, stop) in enumerate(spans[1:])]
    middle = width * 3 // 1024 * 256
    units = [(number, 0, width) for number in range(len(groups) - 1)]
    units += [(len(groups) - 1, 0, middle), (len(groups) - 1, middle, width)]
    return chunks, groups, units, base


def local_fused(layers, table, fitting, owner, local_slice, block_index, weight_index):
    rows_dev, columns = layers.shape[1:]
    weights, points, block_rows = table.shape
    entries = owner.shape[1]
    peers = lax.axis_size("row")
    depth, width = fitting.shape
    owned = depth // points
    half = columns // 2
    out_rows = columns // peers
    pairs = rows_dev // points
    chunks, groups, units, held = plan_of(out_rows, width)
    split_chunks = 1
    bf16, f32 = jnp.bfloat16, jnp.float32
    dma = pltpu.SemaphoreType.DMA

    def chunk_scratch(number):
        cols = chunks[number]["columns"]
        slots = owned // 2
        refs = {
            "core_out": pltpu.VMEM((4, slots, cols, points), bf16),
            "core_in": pltpu.VMEM((4, slots, cols, points), bf16),
            "row_out": pltpu.VMEM((3, slots, cols, points), bf16),
            "row_in": pltpu.VMEM((4, slots, cols, points), bf16),
            "pieces": pltpu.VMEM((4, slots, cols, points), bf16),
        }
        if number > 0:
            refs["swap_out"] = pltpu.VMEM((pairs, cols, points), bf16)
            refs["swap_in"] = pltpu.VMEM((pairs, cols, points), bf16)
        return refs

    def unit_scratch(unit):
        number, begins, ends = unit
        low, high, _ = groups[number]
        padded = -(-(ends - begins) // 128) * 128
        return {
            "product": pltpu.VMEM((3, high - low, padded), bf16),
            "landed": pltpu.VMEM((4, high - low, padded), bf16),
        }

    widest = max(chunk["columns"] for chunk in chunks[1:])
    tallest = max(4 * (high - low) for low, high, _ in groups)
    hbm = pl.BlockSpec(memory_space=pltpu.HBM)
    vmem = pl.BlockSpec(memory_space=pltpu.VMEM)
    return pl.pallas_call(
        functools.partial(fused_kernel, peers, owned, chunks, groups, units, split_chunks),
        out_shape=pltpu.VMEM((out_rows, width), bf16),
        in_specs=[hbm] * 7,
        out_specs=vmem,
        scratch_shapes=[
            pltpu.VMEM((rows_dev, half), bf16),
            pltpu.VMEM((rows_dev, half), bf16),
            pltpu.VMEM((weights, block_rows, points), bf16),
            pltpu.VMEM((1, entries), jnp.int32),
            pltpu.VMEM((1, entries), jnp.int32),
            pltpu.VMEM((1, entries), jnp.int32),
            pltpu.VMEM((1, entries), jnp.int32),
            pltpu.VMEM((pairs, held, points), bf16),
            pltpu.VMEM((2 * weights, points, points), bf16),
            pltpu.VMEM((entries + 1, held, points), f32),
            pltpu.VMEM((entries + 1, widest, points), f32),
            pltpu.VMEM((8, 128), jnp.int32),
            pltpu.SMEM((8, 128), jnp.int32),
            pltpu.SMEM((8, 128), jnp.int32),
            pltpu.VMEM((width, depth), bf16),
            pltpu.VMEM((tallest, depth), bf16),
            pltpu.VMEM((columns, width), f32),
            pltpu.VMEM((owned // 2, held, points), f32),
            [chunk_scratch(number) for number in range(len(chunks))],
            [unit_scratch(unit) for unit in units],
            dma((9,)),
            dma((3,)),
            dma((2, len(chunks) - 1)),
            dma((2, len(chunks) + 3 * split_chunks)),
            dma((len(chunks),)),
            dma((len(chunks), 3)),
            dma((len(chunks),)),
            dma((len(chunks),)),
            dma((len(units),)),
            dma((len(units), 3)),
        ],
        compiler_params=pltpu.CompilerParams(
            collective_id=0, has_side_effects=True
        ),
    )(
        layers[0],
        table.transpose(0, 2, 1),
        owner[:, :, 0],
        local_slice,
        block_index,
        weight_index,
        fitting.T,
    )


def local(layers, table, fitting, owner, local_slice, block_index, weight_index):
    arguments = (layers, table, fitting, owner, local_slice, block_index, weight_index)
    entries, peers, group = owner.shape[1], lax.axis_size("row"), lax.axis_size("layer")
    _, points, block_rows = table.shape
    raw_rows = max(2, 2 * entries // peers) * block_rows
    reduced_rows = fitting.shape[0] // group
    slices = peers * fitting.shape[0] // points
    fits = points == 128 and block_rows == 64 and layers.shape[2] == 256
    fits = fits and entries <= 128 and slices <= 128
    if group == 4 and peers == 4 and raw_rows > reduced_rows and fits:
        return local_fused(*arguments)
    return local_rows(*arguments)


def solution(mesh):
    return jax.shard_map(
        local,
        mesh=mesh,
        in_specs=(
            P("layer", "row", "panel"),
            P(),
            P("row", "layer"),
            P("layer", "row", None),
            P("layer", "row"),
            P("layer", "row"),
            P("layer", "row"),
        ),
        out_specs=P(("panel", "row"), "layer"),
        check_vma=False,
    )
```
